32 devices in a mesh: frame: 8 (over y, x, core), tensor: 4 (over z).
Axes of the slice: x: 2, y: 2, z: 4, core: 2. Of those that a mesh axis runs over, the one named last changes fastest.
Arguments:
- tokens: bfloat16 [4, 16, 256, 1024], P(None, 'frame', 'tensor'), may hold values from -6 to 6
- noise_steps: int32 [4, 16], P(None, 'frame'), may hold values from 0 to 999
- ada_weight: bfloat16 [1024, 6, 1024], P(None, None, 'tensor'), may hold values from -0.1875 to 0.1875
- ada_bias: bfloat16 [6, 1024], P(None, 'tensor'), may hold values from -3 to 3
- qkv_weight: bfloat16 [1024, 3, 1024], P(None, None, 'tensor'), may hold values from -0.1875 to 0.1875
- qv_bias: bfloat16 [2, 1024], P(None, 'tensor'), may hold values from -3 to 3
- out_weight: bfloat16 [1024, 1024], P('tensor'), may hold values from -2 to 2
- out_bias: bfloat16 [1024], replicated, may hold values from -3 to 3
- up_weight: bfloat16 [1024, 4096], P(None, 'tensor'), may hold values from -0.1875 to 0.1875
- up_bias: bfloat16 [4096], P('tensor'), may hold values from -3 to 3
- down_weight: bfloat16 [4096, 1024], P('tensor'), may hold values from -0.09375 to 0.09375
- down_bias: bfloat16 [1024], replicated, may hold values from -3 to 3
- cotangent: bfloat16 [4, 16, 256, 1024], P(None, 'frame', 'tensor'), may hold values from -6 to 6
Outputs:
- out: bfloat16 [4, 16, 256, 1024], P(None, 'frame', 'tensor')
- grad_tokens: float32 [4, 16, 256, 1024], P(None, 'frame', 'tensor')
- grad_ada_weight: float32 [1024, 6, 1024], P(None, None, 'tensor')
- grad_ada_bias: float32 [6, 1024], P(None, 'tensor')
- grad_qkv_weight: float32 [1024, 3, 1024], P(None, None, 'tensor')
- grad_qv_bias: float32 [2, 1024], P(None, 'tensor')
- grad_out_weight: float32 [1024, 1024], P('tensor')
- grad_out_bias: float32 [1024], replicated
- grad_up_weight: float32 [1024, 4096], P(None, 'tensor')
- grad_up_bias: float32 [4096], P('tensor')
- grad_down_weight: float32 [4096, 1024], P('tensor')
- grad_down_bias: float32 [1024], replicated
The draws below stay inside these ranges and needn't reach their ends.
Inputs may be any that keep to these rules, and one draw needn't show every extreme that they name: `noise_steps`: timestep of each frame of each clip; a few timesteps are very common.
All inputs are finite; a program needn't handle non-finite values.
Results may differ from the reference program's by a relative error of at most 0.014.
The reference program's roundings to bfloat16 on the way count: a program that leaves them out, or rounds other values in their place, can miss the bound.
Values may be sent and summed in bfloat16 or wider, within the bound.
No kernel may reach another device: no remote copies, remote signals or barrier semaphores. Data moves between devices by JAX's collectives and lax.ppermute only.
A program may use at most 192 MiB of HBM per device.

```python
import math
import jax
import jax.numpy as jnp
import numpy as np
from jax import lax

D = 1024
H = 16
HD = 64
FF = 4096
PATCH = 256
NSTEPS = 1000
CLIPS = 4
FRAMES = 16


def touch_ends(values, key, low, high):
    spot = [jax.random.randint(jax.random.fold_in(key, axis), (), 0, length) for axis, length in enumerate(values.shape)]
    longest = values.shape.index(max(values.shape))
    beside = spot[:longest] + [(spot[longest] + 1) % values.shape[longest]] + spot[longest + 1:]
    return values.at[tuple(spot)].set(low).at[tuple(beside)].set(high)


def steps_of(rng, dims, cuts, low, high):
    factor_of = 1.0
    for dim, parts in cuts:
        heights = jax.random.uniform(jax.random.fold_in(jax.random.fold_in(rng, 6), dim), (parts,), jnp.float32, low / len(cuts), high / len(cuts))
        factor_of = factor_of * jnp.repeat(jnp.exp(heights), dims[dim] // parts).reshape((-1,) + (1,) * (len(dims) - 1 - dim))
    return factor_of


def rank_table(number_of, slope):
    portions = [(1 << 20) // math.isqrt(grade ** slope) + 1 for grade in range(1, number_of + 1)]
    scale = 1 + sum(portions) // (1 << 30)
    return np.cumsum(np.array([max(1, weight // scale) for weight in portions]))


def ranked_ids(own_key, extent, count, skew):
    table = rank_table(count, skew)
    pick = jax.random.randint(jax.random.fold_in(own_key, 1), extent, 0, int(table[count - 1]))
    grade = jnp.searchsorted(jnp.asarray(table, jnp.int32), pick, side="right")
    return jax.random.permutation(jax.random.fold_in(own_key, 2), count)[grade].astype(jnp.int32)


def bell_draw(own_key, extent, deviation, reach, pieces=(), kind=jnp.bfloat16):
    result = jax.random.normal(own_key, extent, jnp.float32) * deviation
    if len(pieces) > 0:
        result = steps_of(own_key, extent, pieces, -0.22, 0.18) * result
    return jnp.clip(result, min=-reach, max=reach).astype(kind)


def setup_inputs(seed: int = 0) -> dict:
    arg_keys = jax.random.split(jax.random.key(seed), 14)
    return {
        "tokens": bell_draw(arg_keys[0], (CLIPS, FRAMES, PATCH, D), 1.0, 6.0, ((1, 8), (2, 4))),
        "noise_steps": touch_ends(ranked_ids(arg_keys[1], (CLIPS, FRAMES), NSTEPS, 2), jax.random.fold_in(arg_keys[1], 3), 0, NSTEPS - 1).astype(jnp.int32),
        "ada_weight": bell_draw(arg_keys[2], (D, 6, D), D ** -0.5, 0.1875, ((2, 4),)),
        "ada_bias": bell_draw(arg_keys[3], (6, D), 0.5, 3.0, ((1, 4),)),
        "qkv_weight": bell_draw(arg_keys[4], (D, 3, D), D ** -0.5, 0.1875, ((2, 4),)),
        "qv_bias": bell_draw(arg_keys[5], (2, D), 0.5, 3.0, ((1, 4),)),
        "out_weight": bell_draw(arg_keys[6], (D, D), (max(D // 128, 1)) ** -0.5, 2.0, ((0, 4),)),
        "out_bias": bell_draw(arg_keys[7], (D,), 0.5, 3.0),
        "up_weight": bell_draw(arg_keys[8], (D, FF), D ** -0.5, 0.1875, ((1, 4),)),
        "up_bias": bell_draw(arg_keys[9], (FF,), 0.5, 3.0, ((0, 4),)),
        "down_weight": bell_draw(arg_keys[10], (FF, D), FF ** -0.5, 0.09375, ((0, 4),)),
        "down_bias": bell_draw(arg_keys[11], (D,), 0.5, 3.0),
        "cotangent": bell_draw(arg_keys[12], (CLIPS, FRAMES, PATCH, D), 1.0, 6.0, ((1, 8), (2, 4))),
    }


highest = lax.Precision.HIGHEST

@jax.custom_vjp
def low(v):
    return lax.optimization_barrier(v.astype(jnp.bfloat16)).astype(jnp.float32)

@jax.custom_vjp
def low_back(v):
    return v

def low_keep(v):
    return (low(v), None)

def low_pass(kept, grad):
    return (grad,)

def back_keep(v):
    return (v, None)

def back_low(kept, grad):
    return (low(grad),)
low.defvjp(low_keep, low_pass)
low_back.defvjp(back_keep, back_low)

def noise_embedding(noise_steps, model_width):
    half_width = model_width // 2
    frequency = jnp.exp(-math.log(10000.0) * jnp.arange(half_width, dtype=jnp.float32) / half_width)
    angles = noise_steps.astype(jnp.float32)[..., None] * frequency
    return jnp.concatenate([jnp.cos(angles), jnp.sin(angles)], axis=-1)

def layer_norm(values):
    centred = values - lax.optimization_barrier(jnp.mean(values, axis=-1, keepdims=True))
    inverse = lax.rsqrt(lax.optimization_barrier(jnp.mean(centred * centred, axis=-1, keepdims=True)) + 1e-06)
    return centred * inverse

def split_heads(values_in):
    return values_in.reshape(FRAMES * PATCH, H, HD).transpose(1, 0, 2)

def clip_layer(weights_in, clip_tokens, clip_steps):
    ada_weight, ada_bias, qkv_weight, qv_bias, out_weight, out_bias, up_weight, up_bias, down_weight, down_bias = weights_in
    act_noise = low(jax.nn.silu(noise_embedding(clip_steps, D)))
    modulation = jnp.einsum('fd,dkj->fkj', act_noise, ada_weight, precision=highest) + ada_bias
    shift_one = modulation[:, None, 0]
    scale_one = modulation[:, None, 1]
    gate_one = modulation[:, None, 2]
    shift_two = modulation[:, None, 3]
    scale_two = modulation[:, None, 4]
    gate_two = modulation[:, None, 5]
    hidden_one = low(layer_norm(clip_tokens) * (1.0 + scale_one) + shift_one)
    projected = jnp.einsum('fpd,dkj->fpkj', hidden_one, qkv_weight, precision=highest)
    queries = low_back(low(projected[:, :, 0] + qv_bias[0]))
    keys = low_back(low(projected[:, :, 1]))
    values = low_back(low(projected[:, :, 2] + qv_bias[1]))
    frame_ids = jnp.arange(FRAMES * PATCH) // PATCH
    allowed = frame_ids[None, :] <= frame_ids[:, None]

    def one_head(head_inputs):
        head_queries, head_keys, head_values = head_inputs
        scores = low_back(jnp.dot(head_queries, head_keys.T, precision=highest) * HD ** (-0.5))
        scores = jnp.where(allowed, scores, -1e+30)
        row_max = lax.optimization_barrier(jnp.max(scores, axis=-1, keepdims=True))
        weights = jnp.exp(scores - row_max)
        attn_probs = weights / lax.optimization_barrier(jnp.sum(weights, axis=-1, keepdims=True))
        return jnp.dot(low(attn_probs), head_values, precision=highest)
    head_outputs = lax.map(jax.checkpoint(one_head), (split_heads(queries), split_heads(keys), split_heads(values)))
    attended = low_back(low(head_outputs.transpose(1, 0, 2).reshape(FRAMES, PATCH, D)))
    branch_one = low_back(jnp.einsum('fpj,jd->fpd', attended, out_weight, precision=highest) + out_bias)
    middle = clip_tokens + gate_one * branch_one
    hidden_two = low(layer_norm(middle) * (1.0 + scale_two) + shift_two)
    pre_gelu = low_back(jnp.einsum('fpd,dh->fph', hidden_two, up_weight, precision=highest) + up_bias)
    activated = low(jax.nn.gelu(pre_gelu, approximate=True))
    branch_two = low_back(jnp.einsum('fph,hd->fpd', activated, down_weight, precision=highest) + down_bias)
    return middle + gate_two * branch_two

def reference(tokens, noise_steps, ada_weight, ada_bias, qkv_weight, qv_bias, out_weight, out_bias, up_weight, up_bias, down_weight, down_bias, cotangent):
    weights_in = tuple((weight.astype(jnp.float32) for weight in (ada_weight, ada_bias, qkv_weight, qv_bias, out_weight, out_bias, up_weight, up_bias, down_weight, down_bias)))

    def forward(weights_now, tokens_now):

        def per_clip(clip_inputs):
            return clip_layer(weights_now, clip_inputs[0], clip_inputs[1])
        return lax.map(jax.checkpoint(per_clip), (tokens_now, noise_steps))
    outputs, pullback = jax.vjp(forward, weights_in, tokens.astype(jnp.float32))
    weight_grads, grad_tokens = pullback(cotangent.astype(jnp.float32))
    return (outputs.astype(jnp.bfloat16), grad_tokens, weight_grads[0], weight_grads[1], weight_grads[2], weight_grads[3], weight_grads[4], weight_grads[5], weight_grads[6], weight_grads[7], weight_grads[8], weight_grads[9])
```

```python
from functools import partial
import math

import jax
import jax.numpy as jnp
from jax import lax
from jax.experimental import pallas as pl
from jax.experimental.pallas import tpu as pltpu
from jax.sharding import PartitionSpec as P

HD = 64
f32 = jnp.float32
bf16 = jnp.bfloat16
score_scale = HD ** (-0.5)


def noise_embedding(noise_steps, model_width):
    half_width = model_width // 2
    frequency = jnp.exp(-math.log(10000.0) * jnp.arange(half_width, dtype=f32) / half_width)
    angles = noise_steps.astype(f32)[..., None] * frequency
    return jnp.concatenate([jnp.cos(angles), jnp.sin(angles)], axis=-1)


def noise_activation(noise_steps, model_width):
    return jax.nn.silu(noise_embedding(noise_steps, model_width)).astype(bf16)


def layer_norm(values):
    centred = values - jnp.mean(values, axis=-1, keepdims=True)
    inverse = lax.rsqrt(jnp.mean(centred * centred, axis=-1, keepdims=True) + 1e-06)
    return (centred * inverse, inverse)


def norm_back(grad_normed, normed, inverse):
    return inverse * (
        grad_normed
        - jnp.mean(grad_normed, axis=-1, keepdims=True)
        - normed * jnp.mean(grad_normed * normed, axis=-1, keepdims=True)
    )


def dot(left, right):
    return lax.dot_general(left, right, (((1,), (0,)), ((), ())), preferred_element_type=f32)


def dot_nt(left, right):
    return lax.dot_general(left, right, (((1,), (1,)), ((), ())), preferred_element_type=f32)


def dot_tn(left, right):
    return lax.dot_general(left, right, (((0,), (0,)), ((), ())), preferred_element_type=f32)


def head_blocks(transposed, head_count, patch_count):
    rows = lax.broadcasted_iota(jnp.int32, transposed.shape, 0) // HD
    return jnp.concatenate(
        [jnp.where(rows == head, transposed, 0.0) for head in range(head_count)], axis=1
    ).astype(bf16)


def head_rows(natural, head_count):
    lanes = lax.broadcasted_iota(jnp.int32, natural.shape, 1) // HD
    return jnp.concatenate(
        [jnp.where(lanes == head, natural, 0.0) for head in range(head_count)], axis=0
    ).astype(bf16)


def attend_kernel(frame_ids, q_ref, k_ref, vt_ref, out_ref, lse_ref, *, head_count, patch_count):
    key_stop = frame_ids[pl.program_id(0)] + 1
    q_cols = head_blocks(
        jnp.swapaxes(q_ref[...].astype(f32), 0, 1) * score_scale, head_count, patch_count
    )
    width = head_count * patch_count

    def step(index, carry):
        row_max, row_total, sums = carry
        start = pl.multiple_of(index * patch_count, patch_count)
        scores = dot(k_ref[pl.ds(start, patch_count), :], q_cols)
        new_max = jnp.maximum(row_max, jnp.max(scores, axis=0, keepdims=True))
        rescale = jnp.exp(row_max - new_max)
        weights = jnp.exp(scores - new_max)
        row_total = row_total * rescale + jnp.sum(weights, axis=0, keepdims=True)
        weights = weights.astype(bf16)
        values_t = vt_ref[:, pl.ds(start, patch_count)]
        parts = []
        for head in range(head_count):
            cols = slice(head * patch_count, (head + 1) * patch_count)
            rows = slice(head * HD, (head + 1) * HD)
            parts.append(sums[head] * rescale[:, cols] + dot(values_t[rows], weights[:, cols]))
        return (new_max, row_total, tuple(parts))

    row_max, row_total, sums = lax.fori_loop(
        0,
        key_stop,
        step,
        (
            jnp.full((1, width), -1e30, f32),
            jnp.zeros((1, width), f32),
            tuple(jnp.zeros((HD, patch_count), f32) for _ in range(head_count)),
        ),
    )
    inverse = 1.0 / row_total
    out_t = jnp.concatenate(
        [
            sums[head] * inverse[:, head * patch_count : (head + 1) * patch_count]
            for head in range(head_count)
        ],
        axis=0,
    )
    out_ref[...] = jnp.swapaxes(out_t, 0, 1).astype(bf16)
    lse_ref[0] = row_max + jnp.log(row_total)


def attend(queries, keys, values, frame_ids, head_count, patch_count):
    row_count, lanes = queries.shape
    key_rows = keys.shape[0]
    steps = row_count // patch_count
    width = head_count * patch_count
    pairs = steps * (key_rows // patch_count + 1) // 2
    work = pairs * patch_count * width
    return pl.pallas_call(
        partial(attend_kernel, head_count=head_count, patch_count=patch_count),
        grid_spec=pltpu.PrefetchScalarGridSpec(
            num_scalar_prefetch=1,
            grid=(steps,),
            in_specs=[
                pl.BlockSpec((patch_count, lanes), lambda j, ids: (j, 0)),
                pl.BlockSpec((key_rows, lanes), lambda j, ids: (0, 0)),
                pl.BlockSpec((lanes, key_rows), lambda j, ids: (0, 0)),
            ],
            out_specs=[
                pl.BlockSpec((patch_count, lanes), lambda j, ids: (j, 0)),
                pl.BlockSpec((1, 1, width), lambda j, ids: (j, 0, 0)),
            ],
        ),
        out_shape=[
            jax.ShapeDtypeStruct((row_count, lanes), bf16),
            jax.ShapeDtypeStruct((steps, 1, width), f32),
        ],
        compiler_params=pltpu.CompilerParams(vmem_limit_bytes=32 << 20),
        cost_estimate=pl.CostEstimate(
            flops=work * 1024, bytes_accessed=8 * row_count * lanes, transcendentals=work
        ),
        name="attend",
    )(frame_ids, queries, keys, values.T)


def attend_back_kernel(
    frame_ids,
    q_ref,
    grad_ref,
    out_ref,
    lse_ref,
    k_ref,
    v_ref,
    kt_ref,
    dq_ref,
    dk_ref,
    dv_ref,
    dk_sum,
    dv_sum,
    *,
    head_count,
    patch_count,
):
    position = pl.program_id(0)
    key_stop = frame_ids[position] + 1

    @pl.when(position == 0)
    def _():
        dk_sum[...] = jnp.zeros_like(dk_sum)
        dv_sum[...] = jnp.zeros_like(dv_sum)

    q_rows = q_ref[...].astype(f32) * score_scale
    grad_rows = grad_ref[...].astype(f32)
    grad_t = jnp.swapaxes(grad_rows, 0, 1)
    grad_out_t = grad_t * jnp.swapaxes(out_ref[...].astype(f32), 0, 1)
    delta = jnp.concatenate(
        [
            jnp.sum(grad_out_t[head * HD : (head + 1) * HD], axis=0, keepdims=True)
            for head in range(head_count)
        ],
        axis=1,
    )
    q_cols = head_blocks(jnp.swapaxes(q_rows, 0, 1), head_count, patch_count)
    grad_cols = head_blocks(grad_t, head_count, patch_count)
    q_stack = head_rows(q_rows, head_count)
    grad_stack = head_rows(grad_rows, head_count)
    lse = lse_ref[0]

    def step(index, sums):
        start = pl.multiple_of(index * patch_count, patch_count)
        here = pl.ds(start, patch_count)
        scores = dot(k_ref[here, :], q_cols)
        grad_probs = dot(v_ref[here, :], grad_cols)
        probs = jnp.exp(scores - lse)
        grad_scores = (probs * (grad_probs - delta)).astype(bf16)
        dv_sum[here, :] += dot(probs.astype(bf16), grad_stack)
        dk_sum[here, :] += dot(grad_scores, q_stack)
        keys_t = kt_ref[:, here]
        return tuple(
            sums[head]
            + dot(
                keys_t[head * HD : (head + 1) * HD],
                grad_scores[:, head * patch_count : (head + 1) * patch_count],
            )
            for head in range(head_count)
        )

    sums = lax.fori_loop(
        0, key_stop, step, tuple(jnp.zeros((HD, patch_count), f32) for _ in range(head_count))
    )
    dq_t = jnp.concatenate(sums, axis=0) * score_scale
    dq_ref[...] = jnp.swapaxes(dq_t, 0, 1).astype(bf16)

    @pl.when(position == pl.num_programs(0) - 1)
    def _():
        dk_ref[...] = dk_sum[...].astype(bf16)
        dv_ref[...] = dv_sum[...].astype(bf16)


def attend_back(queries, keys, values, out, lse, grad, frame_ids, head_count, patch_count):
    row_count, lanes = queries.shape
    key_rows = keys.shape[0]
    steps = row_count // patch_count
    width = head_count * patch_count
    pairs = steps * (key_rows // patch_count + 1) // 2
    work = pairs * patch_count * width
    block = pl.BlockSpec((patch_count, lanes), lambda j, ids: (j, 0))
    whole = pl.BlockSpec((key_rows, lanes), lambda j, ids: (0, 0))
    return pl.pallas_call(
        partial(attend_back_kernel, head_count=head_count, patch_count=patch_count),
        grid_spec=pltpu.PrefetchScalarGridSpec(
            num_scalar_prefetch=1,
            grid=(steps,),
            in_specs=[
                block,
                block,
                block,
                pl.BlockSpec((1, 1, width), lambda j, ids: (j, 0, 0)),
                whole,
                whole,
                pl.BlockSpec((lanes, key_rows), lambda j, ids: (0, 0)),
            ],
            out_specs=[block, whole, whole],
            scratch_shapes=[
                pltpu.VMEM((key_rows, lanes), f32),
                pltpu.VMEM((key_rows, lanes), f32),
            ],
        ),
        out_shape=[
            jax.ShapeDtypeStruct((row_count, lanes), bf16),
            jax.ShapeDtypeStruct((key_rows, lanes), bf16),
            jax.ShapeDtypeStruct((key_rows, lanes), bf16),
        ],
        compiler_params=pltpu.CompilerParams(vmem_limit_bytes=40 << 20),
        cost_estimate=pl.CostEstimate(
            flops=work * 2560, bytes_accessed=16 * row_count * lanes, transcendentals=work
        ),
        name="attend_back",
    )(frame_ids, queries, grad, out, lse, keys, values, keys.T)


def on_device(
    tokens,
    noise_steps,
    ada_weight,
    ada_bias,
    qkv_weight,
    qv_bias,
    out_weight,
    out_bias,
    up_weight,
    up_bias,
    down_weight,
    down_bias,
    cotangent,
):
    clip_count, local_frames, local_patches, model_width = tokens.shape
    tensor_count = lax.axis_size("tensor")
    frame_devices = lax.axis_size("frame")
    frame_at = lax.axis_index("frame")
    tensor_at = lax.axis_index("tensor")
    patch_count = local_patches * tensor_count
    hidden_width = up_weight.shape[1] * tensor_count
    head_total = model_width // HD
    shard_heads = head_total // tensor_count
    head_count = head_total // frame_devices
    lanes = head_count * HD
    unit_total = clip_count * local_frames
    units = unit_total // tensor_count
    sharers = tensor_count // clip_count
    share_at = tensor_at % sharers
    frame_count = frame_devices * local_frames
    own_rows = units * patch_count
    all_rows = frame_devices * own_rows
    slot = frame_at % shard_heads
    first_shard = (frame_at // shard_heads) * head_count
    shard_groups = tensor_count // head_count


    def to_units(values):
        return lax.all_to_all(
            values.reshape(unit_total, local_patches, model_width),
            "tensor",
            split_axis=0,
            concat_axis=1,
            tiled=True,
        )

    def from_units(values):
        return lax.all_to_all(
            values, "tensor", split_axis=1, concat_axis=0, tiled=True
        ).reshape(clip_count, local_frames, local_patches, model_width)

    unit_tokens = to_units(tokens)
    act_noise = noise_activation(noise_steps, model_width).reshape(unit_total, model_width)
    mod_local = jnp.einsum(
        "ud,dkj->ukj", act_noise, ada_weight, preferred_element_type=f32
    ) + ada_bias.astype(f32)
    modulation = lax.all_to_all(mod_local, "tensor", split_axis=0, concat_axis=2, tiled=True)
    shift_one = modulation[:, None, 0]
    scale_one = modulation[:, None, 1]
    gate_one = modulation[:, None, 2]
    shift_two = modulation[:, None, 3]
    scale_two = modulation[:, None, 4]
    gate_two = modulation[:, None, 5]

    slot_weight = lax.dynamic_slice_in_dim(qkv_weight, slot * HD, HD, axis=2)
    slot_weight = slot_weight.transpose(1, 2, 0).reshape(3 * HD, model_width)
    slots_all = lax.all_gather(slot_weight, "tensor", axis=0)
    head_weight = lax.dynamic_slice_in_dim(slots_all, first_shard, head_count, axis=0)
    head_weight = (
        head_weight.reshape(head_count, 3, HD, model_width)
        .transpose(1, 0, 2, 3)
        .reshape(3 * lanes, model_width)
    )
    slot_bias = lax.dynamic_slice_in_dim(qv_bias, slot * HD, HD, axis=1).reshape(2 * HD)
    small_all = lax.all_gather(jnp.concatenate([slot_bias, up_bias]), "tensor", axis=0)
    head_bias = lax.dynamic_slice_in_dim(small_all[:, : 2 * HD], first_shard, head_count, axis=0)
    head_bias = head_bias.reshape(head_count, 2, HD).transpose(1, 0, 2).reshape(2, lanes)
    head_bias = head_bias.astype(f32)
    qkv_bias = jnp.concatenate([head_bias[0], jnp.zeros((lanes,), f32), head_bias[1]])
    hidden_part = hidden_width // (tensor_count * frame_devices)
    up_bias_all = (
        small_all[:, 2 * HD :]
        .reshape(tensor_count, frame_devices, hidden_part)
        .transpose(1, 0, 2)
        .reshape(hidden_width)
        .astype(f32)
    )

    token_values = unit_tokens.astype(f32)
    normed_one, inverse_one = layer_norm(token_values)
    hidden_one = (normed_one * (1.0 + scale_one) + shift_one).astype(bf16)
    hidden_all = lax.all_gather(
        hidden_one.reshape(own_rows, model_width), "frame", axis=0, tiled=True
    )

    def own_part(values):
        size = values.shape[0] // frame_devices
        return lax.dynamic_slice_in_dim(values, frame_at * size, size, axis=0)

    out_part = lax.all_gather(own_part(out_weight), "tensor", axis=0)
    up_part = lax.all_gather(own_part(up_weight), "tensor", axis=0)
    down_part = lax.all_gather(own_part(down_weight), "tensor", axis=0)
    out_rows = out_part.shape[1]
    up_rows = up_part.shape[1]
    up_part = (
        up_part.reshape(tensor_count, up_rows, frame_devices, hidden_part)
        .transpose(1, 2, 0, 3)
        .reshape(up_rows, hidden_width)
    )
    out_full = lax.all_gather(out_part, "frame", axis=0)
    head_parts = HD // out_rows
    out_full = (
        out_full.reshape(
            shard_heads, head_parts, shard_groups, head_count, out_rows, model_width
        )
        .transpose(2, 0, 3, 1, 4, 5)
        .reshape(model_width, model_width)
    )
    up_full = lax.all_gather(up_part, "frame", axis=0, tiled=True)
    down_full = lax.all_gather(down_part, "frame", axis=0).reshape(hidden_width, model_width)

    projected = (dot_nt(hidden_all, head_weight) + qkv_bias).astype(bf16)
    queries = projected[:, :lanes]
    keys = projected[:, lanes : 2 * lanes]
    values = projected[:, 2 * lanes :]

    def share(mine):
        if sharers == 1:
            return mine
        pieces = [mine]
        for shift in range(1, sharers):
            perm = [
                (t, (t // sharers) * sharers + (t + shift) % sharers) for t in range(tensor_count)
            ]
            pieces.append(lax.ppermute(mine, "tensor", perm))
        stacked = jnp.stack(pieces)
        stacked = jnp.stack(
            [
                lax.dynamic_index_in_dim(
                    stacked, (share_at - member) % sharers, 0, keepdims=False
                )
                for member in range(sharers)
            ]
        )
        return (
            stacked.reshape(sharers, frame_devices, own_rows, lanes)
            .transpose(1, 0, 2, 3)
            .reshape(sharers * all_rows, lanes)
        )

    def unshare(partial_sums):
        if sharers == 1:
            return partial_sums
        pieces = (
            partial_sums.reshape(frame_devices, sharers, own_rows, lanes)
            .transpose(1, 0, 2, 3)
            .reshape(sharers, all_rows, lanes)
        )
        total = lax.dynamic_index_in_dim(pieces, share_at, 0, keepdims=False).astype(f32)
        for shift in range(1, sharers):
            perm = [
                (t, (t // sharers) * sharers + (t + shift) % sharers) for t in range(tensor_count)
            ]
            piece = lax.dynamic_index_in_dim(
                pieces, (share_at + shift) % sharers, 0, keepdims=False
            )
            total = total + lax.ppermute(piece, "tensor", perm).astype(f32)
        return total.astype(bf16)

    keys_all = share(keys)
    values_all = share(values)
    unit_ids = jnp.arange(frame_devices * units, dtype=jnp.int32)
    frame_ids = (
        (unit_ids // units) * local_frames + share_at.astype(jnp.int32) * units + unit_ids % units
    )
    attended_heads, row_lse = attend(
        queries, keys_all, values_all, frame_ids, head_count, patch_count
    )
    attended = lax.all_to_all(
        attended_heads.reshape(frame_devices, own_rows, lanes),
        "frame",
        split_axis=0,
        concat_axis=2,
        tiled=True,
    ).reshape(own_rows, model_width)

    unit_shape = (units, patch_count, model_width)
    branch_one = dot(attended, out_full).reshape(unit_shape) + out_bias.astype(f32)
    middle = token_values + gate_one * branch_one
    normed_two, inverse_two = layer_norm(middle)
    hidden_two = (normed_two * (1.0 + scale_two) + shift_two).astype(bf16)
    hidden_two = hidden_two.reshape(own_rows, model_width)
    pre_gelu = dot(hidden_two, up_full) + up_bias_all
    activated = jax.nn.gelu(pre_gelu, approximate=True).astype(bf16)
    branch_two = dot(activated, down_full).reshape(unit_shape) + down_bias.astype(f32)
    result = from_units((middle + gate_two * branch_two).astype(bf16))

    upstream = to_units(cotangent).astype(f32)
    grad_branch_two = (gate_two * upstream).astype(bf16)
    grad_gate_two = jnp.sum(upstream * branch_two, axis=1)
    grad_two = grad_branch_two.reshape(own_rows, model_width)
    grad_down_bias = jnp.sum(grad_two.astype(f32), axis=0)
    grad_down = dot_tn(activated, grad_two).astype(bf16)
    grad_down_sum = lax.psum_scatter(grad_down, "frame", scatter_dimension=0, tiled=True)
    grad_activated = dot_nt(grad_two, down_full)
    gelu_back = jax.vjp(partial(jax.nn.gelu, approximate=True), pre_gelu)[1]
    grad_pre = gelu_back(grad_activated)[0].astype(bf16)
    grad_up_bias = jnp.sum(grad_pre.astype(f32), axis=0)
    grad_up = dot_tn(hidden_two, grad_pre).astype(bf16)
    grad_up_sum = lax.psum_scatter(grad_up, "frame", scatter_dimension=0, tiled=True)
    grad_hidden_two = dot_nt(grad_pre, up_full).reshape(unit_shape)
    grad_scale_two = jnp.sum(grad_hidden_two * normed_two, axis=1)
    grad_shift_two = jnp.sum(grad_hidden_two, axis=1)
    grad_middle = upstream + norm_back(grad_hidden_two * (1.0 + scale_two), normed_two, inverse_two)
    grad_branch_one = (gate_one * grad_middle).astype(bf16)
    grad_gate_one = jnp.sum(grad_middle * branch_one, axis=1)
    grad_one = grad_branch_one.reshape(own_rows, model_width)
    grad_out_bias = jnp.sum(grad_one.astype(f32), axis=0)
    grad_attended = dot_nt(grad_one, out_full).astype(bf16)
    grad_heads = lax.all_to_all(
        grad_attended.reshape(own_rows, frame_devices, lanes),
        "frame",
        split_axis=1,
        concat_axis=0,
        tiled=True,
    ).reshape(all_rows, lanes)
    grad_out = (
        dot_tn(attended, grad_one)
        .astype(bf16)
        .reshape(shard_groups, shard_heads, head_count, head_parts, out_rows, model_width)
        .transpose(1, 3, 0, 2, 4, 5)
        .reshape(frame_devices, tensor_count * out_rows, model_width)
    )
    width_part = model_width // frame_devices
    bias_row = jnp.concatenate(
        [
            grad_down_bias.reshape(frame_devices, width_part),
            grad_out_bias.reshape(frame_devices, width_part),
            grad_up_bias.reshape(frame_devices, tensor_count * hidden_part),
        ],
        axis=1,
    ).astype(bf16)
    bias_row = jnp.pad(
        bias_row[:, None, :], ((0, 0), (0, 15), (0, model_width - bias_row.shape[1]))
    )
    grad_out_sum = lax.psum_scatter(
        jnp.concatenate([grad_out, bias_row], axis=1).reshape(-1, model_width),
        "frame",
        scatter_dimension=0,
        tiled=True,
    )
    bias_sum = grad_out_sum[tensor_count * out_rows]
    down_out_bias = jnp.broadcast_to(bias_sum[: 2 * width_part], (tensor_count, 2 * width_part))
    up_bias_sum = bias_sum[2 * width_part : 2 * width_part + tensor_count * hidden_part].reshape(
        tensor_count, hidden_part
    )
    bias_tail = jnp.concatenate([down_out_bias, up_bias_sum], axis=1)
    bias_tail = jnp.pad(
        bias_tail[:, None, :], ((0, 0), (0, 15), (0, model_width - bias_tail.shape[1]))
    )
    up_tail = (
        grad_up_sum.reshape(up_rows, frame_devices, tensor_count, hidden_part)
        .transpose(2, 0, 1, 3)
        .reshape(tensor_count, -1, model_width)
    )
    tails = [
        grad_down_sum.reshape(tensor_count, hidden_part, model_width),
        up_tail,
        grad_out_sum[: tensor_count * out_rows].reshape(tensor_count, out_rows, model_width),
        bias_tail,
    ]
    sizes = [tail.shape[1] for tail in tails]
    tail_sum = lax.psum_scatter(
        jnp.concatenate(tails, axis=1), "tensor", scatter_dimension=0, tiled=False
    )
    tail_all = lax.all_gather(tail_sum, "frame", axis=0)
    cuts = [0]
    for size in sizes:
        cuts.append(cuts[-1] + size)
    tail_down, tail_up, tail_out, tail_bias = (
        tail_all[:, cuts[n] : cuts[n + 1]].astype(f32) for n in range(4)
    )
    final_down = tail_down.reshape(down_weight.shape)
    final_up = tail_up.reshape(up_weight.shape)
    final_out = tail_out.reshape(out_weight.shape)
    tail_bias = tail_bias[:, 0]
    final_down_bias = tail_bias[:, :width_part].reshape(model_width)
    final_out_bias = tail_bias[:, width_part : 2 * width_part].reshape(model_width)
    final_up_bias = tail_bias[:, 2 * width_part : 2 * width_part + hidden_part].reshape(
        up_bias.shape
    )

    grad_q, grad_k_all, grad_v_all = attend_back(
        queries,
        keys_all,
        values_all,
        attended_heads,
        row_lse,
        grad_heads,
        frame_ids,
        head_count,
        patch_count,
    )
    grad_k = unshare(grad_k_all)
    grad_v = unshare(grad_v_all)
    grad_projected = jnp.concatenate([grad_q, grad_k, grad_v], axis=1)
    grad_hidden_one = lax.psum_scatter(
        dot(grad_projected, head_weight).astype(bf16), "frame", scatter_dimension=0, tiled=True
    )
    grad_hidden_one = grad_hidden_one.astype(f32).reshape(unit_shape)

    grad_head_weight = dot_tn(grad_projected, hidden_all).astype(bf16)
    grad_slots = (
        grad_head_weight.reshape(3, head_count, HD, model_width)
        .transpose(1, 0, 2, 3)
        .reshape(head_count, 3 * HD, model_width)
    )
    grad_head_bias = jnp.stack(
        [jnp.sum(grad_q.astype(f32), axis=0), jnp.sum(grad_v.astype(f32), axis=0)]
    ).astype(bf16)
    grad_head_bias = grad_head_bias.reshape(2, head_count, HD).transpose(1, 0, 2)
    grad_head_bias = jnp.pad(
        grad_head_bias.reshape(head_count, 1, 2 * HD),
        ((0, 0), (0, 15), (0, model_width - 2 * HD)),
    )
    grad_slots = jnp.concatenate([grad_slots, grad_head_bias], axis=1)
    slot_rows = grad_slots.shape[1]
    grad_slots = lax.dynamic_update_slice_in_dim(
        jnp.zeros((tensor_count, slot_rows, model_width), bf16), grad_slots, first_shard, axis=0
    )
    slots_sum = lax.psum_scatter(grad_slots, "tensor", scatter_dimension=0, tiled=False)
    slots_sum = lax.all_gather(slots_sum, "frame", axis=0)
    slots_sum = lax.dynamic_slice_in_dim(
        slots_sum, (tensor_at // head_count) * shard_heads, shard_heads, axis=0
    ).astype(f32)
    final_qkv = (
        slots_sum[:, : 3 * HD]
        .reshape(shard_heads, 3, HD, model_width)
        .transpose(3, 1, 0, 2)
        .reshape(qkv_weight.shape)
    )
    final_qv_bias = (
        slots_sum[:, 3 * HD, : 2 * HD]
        .reshape(shard_heads, 2, HD)
        .transpose(1, 0, 2)
        .reshape(qv_bias.shape)
    )

    grad_scale_one = jnp.sum(grad_hidden_one * normed_one, axis=1)
    grad_shift_one = jnp.sum(grad_hidden_one, axis=1)
    grad_tokens = grad_middle + norm_back(
        grad_hidden_one * (1.0 + scale_one), normed_one, inverse_one
    )
    grad_tokens = from_units(grad_tokens.astype(bf16)).astype(f32)
    grad_modulation = jnp.stack(
        [
            grad_shift_one,
            grad_scale_one,
            grad_gate_one,
            grad_shift_two,
            grad_scale_two,
            grad_gate_two,
        ],
        axis=1,
    )
    grad_mod_local = lax.all_to_all(
        grad_modulation, "tensor", split_axis=2, concat_axis=0, tiled=True
    )
    grad_mod_all = lax.all_gather(grad_mod_local, "frame", axis=0, tiled=True)
    noise_all = lax.all_gather(noise_steps, "frame", axis=0)
    act_all = noise_activation(noise_all, model_width).reshape(-1, model_width)
    grad_ada_weight = jnp.einsum(
        "ud,ukj->dkj", act_all.astype(f32), grad_mod_all, precision=lax.Precision.HIGH
    )
    grad_ada_bias = jnp.sum(grad_mod_all, axis=0)
    return (
        result,
        grad_tokens,
        grad_ada_weight,
        grad_ada_bias,
        final_qkv,
        final_qv_bias,
        final_out,
        final_out_bias,
        final_up,
        final_up_bias,
        final_down,
        final_down_bias,
    )


def solution(mesh):
    in_specs = (
        P(None, "frame", "tensor", None),
        P(None, "frame"),
        P(None, None, "tensor"),
        P(None, "tensor"),
        P(None, None, "tensor"),
        P(None, "tensor"),
        P("tensor", None),
        P(),
        P(None, "tensor"),
        P("tensor"),
        P("tensor", None),
        P(),
        P(None, "frame", "tensor", None),
    )
    out_specs = (
        P(None, "frame", "tensor", None),
        P(None, "frame", "tensor", None),
        P(None, None, "tensor"),
        P(None, "tensor"),
        P(None, None, "tensor"),
        P(None, "tensor"),
        P("tensor", None),
        P(),
        P(None, "tensor"),
        P("tensor"),
        P("tensor", None),
        P(),
    )
    return jax.shard_map(
        on_device, mesh=mesh, in_specs=in_specs, out_specs=out_specs, check_vma=False
    )
```

```python
from functools import partial
import math

import jax
import jax.numpy as jnp
from jax import lax
from jax.experimental import pallas as pl
from jax.experimental.pallas import tpu as pltpu
from jax.sharding import PartitionSpec as P

HD = 64
f32 = jnp.float32
bf16 = jnp.bfloat16
score_scale = HD ** (-0.5)


def noise_embedding(noise_steps, model_width):
    half_width = model_width // 2
    frequency = jnp.exp(-math.log(10000.0) * jnp.arange(half_width, dtype=f32) / half_width)
    angles = noise_steps.astype(f32)[..., None] * frequency
    return jnp.concatenate([jnp.cos(angles), jnp.sin(angles)], axis=-1)


def noise_activation(noise_steps, model_width):
    return jax.nn.silu(noise_embedding(noise_steps, model_width)).astype(bf16)


def layer_norm(values):
    centred = values - jnp.mean(values, axis=-1, keepdims=True)
    inverse = lax.rsqrt(jnp.mean(centred * centred, axis=-1, keepdims=True) + 1e-06)
    return (centred * inverse, inverse)


def norm_back(grad_normed, normed, inverse):
    return inverse * (
        grad_normed
        - jnp.mean(grad_normed, axis=-1, keepdims=True)
        - normed * jnp.mean(grad_normed * normed, axis=-1, keepdims=True)
    )


def dot(left, right):
    return lax.dot_general(left, right, (((1,), (0,)), ((), ())), preferred_element_type=f32)


def dot_nt(left, right):
    return lax.dot_general(left, right, (((1,), (1,)), ((), ())), preferred_element_type=f32)


def dot_tn(left, right):
    return lax.dot_general(left, right, (((0,), (0,)), ((), ())), preferred_element_type=f32)


GROUP = 4


def head_blocks(transposed, head_count):
    rows = lax.broadcasted_iota(jnp.int32, transposed.shape, 0) // HD
    return jnp.concatenate(
        [jnp.where(rows == head, transposed, 0.0) for head in range(head_count)], axis=1
    ).astype(bf16)


def head_rows(natural, head_count):
    lanes = lax.broadcasted_iota(jnp.int32, natural.shape, 1) // HD
    return jnp.concatenate(
        [jnp.where(lanes == head, natural, 0.0) for head in range(head_count)], axis=0
    ).astype(bf16)


def over_key_frames(key_stop, step, carry):
    done = 0
    size = 1
    while size < GROUP:
        once = (key_stop // size) % 2
        carry = lax.fori_loop(
            0, once, lambda _, c, first=done, size=size: step(first, size, c), carry
        )
        done = done + once * size
        size *= 2
    return lax.fori_loop(
        0, key_stop // GROUP, lambda n, c: step(done + GROUP * n, GROUP, c), carry
    )


def attend_kernel(frame_ids, q_ref, k_ref, vt_ref, *refs, head_count, patch_count, first):
    out_ref, lse_ref = refs[-2:]
    key_stop = frame_ids[pl.program_id(0) + first] + 1
    q_cols = head_blocks(jnp.swapaxes(q_ref[...].astype(f32), 0, 1) * score_scale, head_count)
    width = head_count * patch_count

    def step(first, frames, carry):
        row_max, row_total, sums = carry
        start = pl.multiple_of(first * patch_count, patch_count)
        scores = dot(k_ref[pl.ds(start, frames * patch_count), :], q_cols)
        new_max = jnp.maximum(row_max, jnp.max(scores, axis=0, keepdims=True))
        rescale = jnp.exp(row_max - new_max)
        weights = jnp.exp(scores - new_max)
        row_total = row_total * rescale + jnp.sum(weights, axis=0, keepdims=True)
        weights = weights.astype(bf16)
        values_t = vt_ref[:, pl.ds(start, frames * patch_count)]
        parts = []
        for head in range(head_count):
            cols = slice(head * patch_count, (head + 1) * patch_count)
            rows = slice(head * HD, (head + 1) * HD)
            parts.append(sums[head] * rescale[:, cols] + dot(values_t[rows], weights[:, cols]))
        return (new_max, row_total, tuple(parts))

    row_max, row_total, sums = over_key_frames(
        key_stop,
        step,
        (
            jnp.full((1, width), -1e30, f32),
            jnp.zeros((1, width), f32),
            tuple(jnp.zeros((HD, patch_count), f32) for _ in range(head_count)),
        ),
    )
    inverse = 1.0 / row_total
    out_t = jnp.concatenate(
        [
            sums[head] * inverse[:, head * patch_count : (head + 1) * patch_count]
            for head in range(head_count)
        ],
        axis=0,
    )
    out_ref[...] = jnp.swapaxes(out_t, 0, 1).astype(bf16)
    lse_ref[0] = row_max + jnp.log(row_total)


def pair_count(frame_total, first, steps):
    return steps * (frame_total * (2 * first + steps) // (2 * (first + steps)) + 1) // 2


def attend(queries, keys, values_t, frame_ids, head_count, patch_count, first, last, waits):
    lanes = queries.shape[1]
    key_rows = keys.shape[0]
    steps = last - first
    row_count = steps * patch_count
    width = head_count * patch_count
    work = pair_count(key_rows // patch_count, first, steps) * patch_count * width
    return pl.pallas_call(
        partial(
            attend_kernel, head_count=head_count, patch_count=patch_count, first=first
        ),
        grid_spec=pltpu.PrefetchScalarGridSpec(
            num_scalar_prefetch=1,
            grid=(steps,),
            in_specs=[
                pl.BlockSpec((patch_count, lanes), lambda j, ids: (j + first, 0)),
                pl.BlockSpec((key_rows, lanes), lambda j, ids: (0, 0)),
                pl.BlockSpec((lanes, key_rows), lambda j, ids: (0, 0)),
            ]
            + [pl.BlockSpec(memory_space=pl.ANY) for _ in waits],
            out_specs=[
                pl.BlockSpec((patch_count, lanes), lambda j, ids: (j, 0)),
                pl.BlockSpec((1, 1, width), lambda j, ids: (j, 0, 0)),
            ],
        ),
        out_shape=[
            jax.ShapeDtypeStruct((row_count, lanes), bf16),
            jax.ShapeDtypeStruct((steps, 1, width), f32),
        ],
        compiler_params=pltpu.CompilerParams(vmem_limit_bytes=40 << 20),
        cost_estimate=pl.CostEstimate(
            flops=work * 1024, bytes_accessed=8 * row_count * lanes, transcendentals=work
        ),
        name="attend",
    )(frame_ids, queries, keys, values_t, *waits)


def attend_back_kernel(
    frame_ids,
    q_ref,
    grad_ref,
    out_ref,
    lse_ref,
    k_ref,
    v_ref,
    kt_ref,
    *refs,
    head_count,
    patch_count,
    first,
    has_start,
):
    dq_ref, dk_ref, dv_ref, dk_sum, dv_sum = refs[-5:]
    position = pl.program_id(0)
    key_stop = frame_ids[position + first] + 1

    @pl.when(position == 0)
    def _():
        dk_sum[...] = refs[0][...] if has_start else jnp.zeros_like(dk_sum)
        dv_sum[...] = refs[1][...] if has_start else jnp.zeros_like(dv_sum)

    q_rows = q_ref[...].astype(f32) * score_scale
    grad_rows = grad_ref[...].astype(f32)
    grad_t = jnp.swapaxes(grad_rows, 0, 1)
    grad_out_t = grad_t * jnp.swapaxes(out_ref[...].astype(f32), 0, 1)
    delta = jnp.concatenate(
        [
            jnp.sum(grad_out_t[head * HD : (head + 1) * HD], axis=0, keepdims=True)
            for head in range(head_count)
        ],
        axis=1,
    )
    q_cols = head_blocks(jnp.swapaxes(q_rows, 0, 1), head_count)
    grad_cols = head_blocks(grad_t, head_count)
    q_stack = head_rows(q_rows, head_count)
    grad_stack = head_rows(grad_rows, head_count)
    lse = lse_ref[0]

    def step(first, frames, sums):
        start = pl.multiple_of(first * patch_count, patch_count)
        here = pl.ds(start, frames * patch_count)
        scores = dot(k_ref[here, :], q_cols)
        grad_probs = dot(v_ref[here, :], grad_cols)
        probs = jnp.exp(scores - lse)
        grad_scores = (probs * (grad_probs - delta)).astype(bf16)
        dv_sum[here, :] += dot(probs.astype(bf16), grad_stack)
        dk_sum[here, :] += dot(grad_scores, q_stack)
        keys_t = kt_ref[:, here]
        return tuple(
            sums[head]
            + dot(
                keys_t[head * HD : (head + 1) * HD],
                grad_scores[:, head * patch_count : (head + 1) * patch_count],
            )
            for head in range(head_count)
        )

    sums = over_key_frames(
        key_stop, step, tuple(jnp.zeros((HD, patch_count), f32) for _ in range(head_count))
    )
    dq_t = jnp.concatenate(sums, axis=0) * score_scale
    dq_ref[...] = jnp.swapaxes(dq_t, 0, 1).astype(bf16)

    @pl.when(position == pl.num_programs(0) - 1)
    def _():
        dk_ref[...] = dk_sum[...].astype(dk_ref.dtype)
        dv_ref[...] = dv_sum[...].astype(dv_ref.dtype)


def attend_back(
    queries, keys, values, keys_t, out, lse, grad, frame_ids, head_count, patch_count, first, last, start, sum_type, waits
):
    lanes = queries.shape[1]
    key_rows = keys.shape[0]
    steps = last - first
    row_count = steps * patch_count
    width = head_count * patch_count
    work = pair_count(key_rows // patch_count, first, steps) * patch_count * width
    block = pl.BlockSpec((patch_count, lanes), lambda j, ids: (j + first, 0))
    whole = pl.BlockSpec((key_rows, lanes), lambda j, ids: (0, 0))
    return pl.pallas_call(
        partial(
            attend_back_kernel,
            head_count=head_count,
            patch_count=patch_count,
            first=first,
            has_start=len(start) > 0,
        ),
        grid_spec=pltpu.PrefetchScalarGridSpec(
            num_scalar_prefetch=1,
            grid=(steps,),
            in_specs=[
                block,
                block,
                block,
                pl.BlockSpec((1, 1, width), lambda j, ids: (j + first, 0, 0)),
                whole,
                whole,
                pl.BlockSpec((lanes, key_rows), lambda j, ids: (0, 0)),
            ]
            + [whole for _ in start]
            + [pl.BlockSpec(memory_space=pl.ANY) for _ in waits],
            out_specs=[
                pl.BlockSpec((patch_count, lanes), lambda j, ids: (j, 0)),
                whole,
                whole,
            ],
            scratch_shapes=[
                pltpu.VMEM((key_rows, lanes), f32),
                pltpu.VMEM((key_rows, lanes), f32),
            ],
        ),
        out_shape=[
            jax.ShapeDtypeStruct((row_count, lanes), bf16),
            jax.ShapeDtypeStruct((key_rows, lanes), sum_type),
            jax.ShapeDtypeStruct((key_rows, lanes), sum_type),
        ],
        compiler_params=pltpu.CompilerParams(vmem_limit_bytes=48 << 20),
        cost_estimate=pl.CostEstimate(
            flops=work * 2560, bytes_accessed=16 * row_count * lanes, transcendentals=work
        ),
        name="attend_back",
    )(frame_ids, queries, grad, out, lse, keys, values, keys_t, *start, *waits)


def mlp_kernel(
    core_ref,
    hidden_ref,
    grad_ref,
    bias_ref,
    bias_other_ref,
    up_ref,
    up_other_ref,
    down_ref,
    down_other_ref,
    branch_ref,
    back_ref,
    keep_ref,
    send_ref,
    keep_bias_ref,
    send_bias_ref,
    hidden_t,
    grad_t,
):
    step = pl.program_id(0)
    rows, width = hidden_ref.shape

    @pl.when(step == 0)
    def _():
        branch_ref[...] = jnp.zeros_like(branch_ref)
        back_ref[...] = jnp.zeros_like(back_ref)
        for start in range(0, width, 256):
            cols = slice(start, start + 256)
            hidden_t[cols, :] = jnp.swapaxes(hidden_ref[:, cols].astype(f32), 0, 1).astype(bf16)
            grad_t[cols, :] = jnp.swapaxes(grad_ref[:, cols].astype(f32), 0, 1).astype(bf16)

    slope = math.sqrt(2.0 / math.pi)
    for up, down, bias, out_ref, out_bias_ref in (
        (up_other_ref, down_other_ref, bias_other_ref, send_ref, send_bias_ref),
        (up_ref, down_ref, bias_ref, keep_ref, keep_bias_ref),
    ):
        shards, part = up.shape[1], up.shape[2]
        units = shards * part
        up_rows = up[0].reshape(units, width)
        down_rows = down[0].reshape(units, width)
        pre = dot(up_rows, hidden_t[...]) + bias[0]
        square = pre * pre
        bend = jnp.tanh(slope * pre * (1.0 + 0.044715 * square))
        activated = (0.5 * pre * (1.0 + bend)).astype(bf16)
        gain = 0.5 * (1.0 + bend) + (0.5 * slope) * pre * (1.0 - bend * bend) * (
            1.0 + (3 * 0.044715) * square
        )
        grad_pre = (dot(down_rows, grad_t[...]) * gain).astype(bf16)
        out_bias_ref[0] = jnp.sum(grad_pre.astype(f32), axis=1, keepdims=True)
        out_ref[0, :, :part, :] = (
            dot(grad_pre, hidden_ref[...]).astype(bf16).reshape(shards, part, width)
        )
        out_ref[0, :, part:, :] = (
            dot(activated, grad_ref[...]).astype(bf16).reshape(shards, part, width)
        )
        branch_ref[...] += dot_tn(activated, down_rows)
        back_ref[...] += dot_tn(grad_pre, up_rows)


def mlp(core, hidden, grad, bias, weights, part):
    frame_parts, shards, _, width = weights.shape
    rows = hidden.shape[0]
    steps = frame_parts // 2
    units = shards * part

    def own(m, c):
        return 2 * m + c[0]

    def other(m, c):
        return 2 * m + 1 - c[0]

    def weight_spec(which, row):
        return pl.BlockSpec((1, shards, part, width), lambda m, c: (which(m, c), 0, row, 0))

    whole = pl.BlockSpec((rows, width), lambda m, c: (0, 0), pipeline_mode=pl.Buffered(1))
    sums = pl.BlockSpec((rows, width), lambda m, c: (0, 0))
    out = pl.BlockSpec((1, shards, 2 * part, width), lambda m, c: (m, 0, 0, 0))
    column = pl.BlockSpec((1, units, 1), lambda m, c: (m, 0, 0))
    work = rows * width * units * frame_parts
    return pl.pallas_call(
        mlp_kernel,
        grid_spec=pltpu.PrefetchScalarGridSpec(
            num_scalar_prefetch=1,
            grid=(steps,),
            in_specs=[
                whole,
                whole,
                pl.BlockSpec((1, units, 1), lambda m, c: (own(m, c), 0, 0)),
                pl.BlockSpec((1, units, 1), lambda m, c: (other(m, c), 0, 0)),
                weight_spec(own, 0),
                weight_spec(other, 0),
                weight_spec(own, 1),
                weight_spec(other, 1),
            ],
            out_specs=[sums, sums, out, out, column, column],
            scratch_shapes=[pltpu.VMEM((width, rows), bf16), pltpu.VMEM((width, rows), bf16)],
        ),
        out_shape=[
            jax.ShapeDtypeStruct((rows, width), f32),
            jax.ShapeDtypeStruct((rows, width), f32),
            jax.ShapeDtypeStruct((steps, shards, 2 * part, width), bf16),
            jax.ShapeDtypeStruct((steps, shards, 2 * part, width), bf16),
            jax.ShapeDtypeStruct((steps, units, 1), f32),
            jax.ShapeDtypeStruct((steps, units, 1), f32),
        ],
        compiler_params=pltpu.CompilerParams(vmem_limit_bytes=48 << 20),
        cost_estimate=pl.CostEstimate(
            flops=12 * work,
            bytes_accessed=frame_parts * units * width * 8,
            transcendentals=rows * units * frame_parts,
        ),
        name="mlp",
    )(core, hidden, grad, bias, bias, weights, weights, weights, weights)


def after(value, *others):
    return lax.optimization_barrier((value,) + others)[0]


def on_device(
    tokens,
    noise_steps,
    ada_weight,
    ada_bias,
    qkv_weight,
    qv_bias,
    out_weight,
    out_bias,
    up_weight,
    up_bias,
    down_weight,
    down_bias,
    cotangent,
):
    clip_count, local_frames, local_patches, model_width = tokens.shape
    tensor_count = lax.axis_size("tensor")
    frame_devices = lax.axis_size("frame")
    frame_at = lax.axis_index("frame")
    tensor_at = lax.axis_index("tensor")
    patch_count = local_patches * tensor_count
    hidden_width = up_weight.shape[1] * tensor_count
    head_total = model_width // HD
    shard_heads = head_total // tensor_count
    head_count = head_total // frame_devices
    lanes = head_count * HD
    unit_total = clip_count * local_frames
    units = unit_total // tensor_count
    sharers = tensor_count // clip_count
    share_at = tensor_at % sharers
    own_rows = units * patch_count
    all_rows = frame_devices * own_rows
    slot = frame_at % shard_heads
    group_at = frame_at // shard_heads
    shard_groups = tensor_count // head_count
    shard_base = (tensor_at // sharers) * sharers
    core = frame_at % 2
    chips = frame_devices // 2
    unit_shape = (units, patch_count, model_width)
    column_part = model_width // tensor_count


    def swap_frame(values):
        return lax.all_to_all(values, "frame", split_axis=0, concat_axis=0, tiled=True)

    def shifted(values, shift):
        return lax.ppermute(
            values, "tensor", [(t, (t + shift) % tensor_count) for t in range(tensor_count)]
        )

    def tensor_parts(values):
        return [shifted(values, tensor_count - 1 - n) for n in range(tensor_count - 1)] + [values]

    def tensor_sum(parts):
        total = parts[-1].astype(f32)
        for n in range(tensor_count - 1):
            total = total + shifted(parts[n], n + 1).astype(f32)
        return total

    def exchange(parts):
        last = tensor_count - 1
        return [shifted(parts[last - 1 - n], last - n) for n in range(last)] + [parts[last]]

    def to_relative(values):
        return [
            lax.dynamic_index_in_dim(
                values, (tensor_at + 1 + n) % tensor_count, 0, keepdims=False
            )
            for n in range(tensor_count)
        ]

    def rolled(values, start):
        return lax.dynamic_slice_in_dim(
            jnp.concatenate([values, values]), start % tensor_count, tensor_count, axis=0
        )

    def from_relative(parts, first=0):
        return rolled(jnp.stack(parts), first - tensor_at - 1)

    def head_pairs(head, member):
        pairs = []
        for i in range(frame_devices):
            for t in range(member, tensor_count, sharers):
                shard = (t - member + i // shard_heads + head * shard_groups) % tensor_count
                pairs.append((i * tensor_count + shard, i * tensor_count + t))
        return pairs

    def from_owners(values, head):
        total = None
        for member in range(sharers):
            got = lax.ppermute(values, ("frame", "tensor"), head_pairs(head, member))
            total = got if total is None else total + got
        return total

    def to_owners(pieces):
        total = 0.0
        for head, piece in enumerate(pieces):
            for member in range(sharers):
                pairs = [(user, owner) for owner, user in head_pairs(head, member)]
                total = total + lax.ppermute(piece, ("frame", "tensor"), pairs).astype(f32)
        return total.astype(bf16)

    def to_units(values):
        parts = to_relative(
            values.reshape(tensor_count, units, local_patches, model_width)
        )
        return jnp.stack(exchange(parts), axis=1).reshape(units, patch_count, model_width)

    def from_units(values):
        parts = values.reshape(units, tensor_count, local_patches, model_width)
        return from_relative(exchange([parts[:, n] for n in range(tensor_count)])).reshape(
            clip_count, local_frames, local_patches, model_width
        )

    def core_sum(keep, send):
        got = lax.ppermute(send, "frame", [(i, i ^ 1) for i in range(frame_devices)])
        return keep + got

    def scatter(values):
        return lax.psum_scatter(
            values.reshape(-1, model_width),
            "frame",
            scatter_dimension=0,
            axis_index_groups=[list(range(c, frame_devices, 2)) for c in range(2)],
            tiled=True,
        ).reshape(values.shape[1:])

    def frame_parts(values):
        return (
            lax.all_gather(values.astype(bf16), "frame", axis=0, tiled=True)
            .reshape(frame_devices, -1, model_width)
            .astype(f32)
        )

    unit_tokens = to_units(tokens)
    act_noise = noise_activation(noise_steps, model_width).reshape(unit_total, model_width)
    mod_local = jnp.einsum(
        "ud,dkj->ukj", act_noise, ada_weight, preferred_element_type=f32
    ) + ada_bias.astype(f32)
    modulation = (
        from_relative(
            exchange(to_relative(mod_local.reshape(tensor_count, units * 6, column_part)))
        )
        .reshape(tensor_count, units, 6, column_part)
        .transpose(1, 2, 0, 3)
        .reshape(units, 6, model_width)
    )
    shift_one = modulation[:, None, 0]
    scale_one = modulation[:, None, 1]
    gate_one = modulation[:, None, 2]
    shift_two = modulation[:, None, 3]
    scale_two = modulation[:, None, 4]
    gate_two = modulation[:, None, 5]

    slot_weight = lax.dynamic_slice_in_dim(qkv_weight, slot * HD, HD, axis=2)
    slot_weight = slot_weight.transpose(1, 2, 0).reshape(3 * HD, model_width)
    slot_bias = lax.dynamic_slice_in_dim(qv_bias, slot * HD, HD, axis=1).reshape(1, 2 * HD)
    slot_bias = jnp.pad(slot_bias, ((0, 15), (0, model_width - 2 * HD)))
    slot_pack = jnp.concatenate([slot_weight, slot_bias])

    def own_part(values):
        size = values.shape[0] // frame_devices
        return lax.dynamic_slice_in_dim(values, frame_at * size, size, axis=0)

    hidden_part = hidden_width // (tensor_count * frame_devices)
    half = hidden_part // 2
    out_rows = out_weight.shape[0] // frame_devices
    up_part = lax.dynamic_slice_in_dim(
        up_weight, frame_at * hidden_part, hidden_part, axis=1
    ).transpose(1, 0)
    down_part = own_part(down_weight)
    bias_part = lax.dynamic_slice_in_dim(up_bias, frame_at * hidden_part, hidden_part, axis=0)
    bias_part = jnp.pad(bias_part[None, :], ((0, 15), (0, model_width - hidden_part)))
    first_pack = jnp.concatenate([up_part[:half], down_part[:half], bias_part])
    second_pack = jnp.concatenate([up_part[half:], down_part[half:]])
    out_pack = own_part(out_weight)
    slot_pack = after(slot_pack, unit_tokens)
    head_pack = jnp.stack([from_owners(slot_pack, head) for head in range(head_count)])
    first_list = tensor_parts(after(jnp.concatenate([first_pack, out_pack]), head_pack))
    out_at = first_pack.shape[0]
    first_parts = jnp.concatenate(
        [
            from_relative([part[:out_at] for part in first_list]),
            from_relative([part[out_at:] for part in first_list], shard_base),
        ],
        axis=1,
    ).reshape(-1, model_width)
    head_weight = (
        head_pack[:, : 3 * HD]
        .reshape(head_count, 3, HD, model_width)
        .transpose(1, 0, 2, 3)
        .reshape(3 * lanes, model_width)
    )
    head_bias = head_pack[:, 3 * HD, : 2 * HD]
    head_bias = head_bias.reshape(head_count, 2, HD).transpose(1, 0, 2).reshape(2, lanes)
    head_bias = head_bias.astype(f32)
    qkv_bias = jnp.concatenate([head_bias[0], jnp.zeros((lanes,), f32), head_bias[1]])

    token_values = unit_tokens.astype(f32)
    normed_one, inverse_one = layer_norm(token_values)
    hidden_one = (normed_one * (1.0 + scale_one) + shift_one).astype(bf16)
    hidden_all = lax.all_gather(
        hidden_one.reshape(own_rows, model_width), "frame", axis=0, tiled=True
    )

    first_all = lax.all_gather(first_parts, "frame", axis=0, tiled=True)
    first_all = first_all.reshape(frame_devices, tensor_count, -1, model_width)
    up_bias_all = first_all[:, :, 2 * half, :hidden_part].astype(f32)
    first_bias = up_bias_all[:, :, :half].reshape(frame_devices, tensor_count * half, 1)
    second_bias = up_bias_all[:, :, half:].reshape(frame_devices, tensor_count * half, 1)
    head_parts = HD // out_rows
    out_full = (
        first_all[:, :, 2 * half + 16 :]
        .reshape(shard_heads, head_parts, head_count, shard_groups, out_rows, model_width)
        .transpose(3, 0, 2, 1, 4, 5)
        .reshape(model_width, model_width)
    )

    projected = (dot_nt(hidden_all, head_weight) + qkv_bias).astype(bf16)
    queries = projected[:, :lanes]
    keys = projected[:, lanes : 2 * lanes]
    values = projected[:, 2 * lanes :]

    def share(mine):
        if sharers == 1:
            return mine
        pieces = [mine]
        for shift in range(1, sharers):
            perm = [
                (t, (t // sharers) * sharers + (t + shift) % sharers) for t in range(tensor_count)
            ]
            pieces.append(lax.ppermute(mine, "tensor", perm))
        stacked = jnp.stack(pieces)
        stacked = jnp.stack(
            [
                lax.dynamic_index_in_dim(
                    stacked, (share_at - member) % sharers, 0, keepdims=False
                )
                for member in range(sharers)
            ]
        )
        return (
            stacked.reshape(sharers, frame_devices, own_rows, lanes)
            .transpose(1, 0, 2, 3)
            .reshape(sharers * all_rows, lanes)
        )

    def unshare(partial_sums):
        if sharers == 1:
            return partial_sums
        pieces = (
            partial_sums.reshape(frame_devices, sharers, own_rows, lanes)
            .transpose(1, 0, 2, 3)
            .reshape(sharers, all_rows, lanes)
        )
        total = lax.dynamic_index_in_dim(pieces, share_at, 0, keepdims=False).astype(f32)
        for shift in range(1, sharers):
            perm = [
                (t, (t // sharers) * sharers + (t + shift) % sharers) for t in range(tensor_count)
            ]
            piece = lax.dynamic_index_in_dim(
                pieces, (share_at + shift) % sharers, 0, keepdims=False
            )
            total = total + lax.ppermute(piece, "tensor", perm).astype(f32)
        return total.astype(bf16)

    keys_all = share(keys)
    values_all = share(values)
    unit_ids = jnp.arange(frame_devices * units, dtype=jnp.int32)
    frame_ids = (
        (unit_ids // units) * local_frames + share_at.astype(jnp.int32) * units + unit_ids % units
    )
    values_t = values_all.T
    steps = all_rows // patch_count
    second_list = tensor_parts(after(second_pack, queries))
    cut = steps * 11 // 16
    heads_a, lse_a = attend(
        queries, keys_all, values_t, frame_ids, head_count, patch_count, 0, cut, ()
    )
    heads_a, *second_list = lax.optimization_barrier((heads_a, *second_list))
    second_parts = from_relative(second_list)
    upstream = to_units(after(cotangent, second_parts)).astype(f32)
    heads_b, lse_b = attend(
        queries, keys_all, values_t, frame_ids, head_count, patch_count, cut, steps,
        (second_parts,),
    )
    attended_heads = jnp.concatenate([heads_a, heads_b])
    row_lse = jnp.concatenate([lse_a, lse_b])
    second_all = lax.all_gather(
        second_parts.reshape(-1, model_width), "frame", axis=0, tiled=True
    ).reshape(frame_devices, tensor_count, -1, model_width)
    attended = (
        swap_frame(attended_heads.reshape(frame_devices, own_rows, lanes))
        .transpose(1, 0, 2)
        .reshape(own_rows, model_width)
    )

    grad_two = (gate_two * upstream).astype(bf16).reshape(own_rows, model_width)
    grad_down_bias = jnp.sum(grad_two.astype(f32), axis=0)

    branch_one = dot(attended, out_full).reshape(unit_shape) + out_bias.astype(f32)
    middle = token_values + gate_one * branch_one
    normed_two, inverse_two = layer_norm(middle)
    hidden_two = (normed_two * (1.0 + scale_two) + shift_two).astype(bf16)
    hidden_two = hidden_two.reshape(own_rows, model_width)

    core_id = core.astype(jnp.int32).reshape(1)
    branch_a, back_a, keep_a, send_a, keep_bias_a, send_bias_a = mlp(
        core_id, hidden_two, grad_two, first_bias, first_all, half
    )
    first_half = core_sum(keep_a, send_a)
    branch_b, back_b, keep_b, send_b, keep_bias_b, send_bias_b = mlp(
        core_id, hidden_two, grad_two, second_bias, second_all, half
    )
    second_half = core_sum(keep_b, send_b)
    back_b, first_half = lax.optimization_barrier((back_b, first_half))
    first_sum = scatter(first_half)
    branch_two = (branch_a + branch_b).reshape(unit_shape) + down_bias.astype(f32)
    result = from_units((middle + gate_two * branch_two).astype(bf16))
    grad_gate_two = jnp.sum(upstream * branch_two, axis=1)
    grad_hidden_two = (back_a + back_b).reshape(unit_shape)
    grad_scale_two = jnp.sum(grad_hidden_two * normed_two, axis=1)
    grad_shift_two = jnp.sum(grad_hidden_two, axis=1)
    grad_middle = upstream + norm_back(grad_hidden_two * (1.0 + scale_two), normed_two, inverse_two)
    grad_branch_one = (gate_one * grad_middle).astype(bf16)
    grad_gate_one = jnp.sum(grad_middle * branch_one, axis=1)
    grad_one = grad_branch_one.reshape(own_rows, model_width)
    grad_out_bias = jnp.sum(grad_one.astype(f32), axis=0)
    grad_attended = dot_nt(grad_one, out_full).astype(bf16)
    grad_heads = swap_frame(
        grad_attended.reshape(own_rows, frame_devices, lanes).transpose(1, 0, 2)
    ).reshape(all_rows, lanes)

    grad_out = (
        dot_tn(attended, grad_one)
        .astype(bf16)
        .reshape(shard_groups, shard_heads, head_count, head_parts, out_rows, model_width)
        .transpose(2, 0, 1, 3, 4, 5)
        .reshape(tensor_count, frame_devices, out_rows, model_width)
    )
    grad_out = rolled(grad_out, -shard_base).transpose(1, 0, 2, 3)
    width_part = model_width // frame_devices

    def by_core(keep_part, send_part):
        pair = jnp.stack([keep_part, send_part], axis=1)
        return jnp.where(core == 0, pair, pair[:, ::-1]).reshape(
            (frame_devices,) + keep_part.shape[1:]
        )

    grad_up_bias = jnp.concatenate(
        [
            by_core(keep_bias_a, send_bias_a).reshape(frame_devices, tensor_count, half),
            by_core(keep_bias_b, send_bias_b).reshape(frame_devices, tensor_count, half),
        ],
        axis=2,
    )
    once = jnp.concatenate(
        [
            grad_down_bias.reshape(frame_devices, 1, width_part),
            grad_out_bias.reshape(frame_devices, 1, width_part),
        ],
        axis=2,
    )
    bias_row = jnp.concatenate(
        [jnp.broadcast_to(once, (frame_devices, tensor_count, 2 * width_part)), grad_up_bias],
        axis=2,
    ).astype(bf16)
    bias_row = jnp.pad(
        bias_row[:, :, None, :], ((0, 0), (0, 0), (0, 15), (0, model_width - bias_row.shape[2]))
    )
    out_pairs = jnp.concatenate([grad_out, bias_row], axis=2).reshape(
        chips, 2, tensor_count, out_rows + 16, model_width
    )
    out_half = core_sum(
        lax.dynamic_index_in_dim(out_pairs, core, 1, keepdims=False),
        lax.dynamic_index_in_dim(out_pairs, 1 - core, 1, keepdims=False),
    )
    late_half = jnp.concatenate([second_half, out_half], axis=2)
    late_sum = scatter(late_half)
    first_total = tensor_sum(to_relative(first_sum)).astype(bf16)

    keys_t = keys_all.T
    grad_q_a, *sums = attend_back(
        queries, keys_all, values_all, keys_t, attended_heads, row_lse, grad_heads,
        frame_ids, head_count, patch_count, 0, cut, (), f32, (late_half, result),
    )
    grad_q_b, grad_k_all, grad_v_all = attend_back(
        queries, keys_all, values_all, keys_t, attended_heads, row_lse, grad_heads,
        frame_ids, head_count, patch_count, cut, steps, tuple(sums), bf16, (first_total,),
    )
    grad_q = jnp.concatenate([grad_q_a, grad_q_b])
    grad_k = unshare(grad_k_all)
    grad_v = unshare(grad_v_all)
    grad_projected = jnp.concatenate([grad_q, grad_k, grad_v], axis=1)
    grad_hidden_part = dot(grad_projected, head_weight).astype(bf16)
    grad_hidden_one = lax.psum_scatter(grad_hidden_part, "frame", scatter_dimension=0, tiled=True)
    grad_hidden_one = grad_hidden_one.astype(f32).reshape(unit_shape)

    late_total = tensor_sum(to_relative(late_sum)).astype(bf16)
    grad_head_weight = dot_tn(after(grad_projected, grad_hidden_part), hidden_all).astype(bf16)
    grad_slots = (
        grad_head_weight.reshape(3, head_count, HD, model_width)
        .transpose(1, 0, 2, 3)
        .reshape(head_count, 3 * HD, model_width)
    )
    grad_head_bias = jnp.stack(
        [jnp.sum(grad_q.astype(f32), axis=0), jnp.sum(grad_v.astype(f32), axis=0)]
    ).astype(bf16)
    grad_head_bias = grad_head_bias.reshape(2, head_count, HD).transpose(1, 0, 2)
    grad_head_bias = jnp.pad(
        grad_head_bias.reshape(head_count, 1, 2 * HD),
        ((0, 0), (0, 15), (0, model_width - 2 * HD)),
    )
    grad_slots = jnp.concatenate([grad_slots, grad_head_bias], axis=1)

    slots_total = to_owners([grad_slots[head] for head in range(head_count)])

    grad_scale_one = jnp.sum(grad_hidden_one * normed_one, axis=1)
    grad_shift_one = jnp.sum(grad_hidden_one, axis=1)
    grad_tokens = (
        grad_middle
        + norm_back(grad_hidden_one * (1.0 + scale_one), normed_one, inverse_one)
    ).astype(bf16)
    tail_sums, grad_tokens = lax.optimization_barrier(
        (jnp.concatenate([first_total, late_total]), grad_tokens)
    )
    tail_all = frame_parts(tail_sums)
    slots_sum = frame_parts(slots_total)
    late_tail = tail_all[:, 2 * half :]
    first_tail = tail_all[:, : 2 * half]
    up_first, down_first = first_tail[:, :half], first_tail[:, half:]
    up_second, down_second = late_tail[:, :half], late_tail[:, half : 2 * half]
    tail_out = late_tail[:, 2 * half : 2 * half + out_rows]
    tail_bias = late_tail[:, 2 * half + out_rows :]
    final_up = (
        jnp.concatenate([up_first, up_second], axis=1)
        .reshape(frame_devices * hidden_part, model_width)
        .transpose(1, 0)
    )
    final_down = jnp.concatenate([down_first, down_second], axis=1).reshape(down_weight.shape)
    final_out = tail_out.reshape(out_weight.shape)
    tail_bias = tail_bias[:, 0]
    final_down_bias = tail_bias[:, :width_part].reshape(model_width)
    final_out_bias = tail_bias[:, width_part : 2 * width_part].reshape(model_width)
    final_up_bias = tail_bias[:, 2 * width_part : 2 * width_part + hidden_part].reshape(
        up_bias.shape
    )
    slots_sum, final_up, final_down, final_out = lax.optimization_barrier(
        (slots_sum, final_up, final_down, final_out)
    )
    slots_sum = jnp.sum(
        slots_sum.reshape(shard_groups, shard_heads, -1, model_width), axis=0
    )
    final_qkv = (
        slots_sum[:, : 3 * HD]
        .reshape(shard_heads, 3, HD, model_width)
        .transpose(3, 1, 0, 2)
        .reshape(qkv_weight.shape)
    )
    final_qv_bias = (
        slots_sum[:, 3 * HD, : 2 * HD]
        .reshape(shard_heads, 2, HD)
        .transpose(1, 0, 2)
        .reshape(qv_bias.shape)
    )

    grad_tokens = from_units(grad_tokens).astype(f32)
    grad_modulation = jnp.stack(
        [
            grad_shift_one,
            grad_scale_one,
            grad_gate_one,
            grad_shift_two,
            grad_scale_two,
            grad_gate_two,
        ],
        axis=1,
    )
    unit_steps = lax.dynamic_slice_in_dim(
        noise_steps.reshape(unit_total), tensor_at * units, units
    ).astype(f32)
    grad_mod_parts = exchange(
        to_relative(
            jnp.concatenate(
                [
                    grad_modulation.reshape(units, 6, tensor_count, column_part)
                    .transpose(2, 0, 1, 3)
                    .reshape(tensor_count, units, 6 * column_part),
                    jnp.broadcast_to(unit_steps[None, :, None], (tensor_count, units, 128)),
                ],
                axis=2,
            )
        )
    )
    grad_mod_all = lax.all_gather(
        jnp.stack(grad_mod_parts).reshape(unit_total, -1), "frame", axis=0, tiled=True
    )
    act_all = noise_activation(grad_mod_all[:, -1], model_width)
    grad_mod_all = grad_mod_all[:, :-128].reshape(-1, 6, column_part)
    grad_ada_weight = jnp.einsum(
        "ud,ukj->dkj", act_all.astype(f32), grad_mod_all, precision=lax.Precision.HIGH
    )
    grad_ada_bias = jnp.sum(grad_mod_all, axis=0)
    return (
        result,
        grad_tokens,
        grad_ada_weight,
        grad_ada_bias,
        final_qkv,
        final_qv_bias,
        final_out,
        final_out_bias,
        final_up,
        final_up_bias,
        final_down,
        final_down_bias,
    )


def solution(mesh):
    in_specs = (
        P(None, "frame", "tensor", None),
        P(None, "frame"),
        P(None, None, "tensor"),
        P(None, "tensor"),
        P(None, None, "tensor"),
        P(None, "tensor"),
        P("tensor", None),
        P(),
        P(None, "tensor"),
        P("tensor"),
        P("tensor", None),
        P(),
        P(None, "frame", "tensor", None),
    )
    out_specs = (
        P(None, "frame", "tensor", None),
        P(None, "frame", "tensor", None),
        P(None, None, "tensor"),
        P(None, "tensor"),
        P(None, None, "tensor"),
        P(None, "tensor"),
        P("tensor", None),
        P(),
        P(None, "tensor"),
        P("tensor"),
        P("tensor", None),
        P(),
    )
    return jax.shard_map(
        on_device, mesh=mesh, in_specs=in_specs, out_specs=out_specs, check_vma=False
    )
```

```python
from functools import partial
import math

import jax
import jax.numpy as jnp
from jax import lax
from jax.experimental import pallas as pl
from jax.experimental.pallas import tpu as pltpu
from jax.sharding import PartitionSpec as P

HD = 64
f32 = jnp.float32
bf16 = jnp.bfloat16
score_scale = HD ** (-0.5)


def noise_embedding(noise_steps, model_width):
    half_width = model_width // 2
    frequency = jnp.exp(-math.log(10000.0) * jnp.arange(half_width, dtype=f32) / half_width)
    angles = noise_steps.astype(f32)[..., None] * frequency
    return jnp.concatenate([jnp.cos(angles), jnp.sin(angles)], axis=-1)


def noise_activation(noise_steps, model_width):
    return jax.nn.silu(noise_embedding(noise_steps, model_width)).astype(bf16)


def layer_norm(values):
    centred = values - jnp.mean(values, axis=-1, keepdims=True)
    inverse = lax.rsqrt(jnp.mean(centred * centred, axis=-1, keepdims=True) + 1e-06)
    return (centred * inverse, inverse)


def norm_back(grad_normed, normed, inverse):
    return inverse * (
        grad_normed
        - jnp.mean(grad_normed, axis=-1, keepdims=True)
        - normed * jnp.mean(grad_normed * normed, axis=-1, keepdims=True)
    )


def dot(left, right):
    return lax.dot_general(left, right, (((1,), (0,)), ((), ())), preferred_element_type=f32)


def dot_nt(left, right):
    return lax.dot_general(left, right, (((1,), (1,)), ((), ())), preferred_element_type=f32)


def dot_tn(left, right):
    return lax.dot_general(left, right, (((0,), (0,)), ((), ())), preferred_element_type=f32)


GROUP = 4


def head_blocks(transposed, head_count):
    rows = lax.broadcasted_iota(jnp.int32, transposed.shape, 0) // HD
    return jnp.concatenate(
        [jnp.where(rows == head, transposed, 0.0) for head in range(head_count)], axis=1
    ).astype(bf16)


def head_rows(natural, head_count):
    lanes = lax.broadcasted_iota(jnp.int32, natural.shape, 1) // HD
    return jnp.concatenate(
        [jnp.where(lanes == head, natural, 0.0) for head in range(head_count)], axis=0
    ).astype(bf16)


def over_key_frames(key_stop, step, carry):
    done = 0
    size = 1
    while size < GROUP:
        once = (key_stop // size) % 2
        carry = lax.fori_loop(
            0, once, lambda _, c, first=done, size=size: step(first, size, c), carry
        )
        done = done + once * size
        size *= 2
    return lax.fori_loop(
        0, key_stop // GROUP, lambda n, c: step(done + GROUP * n, GROUP, c), carry
    )


def attend_kernel(frame_ids, q_ref, k_ref, vt_ref, *refs, head_count, patch_count, first):
    out_ref, lse_ref = refs[-2:]
    key_stop = frame_ids[pl.program_id(0) + first] + 1
    q_cols = head_blocks(jnp.swapaxes(q_ref[...].astype(f32), 0, 1) * score_scale, head_count)
    width = head_count * patch_count

    def step(first, frames, carry):
        row_max, row_total, sums = carry
        start = pl.multiple_of(first * patch_count, patch_count)
        scores = dot(k_ref[pl.ds(start, frames * patch_count), :], q_cols)
        new_max = jnp.maximum(row_max, jnp.max(scores, axis=0, keepdims=True))
        rescale = jnp.exp(row_max - new_max)
        weights = jnp.exp(scores - new_max)
        row_total = row_total * rescale + jnp.sum(weights, axis=0, keepdims=True)
        weights = weights.astype(bf16)
        values_t = vt_ref[:, pl.ds(start, frames * patch_count)]
        parts = []
        for head in range(head_count):
            cols = slice(head * patch_count, (head + 1) * patch_count)
            rows = slice(head * HD, (head + 1) * HD)
            parts.append(sums[head] * rescale[:, cols] + dot(values_t[rows], weights[:, cols]))
        return (new_max, row_total, tuple(parts))

    row_max, row_total, sums = over_key_frames(
        key_stop,
        step,
        (
            jnp.full((1, width), -1e30, f32),
            jnp.zeros((1, width), f32),
            tuple(jnp.zeros((HD, patch_count), f32) for _ in range(head_count)),
        ),
    )
    inverse = 1.0 / row_total
    out_t = jnp.concatenate(
        [
            sums[head] * inverse[:, head * patch_count : (head + 1) * patch_count]
            for head in range(head_count)
        ],
        axis=0,
    )
    out_ref[...] = jnp.swapaxes(out_t, 0, 1).astype(bf16)
    lse_ref[0] = row_max + jnp.log(row_total)


def pair_count(frame_total, first, steps):
    return steps * (frame_total * (2 * first + steps) // (2 * (first + steps)) + 1) // 2


def attend(queries, keys, values_t, frame_ids, head_count, patch_count, first, last, waits):
    lanes = queries.shape[1]
    key_rows = keys.shape[0]
    steps = last - first
    row_count = steps * patch_count
    width = head_count * patch_count
    work = pair_count(key_rows // patch_count, first, steps) * patch_count * width
    return pl.pallas_call(
        partial(
            attend_kernel, head_count=head_count, patch_count=patch_count, first=first
        ),
        grid_spec=pltpu.PrefetchScalarGridSpec(
            num_scalar_prefetch=1,
            grid=(steps,),
            in_specs=[
                pl.BlockSpec((patch_count, lanes), lambda j, ids: (j + first, 0)),
                pl.BlockSpec((key_rows, lanes), lambda j, ids: (0, 0)),
                pl.BlockSpec((lanes, key_rows), lambda j, ids: (0, 0)),
            ]
            + [pl.BlockSpec(memory_space=pl.ANY) for _ in waits],
            out_specs=[
                pl.BlockSpec((patch_count, lanes), lambda j, ids: (j, 0)),
                pl.BlockSpec((1, 1, width), lambda j, ids: (j, 0, 0)),
            ],
        ),
        out_shape=[
            jax.ShapeDtypeStruct((row_count, lanes), bf16),
            jax.ShapeDtypeStruct((steps, 1, width), f32),
        ],
        compiler_params=pltpu.CompilerParams(vmem_limit_bytes=40 << 20),
        cost_estimate=pl.CostEstimate(
            flops=work * 1024, bytes_accessed=8 * row_count * lanes, transcendentals=work
        ),
        name="attend",
    )(frame_ids, queries, keys, values_t, *waits)


def attend_back_kernel(
    frame_ids,
    q_ref,
    grad_ref,
    out_ref,
    lse_ref,
    k_ref,
    v_ref,
    kt_ref,
    *refs,
    head_count,
    patch_count,
    first,
    has_start,
):
    dq_ref, dk_ref, dv_ref, dk_sum, dv_sum = refs[-5:]
    position = pl.program_id(0)
    key_stop = frame_ids[position + first] + 1

    @pl.when(position == 0)
    def _():
        dk_sum[...] = refs[0][...] if has_start else jnp.zeros_like(dk_sum)
        dv_sum[...] = refs[1][...] if has_start else jnp.zeros_like(dv_sum)

    q_rows = q_ref[...].astype(f32) * score_scale
    grad_rows = grad_ref[...].astype(f32)
    grad_t = jnp.swapaxes(grad_rows, 0, 1)
    grad_out_t = grad_t * jnp.swapaxes(out_ref[...].astype(f32), 0, 1)
    delta = jnp.concatenate(
        [
            jnp.sum(grad_out_t[head * HD : (head + 1) * HD], axis=0, keepdims=True)
            for head in range(head_count)
        ],
        axis=1,
    )
    q_cols = head_blocks(jnp.swapaxes(q_rows, 0, 1), head_count)
    grad_cols = head_blocks(grad_t, head_count)
    q_stack = head_rows(q_rows, head_count)
    grad_stack = head_rows(grad_rows, head_count)
    lse = lse_ref[0]

    def step(first, frames, sums):
        start = pl.multiple_of(first * patch_count, patch_count)
        here = pl.ds(start, frames * patch_count)
        scores = dot(k_ref[here, :], q_cols)
        grad_probs = dot(v_ref[here, :], grad_cols)
        probs = jnp.exp(scores - lse)
        grad_scores = (probs * (grad_probs - delta)).astype(bf16)
        dv_sum[here, :] += dot(probs.astype(bf16), grad_stack)
        dk_sum[here, :] += dot(grad_scores, q_stack)
        keys_t = kt_ref[:, here]
        return tuple(
            sums[head]
            + dot(
                keys_t[head * HD : (head + 1) * HD],
                grad_scores[:, head * patch_count : (head + 1) * patch_count],
            )
            for head in range(head_count)
        )

    sums = over_key_frames(
        key_stop, step, tuple(jnp.zeros((HD, patch_count), f32) for _ in range(head_count))
    )
    dq_t = jnp.concatenate(sums, axis=0) * score_scale
    dq_ref[...] = jnp.swapaxes(dq_t, 0, 1).astype(bf16)

    @pl.when(position == pl.num_programs(0) - 1)
    def _():
        dk_ref[...] = dk_sum[...].astype(dk_ref.dtype)
        dv_ref[...] = dv_sum[...].astype(dv_ref.dtype)


def attend_back(
    queries, keys, values, keys_t, out, lse, grad, frame_ids, head_count, patch_count, first, last, start, sum_type, waits
):
    lanes = queries.shape[1]
    key_rows = keys.shape[0]
    steps = last - first
    row_count = steps * patch_count
    width = head_count * patch_count
    work = pair_count(key_rows // patch_count, first, steps) * patch_count * width
    block = pl.BlockSpec((patch_count, lanes), lambda j, ids: (j + first, 0))
    whole = pl.BlockSpec((key_rows, lanes), lambda j, ids: (0, 0))
    return pl.pallas_call(
        partial(
            attend_back_kernel,
            head_count=head_count,
            patch_count=patch_count,
            first=first,
            has_start=len(start) > 0,
        ),
        grid_spec=pltpu.PrefetchScalarGridSpec(
            num_scalar_prefetch=1,
            grid=(steps,),
            in_specs=[
                block,
                block,
                block,
                pl.BlockSpec((1, 1, width), lambda j, ids: (j + first, 0, 0)),
                whole,
                whole,
                pl.BlockSpec((lanes, key_rows), lambda j, ids: (0, 0)),
            ]
            + [whole for _ in start]
            + [pl.BlockSpec(memory_space=pl.ANY) for _ in waits],
            out_specs=[
                pl.BlockSpec((patch_count, lanes), lambda j, ids: (j, 0)),
                whole,
                whole,
            ],
            scratch_shapes=[
                pltpu.VMEM((key_rows, lanes), f32),
                pltpu.VMEM((key_rows, lanes), f32),
            ],
        ),
        out_shape=[
            jax.ShapeDtypeStruct((row_count, lanes), bf16),
            jax.ShapeDtypeStruct((key_rows, lanes), sum_type),
            jax.ShapeDtypeStruct((key_rows, lanes), sum_type),
        ],
        compiler_params=pltpu.CompilerParams(vmem_limit_bytes=48 << 20),
        cost_estimate=pl.CostEstimate(
            flops=work * 2560, bytes_accessed=16 * row_count * lanes, transcendentals=work
        ),
        name="attend_back",
    )(frame_ids, queries, grad, out, lse, keys, values, keys_t, *start, *waits)


def unpack_kernel(tail_ref, *refs, half, out_rows):
    up_ref, down_ref, out_ref = refs[-3:]
    ups, downs, outs = [], [], []
    for part in range(tail_ref.shape[0]):
        for row in (0, 2 * half):
            ups.append(tail_ref[part, row : row + half].astype(f32))
            downs.append(tail_ref[part, row + half : row + 2 * half].astype(f32))
        outs.append(tail_ref[part, 4 * half : 4 * half + out_rows].astype(f32))
    up_ref[...] = jnp.swapaxes(jnp.concatenate(ups, axis=0), 0, 1)
    down_ref[...] = jnp.concatenate(downs, axis=0)
    out_ref[...] = jnp.concatenate(outs, axis=0)


def unpack(tail, half, out_rows, waits):
    frame_parts, rows, width = tail.shape
    parts = max(1, 128 // (2 * half))
    return pl.pallas_call(
        partial(unpack_kernel, half=half, out_rows=out_rows),
        grid=(frame_parts // parts,),
        in_specs=[pl.BlockSpec((parts, rows, width), lambda n: (n, 0, 0))]
        + [pl.BlockSpec(memory_space=pl.ANY) for _ in waits],
        out_specs=[
            pl.BlockSpec((width, parts * 2 * half), lambda n: (0, n)),
            pl.BlockSpec((parts * 2 * half, width), lambda n: (n, 0)),
            pl.BlockSpec((parts * out_rows, width), lambda n: (n, 0)),
        ],
        out_shape=[
            jax.ShapeDtypeStruct((width, frame_parts * 2 * half), f32),
            jax.ShapeDtypeStruct((frame_parts * 2 * half, width), f32),
            jax.ShapeDtypeStruct((frame_parts * out_rows, width), f32),
        ],
        compiler_params=pltpu.CompilerParams(vmem_limit_bytes=32 << 20),
        cost_estimate=pl.CostEstimate(
            flops=0, bytes_accessed=frame_parts * rows * width * 6, transcendentals=0
        ),
        name="unpack",
    )(tail, *waits)


def unpack_heads_kernel(slots_ref, *refs):
    out_ref = refs[-1]
    groups, slots = slots_ref.shape[:2]
    for kind in range(3):
        rows = slice(kind * HD, (kind + 1) * HD)
        pieces = []
        for slot in range(slots):
            total = slots_ref[0, slot, rows].astype(f32)
            for group in range(1, groups):
                total = total + slots_ref[group, slot, rows].astype(f32)
            pieces.append(total)
        out_ref[kind] = jnp.swapaxes(jnp.concatenate(pieces, axis=0), 0, 1)


def unpack_heads(slots, waits):
    groups, count, rows, width = slots.shape
    pair = 128 // HD
    return pl.pallas_call(
        unpack_heads_kernel,
        grid=(count // pair,),
        in_specs=[pl.BlockSpec((groups, pair, rows, width), lambda n: (0, n, 0, 0))]
        + [pl.BlockSpec(memory_space=pl.ANY) for _ in waits],
        out_specs=pl.BlockSpec((3, width, 128), lambda n: (0, 0, n)),
        out_shape=jax.ShapeDtypeStruct((3, width, count * HD), f32),
        compiler_params=pltpu.CompilerParams(vmem_limit_bytes=40 << 20),
        cost_estimate=pl.CostEstimate(
            flops=0, bytes_accessed=groups * count * rows * width * 4, transcendentals=0
        ),
        name="unpack_heads",
    )(slots, *waits)


ROWS = 128


def project_kernel(
    heads_ref, weight_ref, bias_ref, tokens_ref, mod_ref, attended_ref, branch_ref, hidden_ref
):
    attended = jnp.concatenate([heads_ref[n] for n in range(heads_ref.shape[0])], axis=1)
    attended_ref[...] = attended
    branch = dot(attended, weight_ref[...]) + bias_ref[...]
    branch_ref[...] = branch
    gate_one, shift_two, scale_two = mod_ref[0, 2:3], mod_ref[0, 3:4], mod_ref[0, 4:5]
    normed = layer_norm(tokens_ref[...].astype(f32) + gate_one * branch)[0]
    hidden_ref[...] = (normed * (1.0 + scale_two) + shift_two).astype(bf16)


def project(heads, weight, bias, tokens, modulation):
    frame_parts, rows, lanes = heads.shape
    width = weight.shape[0]
    unit_steps = rows // modulation.shape[0] // ROWS
    block = pl.BlockSpec((ROWS, width), lambda n: (n, 0))
    return pl.pallas_call(
        project_kernel,
        grid=(rows // ROWS,),
        in_specs=[
            pl.BlockSpec((frame_parts, ROWS, lanes), lambda n: (0, n, 0)),
            pl.BlockSpec((width, width), lambda n: (0, 0)),
            pl.BlockSpec((1, width), lambda n: (0, 0)),
            block,
            pl.BlockSpec((1, 6, width), lambda n: (n // unit_steps, 0, 0)),
        ],
        out_specs=[block, block, block],
        out_shape=[
            jax.ShapeDtypeStruct((rows, width), bf16),
            jax.ShapeDtypeStruct((rows, width), f32),
            jax.ShapeDtypeStruct((rows, width), bf16),
        ],
        compiler_params=pltpu.CompilerParams(vmem_limit_bytes=32 << 20),
        cost_estimate=pl.CostEstimate(
            flops=2 * rows * width * width, bytes_accessed=12 * rows * width, transcendentals=0
        ),
        name="project",
    )(heads, weight, bias, tokens, modulation)


def middle_kernel(
    tokens_ref,
    branch_ref,
    two_a_ref,
    two_b_ref,
    back_a_ref,
    back_b_ref,
    grad_ref,
    mod_ref,
    bias_ref,
    weight_ref,
    result_ref,
    middle_grad_ref,
    one_ref,
    heads_ref,
    sums_ref,
    *,
    unit_steps,
):
    gate_one, scale_two, gate_two = mod_ref[0, 2:3], mod_ref[0, 4:5], mod_ref[0, 5:6]
    branch_one = branch_ref[...]
    middle = tokens_ref[...].astype(f32) + gate_one * branch_one
    normed, inverse = layer_norm(middle)
    branch_two = two_a_ref[...] + two_b_ref[...] + bias_ref[...]
    grad = grad_ref[...].astype(f32)
    result_ref[...] = (middle + gate_two * branch_two).astype(bf16)
    back = back_a_ref[...] + back_b_ref[...]
    grad_middle = grad + norm_back(back * (1.0 + scale_two), normed, inverse)
    middle_grad_ref[...] = grad_middle
    grad_one = (gate_one * grad_middle).astype(bf16)
    one_ref[...] = grad_one
    heads = dot_nt(grad_one, weight_ref[...]).astype(bf16)
    lanes = heads_ref.shape[2]
    for part in range(heads_ref.shape[0]):
        heads_ref[part] = heads[:, part * lanes : (part + 1) * lanes]

    @pl.when(pl.program_id(0) % unit_steps == 0)
    def _():
        sums_ref[...] = jnp.zeros_like(sums_ref)

    for row, values in enumerate(
        (grad_middle * branch_one, back, back * normed, grad * branch_two, grad_one.astype(f32))
    ):
        sums_ref[0, row : row + 1] += jnp.sum(values, axis=0, keepdims=True)


def middle_back(
    tokens, branch_one, two_a, two_b, back_a, back_b, grad, modulation, bias, weight, frame_parts
):
    rows, width = tokens.shape
    units = modulation.shape[0]
    unit_steps = rows // units // ROWS
    lanes = width // frame_parts
    block = pl.BlockSpec((ROWS, width), lambda n: (n, 0))
    return pl.pallas_call(
        partial(middle_kernel, unit_steps=unit_steps),
        grid=(rows // ROWS,),
        in_specs=[block] * 7
        + [
            pl.BlockSpec((1, 6, width), lambda n: (n // unit_steps, 0, 0)),
            pl.BlockSpec((1, width), lambda n: (0, 0)),
            pl.BlockSpec((width, width), lambda n: (0, 0)),
        ],
        out_specs=[
            block,
            block,
            block,
            pl.BlockSpec((frame_parts, ROWS, lanes), lambda n: (0, n, 0)),
            pl.BlockSpec((1, 8, width), lambda n: (n // unit_steps, 0, 0)),
        ],
        out_shape=[
            jax.ShapeDtypeStruct((rows, width), bf16),
            jax.ShapeDtypeStruct((rows, width), f32),
            jax.ShapeDtypeStruct((rows, width), bf16),
            jax.ShapeDtypeStruct((frame_parts, rows, lanes), bf16),
            jax.ShapeDtypeStruct((units, 8, width), f32),
        ],
        compiler_params=pltpu.CompilerParams(vmem_limit_bytes=40 << 20),
        cost_estimate=pl.CostEstimate(
            flops=2 * rows * width * width, bytes_accessed=40 * rows * width, transcendentals=0
        ),
        name="middle_back",
    )(tokens, branch_one, two_a, two_b, back_a, back_b, grad, modulation, bias, weight)


def add_pairs_kernel(*refs):
    out_ref = refs[-1]
    row = 0
    for pair in range(len(refs) // 2):
        left, right = refs[2 * pair], refs[2 * pair + 1]
        size = left.shape[2]
        out_ref[:, :, row : row + size, :] = left[...] + right[...]
        row += size


def add_pairs(*pairs):
    chips, shards, _, width = pairs[0].shape
    rows = sum(values.shape[2] for values in pairs[::2])

    def spec(size):
        return pl.BlockSpec((1, shards, size, width), lambda n: (n, 0, 0, 0))

    return pl.pallas_call(
        add_pairs_kernel,
        grid=(chips,),
        in_specs=[spec(values.shape[2]) for values in pairs],
        out_specs=spec(rows),
        out_shape=jax.ShapeDtypeStruct((chips, shards, rows, width), bf16),
        compiler_params=pltpu.CompilerParams(vmem_limit_bytes=32 << 20),
        cost_estimate=pl.CostEstimate(
            flops=0, bytes_accessed=6 * chips * shards * rows * width, transcendentals=0
        ),
        name="add_pairs",
    )(*pairs)


def mlp_kernel(
    core_ref,
    hidden_ref,
    grad_ref,
    bias_ref,
    bias_other_ref,
    up_ref,
    up_other_ref,
    down_ref,
    down_other_ref,
    branch_ref,
    back_ref,
    keep_ref,
    send_ref,
    keep_bias_ref,
    send_bias_ref,
    hidden_t,
    grad_t,
):
    step = pl.program_id(0)
    rows, width = hidden_ref.shape

    @pl.when(step == 0)
    def _():
        branch_ref[...] = jnp.zeros_like(branch_ref)
        back_ref[...] = jnp.zeros_like(back_ref)
        for start in range(0, width, 256):
            cols = slice(start, start + 256)
            hidden_t[cols, :] = jnp.swapaxes(hidden_ref[:, cols].astype(f32), 0, 1).astype(bf16)
            grad_t[cols, :] = jnp.swapaxes(grad_ref[:, cols].astype(f32), 0, 1).astype(bf16)

    slope = math.sqrt(2.0 / math.pi)
    for up, down, bias, out_ref, out_bias_ref in (
        (up_other_ref, down_other_ref, bias_other_ref, send_ref, send_bias_ref),
        (up_ref, down_ref, bias_ref, keep_ref, keep_bias_ref),
    ):
        shards, part = up.shape[1], up.shape[2]
        units = shards * part
        up_rows = up[0].reshape(units, width)
        down_rows = down[0].reshape(units, width)
        pre = dot(up_rows, hidden_t[...]) + bias[0]
        square = pre * pre
        bend = jnp.tanh(slope * pre * (1.0 + 0.044715 * square))
        activated = (0.5 * pre * (1.0 + bend)).astype(bf16)
        gain = 0.5 * (1.0 + bend) + (0.5 * slope) * pre * (1.0 - bend * bend) * (
            1.0 + (3 * 0.044715) * square
        )
        grad_pre = (dot(down_rows, grad_t[...]) * gain).astype(bf16)
        out_bias_ref[0] = jnp.sum(grad_pre.astype(f32), axis=1, keepdims=True)
        out_ref[0, :, :part, :] = (
            dot(grad_pre, hidden_ref[...]).astype(bf16).reshape(shards, part, width)
        )
        out_ref[0, :, part:, :] = (
            dot(activated, grad_ref[...]).astype(bf16).reshape(shards, part, width)
        )
        branch_ref[...] += dot_tn(activated, down_rows)
        back_ref[...] += dot_tn(grad_pre, up_rows)


def mlp(core, hidden, grad, bias, weights, part):
    frame_parts, shards, _, width = weights.shape
    rows = hidden.shape[0]
    steps = frame_parts // 2
    units = shards * part

    def own(m, c):
        return 2 * m + c[0]

    def other(m, c):
        return 2 * m + 1 - c[0]

    def weight_spec(which, row):
        return pl.BlockSpec((1, shards, part, width), lambda m, c: (which(m, c), 0, row, 0))

    whole = pl.BlockSpec((rows, width), lambda m, c: (0, 0), pipeline_mode=pl.Buffered(1))
    sums = pl.BlockSpec((rows, width), lambda m, c: (0, 0))
    out = pl.BlockSpec((1, shards, 2 * part, width), lambda m, c: (m, 0, 0, 0))
    column = pl.BlockSpec((1, units, 1), lambda m, c: (m, 0, 0))
    work = rows * width * units * frame_parts
    return pl.pallas_call(
        mlp_kernel,
        grid_spec=pltpu.PrefetchScalarGridSpec(
            num_scalar_prefetch=1,
            grid=(steps,),
            in_specs=[
                whole,
                whole,
                pl.BlockSpec((1, units, 1), lambda m, c: (own(m, c), 0, 0)),
                pl.BlockSpec((1, units, 1), lambda m, c: (other(m, c), 0, 0)),
                weight_spec(own, 0),
                weight_spec(other, 0),
                weight_spec(own, 1),
                weight_spec(other, 1),
            ],
            out_specs=[sums, sums, out, out, column, column],
            scratch_shapes=[pltpu.VMEM((width, rows), bf16), pltpu.VMEM((width, rows), bf16)],
        ),
        out_shape=[
            jax.ShapeDtypeStruct((rows, width), f32),
            jax.ShapeDtypeStruct((rows, width), f32),
            jax.ShapeDtypeStruct((steps, shards, 2 * part, width), bf16),
            jax.ShapeDtypeStruct((steps, shards, 2 * part, width), bf16),
            jax.ShapeDtypeStruct((steps, units, 1), f32),
            jax.ShapeDtypeStruct((steps, units, 1), f32),
        ],
        compiler_params=pltpu.CompilerParams(vmem_limit_bytes=48 << 20),
        cost_estimate=pl.CostEstimate(
            flops=12 * work,
            bytes_accessed=frame_parts * units * width * 8,
            transcendentals=rows * units * frame_parts,
        ),
        name="mlp",
    )(core, hidden, grad, bias, bias, weights, weights, weights, weights)


def after(value, *others):
    return lax.optimization_barrier((value,) + others)[0]


def on_device(
    tokens,
    noise_steps,
    ada_weight,
    ada_bias,
    qkv_weight,
    qv_bias,
    out_weight,
    out_bias,
    up_weight,
    up_bias,
    down_weight,
    down_bias,
    cotangent,
):
    clip_count, local_frames, local_patches, model_width = tokens.shape
    tensor_count = lax.axis_size("tensor")
    frame_devices = lax.axis_size("frame")
    frame_at = lax.axis_index("frame")
    tensor_at = lax.axis_index("tensor")
    patch_count = local_patches * tensor_count
    hidden_width = up_weight.shape[1] * tensor_count
    head_total = model_width // HD
    shard_heads = head_total // tensor_count
    head_count = head_total // frame_devices
    lanes = head_count * HD
    unit_total = clip_count * local_frames
    units = unit_total // tensor_count
    sharers = tensor_count // clip_count
    share_at = tensor_at % sharers
    own_rows = units * patch_count
    all_rows = frame_devices * own_rows
    slot = frame_at % shard_heads
    group_at = frame_at // shard_heads
    shard_groups = tensor_count // head_count
    shard_base = (tensor_at // sharers) * sharers
    core = frame_at % 2
    chips = frame_devices // 2
    unit_shape = (units, patch_count, model_width)
    column_part = model_width // tensor_count


    def swap_frame(values):
        return lax.all_to_all(values, "frame", split_axis=0, concat_axis=0, tiled=True)

    def shifted(values, shift):
        return lax.ppermute(
            values, "tensor", [(t, (t + shift) % tensor_count) for t in range(tensor_count)]
        )

    def tensor_parts(values):
        return [shifted(values, tensor_count - 1 - n) for n in range(tensor_count - 1)] + [values]

    def tensor_sum(parts):
        total = parts[-1].astype(f32)
        for n in range(tensor_count - 1):
            total = total + shifted(parts[n], n + 1).astype(f32)
        return total

    def exchange(parts):
        last = tensor_count - 1
        return [shifted(parts[last - 1 - n], last - n) for n in range(last)] + [parts[last]]

    def to_relative(values):
        return [
            lax.dynamic_index_in_dim(
                values, (tensor_at + 1 + n) % tensor_count, 0, keepdims=False
            )
            for n in range(tensor_count)
        ]

    def rolled(values, start):
        return lax.dynamic_slice_in_dim(
            jnp.concatenate([values, values]), start % tensor_count, tensor_count, axis=0
        )

    def from_relative(parts, first=0):
        return rolled(jnp.stack(parts), first - tensor_at - 1)

    def head_pairs(head, member):
        pairs = []
        for i in range(frame_devices):
            for t in range(member, tensor_count, sharers):
                shard = (t - member + i // shard_heads + head * shard_groups) % tensor_count
                pairs.append((i * tensor_count + shard, i * tensor_count + t))
        return pairs

    def from_owners(values, head):
        total = None
        for member in range(sharers):
            got = lax.ppermute(values, ("frame", "tensor"), head_pairs(head, member))
            total = got if total is None else total + got
        return total

    def to_owners(pieces):
        total = 0.0
        for head, piece in enumerate(pieces):
            for member in range(sharers):
                pairs = [(user, owner) for owner, user in head_pairs(head, member)]
                total = total + lax.ppermute(piece, ("frame", "tensor"), pairs).astype(f32)
        return total.astype(bf16)

    def to_units(values):
        parts = to_relative(
            values.reshape(tensor_count, units, local_patches, model_width)
        )
        return jnp.stack(exchange(parts), axis=1).reshape(units, patch_count, model_width)

    def from_units(values):
        parts = values.reshape(units, tensor_count, local_patches, model_width)
        return from_relative(exchange([parts[:, n] for n in range(tensor_count)])).reshape(
            clip_count, local_frames, local_patches, model_width
        )

    def core_swap(values):
        return lax.ppermute(values, "frame", [(i, i ^ 1) for i in range(frame_devices)])

    def scatter(values):
        return lax.psum_scatter(
            values.reshape(-1, model_width),
            "frame",
            scatter_dimension=0,
            axis_index_groups=[list(range(c, frame_devices, 2)) for c in range(2)],
            tiled=True,
        ).reshape(values.shape[1:])

    def frame_parts(values):
        return (
            lax.all_gather(values, "frame", axis=0, tiled=True)
            .reshape(frame_devices, -1, model_width)
        )

    unit_tokens = to_units(tokens)
    act_noise = noise_activation(noise_steps, model_width).reshape(unit_total, model_width)
    mod_local = jnp.einsum(
        "ud,dkj->ukj", act_noise, ada_weight, preferred_element_type=f32
    ) + ada_bias.astype(f32)
    modulation = (
        from_relative(
            exchange(to_relative(mod_local.reshape(tensor_count, units * 6, column_part)))
        )
        .reshape(tensor_count, units, 6, column_part)
        .transpose(1, 2, 0, 3)
        .reshape(units, 6, model_width)
    )
    shift_one = modulation[:, None, 0]
    scale_one = modulation[:, None, 1]
    gate_one = modulation[:, None, 2]
    shift_two = modulation[:, None, 3]
    scale_two = modulation[:, None, 4]
    gate_two = modulation[:, None, 5]

    slot_weight = lax.dynamic_slice_in_dim(qkv_weight, slot * HD, HD, axis=2)
    slot_weight = slot_weight.transpose(1, 2, 0).reshape(3 * HD, model_width)
    slot_bias = lax.dynamic_slice_in_dim(qv_bias, slot * HD, HD, axis=1).reshape(1, 2 * HD)
    slot_bias = jnp.pad(slot_bias, ((0, 15), (0, model_width - 2 * HD)))
    slot_pack = jnp.concatenate([slot_weight, slot_bias])

    def own_part(values):
        size = values.shape[0] // frame_devices
        return lax.dynamic_slice_in_dim(values, frame_at * size, size, axis=0)

    hidden_part = hidden_width // (tensor_count * frame_devices)
    half = hidden_part // 2
    out_rows = out_weight.shape[0] // frame_devices
    up_part = lax.dynamic_slice_in_dim(
        up_weight, frame_at * hidden_part, hidden_part, axis=1
    ).transpose(1, 0)
    down_part = own_part(down_weight)
    bias_part = lax.dynamic_slice_in_dim(up_bias, frame_at * hidden_part, hidden_part, axis=0)
    bias_part = jnp.pad(bias_part[None, :], ((0, 15), (0, model_width - hidden_part)))
    first_pack = jnp.concatenate([up_part[:half], down_part[:half], bias_part])
    second_pack = jnp.concatenate([up_part[half:], down_part[half:]])
    out_pack = own_part(out_weight)
    slot_pack = after(slot_pack, unit_tokens)
    head_pack = jnp.stack([from_owners(slot_pack, head) for head in range(head_count)])
    first_list = tensor_parts(after(jnp.concatenate([first_pack, out_pack]), head_pack))
    out_at = first_pack.shape[0]
    first_parts = jnp.concatenate(
        [
            from_relative([part[:out_at] for part in first_list]),
            from_relative([part[out_at:] for part in first_list], shard_base),
        ],
        axis=1,
    ).reshape(-1, model_width)
    head_weight = (
        head_pack[:, : 3 * HD]
        .reshape(head_count, 3, HD, model_width)
        .transpose(1, 0, 2, 3)
        .reshape(3 * lanes, model_width)
    )
    head_bias = head_pack[:, 3 * HD, : 2 * HD]
    head_bias = head_bias.reshape(head_count, 2, HD).transpose(1, 0, 2).reshape(2, lanes)
    head_bias = head_bias.astype(f32)
    qkv_bias = jnp.concatenate([head_bias[0], jnp.zeros((lanes,), f32), head_bias[1]])

    token_values = unit_tokens.astype(f32)
    normed_one, inverse_one = layer_norm(token_values)
    hidden_one = (normed_one * (1.0 + scale_one) + shift_one).astype(bf16)
    hidden_all = lax.all_gather(
        hidden_one.reshape(own_rows, model_width), "frame", axis=0, tiled=True
    )

    first_all = lax.all_gather(first_parts, "frame", axis=0, tiled=True)
    first_all = first_all.reshape(frame_devices, tensor_count, -1, model_width)
    up_bias_all = first_all[:, :, 2 * half, :hidden_part].astype(f32)
    first_bias = up_bias_all[:, :, :half].reshape(frame_devices, tensor_count * half, 1)
    second_bias = up_bias_all[:, :, half:].reshape(frame_devices, tensor_count * half, 1)
    head_parts = HD // out_rows
    out_full = (
        first_all[:, :, 2 * half + 16 :]
        .reshape(shard_heads, head_parts, head_count, shard_groups, out_rows, model_width)
        .transpose(3, 0, 2, 1, 4, 5)
        .reshape(model_width, model_width)
    )

    projected = (dot_nt(hidden_all, head_weight) + qkv_bias).astype(bf16)
    queries = projected[:, :lanes]
    keys = projected[:, lanes : 2 * lanes]
    values = projected[:, 2 * lanes :]

    def share(mine):
        if sharers == 1:
            return mine
        pieces = [mine]
        for shift in range(1, sharers):
            perm = [
                (t, (t // sharers) * sharers + (t + shift) % sharers) for t in range(tensor_count)
            ]
            pieces.append(lax.ppermute(mine, "tensor", perm))
        stacked = jnp.stack(pieces)
        stacked = jnp.stack(
            [
                lax.dynamic_index_in_dim(
                    stacked, (share_at - member) % sharers, 0, keepdims=False
                )
                for member in range(sharers)
            ]
        )
        return (
            stacked.reshape(sharers, frame_devices, own_rows, lanes)
            .transpose(1, 0, 2, 3)
            .reshape(sharers * all_rows, lanes)
        )

    def unshare(partial_sums):
        if sharers == 1:
            return partial_sums
        pieces = (
            partial_sums.reshape(frame_devices, sharers, own_rows, lanes)
            .transpose(1, 0, 2, 3)
            .reshape(sharers, all_rows, lanes)
        )
        total = lax.dynamic_index_in_dim(pieces, share_at, 0, keepdims=False).astype(f32)
        for shift in range(1, sharers):
            perm = [
                (t, (t // sharers) * sharers + (t + shift) % sharers) for t in range(tensor_count)
            ]
            piece = lax.dynamic_index_in_dim(
                pieces, (share_at + shift) % sharers, 0, keepdims=False
            )
            total = total + lax.ppermute(piece, "tensor", perm).astype(f32)
        return total.astype(bf16)

    keys_all = share(keys)
    values_all = share(values)
    unit_ids = jnp.arange(frame_devices * units, dtype=jnp.int32)
    frame_ids = (
        (unit_ids // units) * local_frames + share_at.astype(jnp.int32) * units + unit_ids % units
    )
    values_t = values_all.T
    steps = all_rows // patch_count
    second_list = tensor_parts(after(second_pack, queries))
    cut = steps * 11 // 16
    heads_a, lse_a = attend(
        queries, keys_all, values_t, frame_ids, head_count, patch_count, 0, cut, ()
    )
    heads_a, *second_list = lax.optimization_barrier((heads_a, *second_list))
    second_parts = from_relative(second_list)
    upstream = to_units(after(cotangent, second_parts))
    heads_b, lse_b = attend(
        queries, keys_all, values_t, frame_ids, head_count, patch_count, cut, steps,
        (second_parts,),
    )
    attended_heads = jnp.concatenate([heads_a, heads_b])
    row_lse = jnp.concatenate([lse_a, lse_b])
    second_all = lax.all_gather(
        second_parts.reshape(-1, model_width), "frame", axis=0, tiled=True
    ).reshape(frame_devices, tensor_count, -1, model_width)
    heads_here = swap_frame(attended_heads.reshape(frame_devices, own_rows, lanes))

    grad_two = (gate_two * upstream.astype(f32)).astype(bf16).reshape(own_rows, model_width)
    grad_down_bias = jnp.sum(grad_two.astype(f32), axis=0)

    flat_tokens = unit_tokens.reshape(own_rows, model_width)
    attended, branch_one, hidden_two = project(
        heads_here, out_full, out_bias.astype(f32)[None, :], flat_tokens, modulation
    )

    core_id = core.astype(jnp.int32).reshape(1)
    branch_a, back_a, keep_a, send_a, keep_bias_a, send_bias_a = mlp(
        core_id, hidden_two, grad_two, first_bias, first_all, half
    )
    got_a = core_swap(send_a)
    branch_b, back_b, keep_b, send_b, keep_bias_b, send_bias_b = mlp(
        core_id, hidden_two, grad_two, second_bias, second_all, half
    )
    got_b = core_swap(send_b)
    got_a, branch_b = lax.optimization_barrier((got_a, branch_b))
    back_b, first_half = lax.optimization_barrier((back_b, add_pairs(keep_a, got_a)))
    first_sum = scatter(first_half)
    result, grad_middle, grad_one, head_grads, unit_sums = middle_back(
        flat_tokens, branch_one, branch_a, branch_b, back_a, back_b,
        upstream.reshape(own_rows, model_width), modulation, down_bias.astype(f32)[None, :],
        out_full, frame_devices,
    )
    grad_heads = swap_frame(head_grads).reshape(all_rows, lanes)
    result = from_units(result.reshape(unit_shape))
    grad_middle = grad_middle.reshape(unit_shape)
    grad_gate_one, grad_shift_two, grad_scale_two, grad_gate_two = (
        unit_sums[:, n] for n in range(4)
    )
    grad_out_bias = jnp.sum(unit_sums[:, 4], axis=0)

    grad_out = (
        dot_tn(attended, grad_one)
        .astype(bf16)
        .reshape(shard_groups, shard_heads, head_count, head_parts, out_rows, model_width)
        .transpose(2, 0, 1, 3, 4, 5)
        .reshape(tensor_count, frame_devices, out_rows, model_width)
    )
    grad_out = rolled(grad_out, -shard_base).transpose(1, 0, 2, 3)
    width_part = model_width // frame_devices

    def by_core(keep_part, send_part):
        pair = jnp.stack([keep_part, send_part], axis=1)
        return jnp.where(core == 0, pair, pair[:, ::-1]).reshape(
            (frame_devices,) + keep_part.shape[1:]
        )

    grad_up_bias = jnp.concatenate(
        [
            by_core(keep_bias_a, send_bias_a).reshape(frame_devices, tensor_count, half),
            by_core(keep_bias_b, send_bias_b).reshape(frame_devices, tensor_count, half),
        ],
        axis=2,
    )
    once = jnp.concatenate(
        [
            grad_down_bias.reshape(frame_devices, 1, width_part),
            grad_out_bias.reshape(frame_devices, 1, width_part),
        ],
        axis=2,
    )
    bias_row = jnp.concatenate(
        [jnp.broadcast_to(once, (frame_devices, tensor_count, 2 * width_part)), grad_up_bias],
        axis=2,
    ).astype(bf16)
    bias_row = jnp.pad(
        bias_row[:, :, None, :], ((0, 0), (0, 0), (0, 15), (0, model_width - bias_row.shape[2]))
    )
    out_pairs = jnp.concatenate([grad_out, bias_row], axis=2).reshape(
        chips, 2, tensor_count, out_rows + 16, model_width
    )
    late_half = add_pairs(
        keep_b,
        got_b,
        lax.dynamic_index_in_dim(out_pairs, core, 1, keepdims=False),
        core_swap(lax.dynamic_index_in_dim(out_pairs, 1 - core, 1, keepdims=False)),
    )
    late_sum = scatter(late_half)
    first_list = exchange(to_relative(first_sum))

    keys_t = keys_all.T
    grad_q_a, *sums = attend_back(
        queries, keys_all, values_all, keys_t, attended_heads, row_lse, grad_heads,
        frame_ids, head_count, patch_count, 0, cut, (), f32, (late_half, result),
    )
    *sums, first_list = lax.optimization_barrier((*sums, first_list))
    first_total = sum(part.astype(f32) for part in first_list).astype(bf16)
    grad_q_b, grad_k_all, grad_v_all = attend_back(
        queries, keys_all, values_all, keys_t, attended_heads, row_lse, grad_heads,
        frame_ids, head_count, patch_count, cut, steps, tuple(sums), bf16, (first_total,),
    )
    grad_q = jnp.concatenate([grad_q_a, grad_q_b])
    grad_k = unshare(grad_k_all)
    grad_v = unshare(grad_v_all)
    grad_projected = jnp.concatenate([grad_q, grad_k, grad_v], axis=1)
    grad_hidden_part = dot(grad_projected, head_weight).astype(bf16)
    grad_hidden_one = lax.psum_scatter(grad_hidden_part, "frame", scatter_dimension=0, tiled=True)
    grad_hidden_one = grad_hidden_one.astype(f32).reshape(unit_shape)

    late_total = tensor_sum(to_relative(late_sum)).astype(bf16)
    grad_head_weight = dot_tn(after(grad_projected, grad_hidden_part), hidden_all).astype(bf16)
    grad_slots = (
        grad_head_weight.reshape(3, head_count, HD, model_width)
        .transpose(1, 0, 2, 3)
        .reshape(head_count, 3 * HD, model_width)
    )
    grad_head_bias = jnp.stack(
        [jnp.sum(grad_q.astype(f32), axis=0), jnp.sum(grad_v.astype(f32), axis=0)]
    ).astype(bf16)
    grad_head_bias = grad_head_bias.reshape(2, head_count, HD).transpose(1, 0, 2)
    grad_head_bias = jnp.pad(
        grad_head_bias.reshape(head_count, 1, 2 * HD),
        ((0, 0), (0, 15), (0, model_width - 2 * HD)),
    )
    grad_slots = jnp.concatenate([grad_slots, grad_head_bias], axis=1)

    slots_total = to_owners([grad_slots[head] for head in range(head_count)])

    grad_scale_one = jnp.sum(grad_hidden_one * normed_one, axis=1)
    grad_shift_one = jnp.sum(grad_hidden_one, axis=1)
    grad_tokens = (
        grad_middle
        + norm_back(grad_hidden_one * (1.0 + scale_one), normed_one, inverse_one)
    ).astype(bf16)
    tail_sums, slots_total, grad_tokens = lax.optimization_barrier(
        (jnp.concatenate([first_total, late_total]), slots_total, grad_tokens)
    )
    tail_all = frame_parts(tail_sums)
    slots_all = frame_parts(slots_total).reshape(
        shard_groups, shard_heads, -1, model_width
    )
    grad_tokens = from_units(grad_tokens)
    grad_modulation = jnp.stack(
        [
            grad_shift_one,
            grad_scale_one,
            grad_gate_one,
            grad_shift_two,
            grad_scale_two,
            grad_gate_two,
        ],
        axis=1,
    )
    unit_steps = lax.dynamic_slice_in_dim(
        noise_steps.reshape(unit_total), tensor_at * units, units
    ).astype(f32)
    grad_mod_parts = exchange(
        to_relative(
            jnp.concatenate(
                [
                    grad_modulation.reshape(units, 6, tensor_count, column_part)
                    .transpose(2, 0, 1, 3)
                    .reshape(tensor_count, units, 6 * column_part),
                    jnp.broadcast_to(unit_steps[None, :, None], (tensor_count, units, 128)),
                ],
                axis=2,
            )
        )
    )
    grad_mod_all = lax.all_gather(
        jnp.stack(grad_mod_parts).reshape(unit_total, -1), "frame", axis=0, tiled=True
    )
    act_all = noise_activation(grad_mod_all[:, -1], model_width)
    grad_mod_all = grad_mod_all[:, :-128].reshape(-1, 6, column_part)
    grad_ada_weight = jnp.einsum(
        "ud,ukj->dkj", act_all.astype(f32), grad_mod_all, precision=lax.Precision.HIGH
    )
    grad_ada_bias = jnp.sum(grad_mod_all, axis=0)
    final_up, final_down, final_out = unpack(tail_all, half, out_rows, (grad_tokens,))
    tail_bias = tail_all[:, 4 * half + out_rows].astype(f32)
    final_down_bias = tail_bias[:, :width_part].reshape(model_width)
    final_out_bias = tail_bias[:, width_part : 2 * width_part].reshape(model_width)
    final_up_bias = tail_bias[:, 2 * width_part : 2 * width_part + hidden_part].reshape(
        up_bias.shape
    )
    final_qkv = unpack_heads(slots_all, (grad_ada_bias, final_up)).transpose(1, 0, 2)
    final_qv_bias = (
        jnp.sum(slots_all[:, :, 3 * HD, : 2 * HD].astype(f32), axis=0)
        .reshape(shard_heads, 2, HD)
        .transpose(1, 0, 2)
        .reshape(qv_bias.shape)
    )
    return (
        result,
        grad_tokens.astype(f32),
        grad_ada_weight,
        grad_ada_bias,
        final_qkv,
        final_qv_bias,
        final_out,
        final_out_bias,
        final_up,
        final_up_bias,
        final_down,
        final_down_bias,
    )


def solution(mesh):
    in_specs = (
        P(None, "frame", "tensor", None),
        P(None, "frame"),
        P(None, None, "tensor"),
        P(None, "tensor"),
        P(None, None, "tensor"),
        P(None, "tensor"),
        P("tensor", None),
        P(),
        P(None, "tensor"),
        P("tensor"),
        P("tensor", None),
        P(),
        P(None, "frame", "tensor", None),
    )
    out_specs = (
        P(None, "frame", "tensor", None),
        P(None, "frame", "tensor", None),
        P(None, None, "tensor"),
        P(None, "tensor"),
        P(None, None, "tensor"),
        P(None, "tensor"),
        P("tensor", None),
        P(),
        P(None, "tensor"),
        P("tensor"),
        P("tensor", None),
        P(),
    )
    return jax.shard_map(
        on_device, mesh=mesh, in_specs=in_specs, out_specs=out_specs, check_vma=False
    )
```

```python
from functools import partial
import math

import jax
import jax.numpy as jnp
from jax import lax
from jax.experimental import pallas as pl
from jax.experimental.pallas import tpu as pltpu
from jax.sharding import PartitionSpec as P

HD = 64
f32 = jnp.float32
bf16 = jnp.bfloat16
score_scale = HD ** (-0.5)


def noise_embedding(noise_steps, model_width):
    half_width = model_width // 2
    frequency = jnp.exp(-math.log(10000.0) * jnp.arange(half_width, dtype=f32) / half_width)
    angles = noise_steps.astype(f32)[..., None] * frequency
    return jnp.concatenate([jnp.cos(angles), jnp.sin(angles)], axis=-1)


def noise_activation(noise_steps, model_width):
    return jax.nn.silu(noise_embedding(noise_steps, model_width)).astype(bf16)


def layer_norm(values):
    centred = values - jnp.mean(values, axis=-1, keepdims=True)
    inverse = lax.rsqrt(jnp.mean(centred * centred, axis=-1, keepdims=True) + 1e-06)
    return (centred * inverse, inverse)


def norm_back(grad_normed, normed, inverse):
    return inverse * (
        grad_normed
        - jnp.mean(grad_normed, axis=-1, keepdims=True)
        - normed * jnp.mean(grad_normed * normed, axis=-1, keepdims=True)
    )


def dot(left, right):
    return lax.dot_general(left, right, (((1,), (0,)), ((), ())), preferred_element_type=f32)


def dot_nt(left, right):
    return lax.dot_general(left, right, (((1,), (1,)), ((), ())), preferred_element_type=f32)


def dot_tn(left, right):
    return lax.dot_general(left, right, (((0,), (0,)), ((), ())), preferred_element_type=f32)


GROUP = 4


def head_blocks(transposed, head_count):
    rows = lax.broadcasted_iota(jnp.int32, transposed.shape, 0) // HD
    return jnp.concatenate(
        [jnp.where(rows == head, transposed, 0.0) for head in range(head_count)], axis=1
    ).astype(bf16)


def head_rows(natural, head_count):
    lanes = lax.broadcasted_iota(jnp.int32, natural.shape, 1) // HD
    return jnp.concatenate(
        [jnp.where(lanes == head, natural, 0.0) for head in range(head_count)], axis=0
    ).astype(bf16)


def over_key_frames(key_stop, step, carry):
    done = 0
    size = 1
    while size < GROUP:
        once = (key_stop // size) % 2
        carry = lax.fori_loop(
            0, once, lambda _, c, first=done, size=size: step(first, size, c), carry
        )
        done = done + once * size
        size *= 2
    return lax.fori_loop(
        0, key_stop // GROUP, lambda n, c: step(done + GROUP * n, GROUP, c), carry
    )


def attend_kernel(frame_ids, q_ref, k_ref, vt_ref, *refs, head_count, patch_count, first):
    out_ref, lse_ref = refs[-2:]
    key_stop = frame_ids[pl.program_id(0) + first] + 1
    q_cols = head_blocks(jnp.swapaxes(q_ref[...].astype(f32), 0, 1) * score_scale, head_count)
    width = head_count * patch_count

    def step(first, frames, carry):
        row_max, row_total, sums = carry
        start = pl.multiple_of(first * patch_count, patch_count)
        scores = dot(k_ref[pl.ds(start, frames * patch_count), :], q_cols)
        new_max = jnp.maximum(row_max, jnp.max(scores, axis=0, keepdims=True))
        rescale = jnp.exp(row_max - new_max)
        weights = jnp.exp(scores - new_max)
        row_total = row_total * rescale + jnp.sum(weights, axis=0, keepdims=True)
        weights = weights.astype(bf16)
        values_t = vt_ref[:, pl.ds(start, frames * patch_count)]
        parts = []
        for head in range(head_count):
            cols = slice(head * patch_count, (head + 1) * patch_count)
            rows = slice(head * HD, (head + 1) * HD)
            parts.append(sums[head] * rescale[:, cols] + dot(values_t[rows], weights[:, cols]))
        return (new_max, row_total, tuple(parts))

    row_max, row_total, sums = over_key_frames(
        key_stop,
        step,
        (
            jnp.full((1, width), -1e30, f32),
            jnp.zeros((1, width), f32),
            tuple(jnp.zeros((HD, patch_count), f32) for _ in range(head_count)),
        ),
    )
    inverse = 1.0 / row_total
    out_t = jnp.concatenate(
        [
            sums[head] * inverse[:, head * patch_count : (head + 1) * patch_count]
            for head in range(head_count)
        ],
        axis=0,
    )
    out_ref[...] = jnp.swapaxes(out_t, 0, 1).astype(bf16)
    lse_ref[0] = row_max + jnp.log(row_total)


def pair_count(frame_total, first, steps):
    return steps * (frame_total * (2 * first + steps) // (2 * (first + steps)) + 1) // 2


def attend(queries, keys, values_t, frame_ids, head_count, patch_count, first, last, waits):
    lanes = queries.shape[1]
    key_rows = keys.shape[0]
    steps = last - first
    row_count = steps * patch_count
    width = head_count * patch_count
    work = pair_count(key_rows // patch_count, first, steps) * patch_count * width
    return pl.pallas_call(
        partial(
            attend_kernel, head_count=head_count, patch_count=patch_count, first=first
        ),
        grid_spec=pltpu.PrefetchScalarGridSpec(
            num_scalar_prefetch=1,
            grid=(steps,),
            in_specs=[
                pl.BlockSpec((patch_count, lanes), lambda j, ids: (j + first, 0)),
                pl.BlockSpec((key_rows, lanes), lambda j, ids: (0, 0)),
                pl.BlockSpec((lanes, key_rows), lambda j, ids: (0, 0)),
            ]
            + [pl.BlockSpec(memory_space=pl.ANY) for _ in waits],
            out_specs=[
                pl.BlockSpec((patch_count, lanes), lambda j, ids: (j, 0)),
                pl.BlockSpec((1, 1, width), lambda j, ids: (j, 0, 0)),
            ],
        ),
        out_shape=[
            jax.ShapeDtypeStruct((row_count, lanes), bf16),
            jax.ShapeDtypeStruct((steps, 1, width), f32),
        ],
        compiler_params=pltpu.CompilerParams(vmem_limit_bytes=40 << 20),
        cost_estimate=pl.CostEstimate(
            flops=work * 1024, bytes_accessed=8 * row_count * lanes, transcendentals=work
        ),
        name="attend",
    )(frame_ids, queries, keys, values_t, *waits)


def attend_back_kernel(
    frame_ids,
    q_ref,
    grad_ref,
    out_ref,
    lse_ref,
    k_ref,
    v_ref,
    kt_ref,
    *refs,
    head_count,
    patch_count,
    first,
    has_start,
):
    dq_ref, dk_ref, dv_ref, dk_sum, dv_sum = refs[-5:]
    position = pl.program_id(0)
    key_stop = frame_ids[position + first] + 1

    @pl.when(position == 0)
    def _():
        dk_sum[...] = refs[0][...] if has_start else jnp.zeros_like(dk_sum)
        dv_sum[...] = refs[1][...] if has_start else jnp.zeros_like(dv_sum)

    q_rows = q_ref[...].astype(f32) * score_scale
    grad_rows = grad_ref[...].astype(f32)
    grad_t = jnp.swapaxes(grad_rows, 0, 1)
    grad_out_t = grad_t * jnp.swapaxes(out_ref[...].astype(f32), 0, 1)
    delta = jnp.concatenate(
        [
            jnp.sum(grad_out_t[head * HD : (head + 1) * HD], axis=0, keepdims=True)
            for head in range(head_count)
        ],
        axis=1,
    )
    q_cols = head_blocks(jnp.swapaxes(q_rows, 0, 1), head_count)
    grad_cols = head_blocks(grad_t, head_count)
    q_stack = head_rows(q_rows, head_count)
    grad_stack = head_rows(grad_rows, head_count)
    lse = lse_ref[0]

    def step(first, frames, sums):
        start = pl.multiple_of(first * patch_count, patch_count)
        here = pl.ds(start, frames * patch_count)
        scores = dot(k_ref[here, :], q_cols)
        grad_probs = dot(v_ref[here, :], grad_cols)
        probs = jnp.exp(scores - lse)
        grad_scores = (probs * (grad_probs - delta)).astype(bf16)
        dv_sum[here, :] += dot(probs.astype(bf16), grad_stack)
        dk_sum[here, :] += dot(grad_scores, q_stack)
        keys_t = kt_ref[:, here]
        return tuple(
            sums[head]
            + dot(
                keys_t[head * HD : (head + 1) * HD],
                grad_scores[:, head * patch_count : (head + 1) * patch_count],
            )
            for head in range(head_count)
        )

    sums = over_key_frames(
        key_stop, step, tuple(jnp.zeros((HD, patch_count), f32) for _ in range(head_count))
    )
    dq_t = jnp.concatenate(sums, axis=0) * score_scale
    dq_ref[...] = jnp.swapaxes(dq_t, 0, 1).astype(bf16)

    @pl.when(position == pl.num_programs(0) - 1)
    def _():
        dk_ref[...] = dk_sum[...].astype(dk_ref.dtype)
        dv_ref[...] = dv_sum[...].astype(dv_ref.dtype)


def attend_back(
    queries, keys, values, keys_t, out, lse, grad, frame_ids, head_count, patch_count, first, last, start, sum_type, waits
):
    lanes = queries.shape[1]
    key_rows = keys.shape[0]
    steps = last - first
    row_count = steps * patch_count
    width = head_count * patch_count
    work = pair_count(key_rows // patch_count, first, steps) * patch_count * width
    block = pl.BlockSpec((patch_count, lanes), lambda j, ids: (j + first, 0))
    whole = pl.BlockSpec((key_rows, lanes), lambda j, ids: (0, 0))
    return pl.pallas_call(
        partial(
            attend_back_kernel,
            head_count=head_count,
            patch_count=patch_count,
            first=first,
            has_start=len(start) > 0,
        ),
        grid_spec=pltpu.PrefetchScalarGridSpec(
            num_scalar_prefetch=1,
            grid=(steps,),
            in_specs=[
                block,
                block,
                block,
                pl.BlockSpec((1, 1, width), lambda j, ids: (j + first, 0, 0)),
                whole,
                whole,
                pl.BlockSpec((lanes, key_rows), lambda j, ids: (0, 0)),
            ]
            + [whole for _ in start]
            + [pl.BlockSpec(memory_space=pl.ANY) for _ in waits],
            out_specs=[
                pl.BlockSpec((patch_count, lanes), lambda j, ids: (j, 0)),
                whole,
                whole,
            ],
            scratch_shapes=[
                pltpu.VMEM((key_rows, lanes), f32),
                pltpu.VMEM((key_rows, lanes), f32),
            ],
        ),
        out_shape=[
            jax.ShapeDtypeStruct((row_count, lanes), bf16),
            jax.ShapeDtypeStruct((key_rows, lanes), sum_type),
            jax.ShapeDtypeStruct((key_rows, lanes), sum_type),
        ],
        compiler_params=pltpu.CompilerParams(vmem_limit_bytes=48 << 20),
        cost_estimate=pl.CostEstimate(
            flops=work * 2560, bytes_accessed=16 * row_count * lanes, transcendentals=work
        ),
        name="attend_back",
    )(frame_ids, queries, grad, out, lse, keys, values, keys_t, *start, *waits)


def unpack_kernel(tail_ref, *refs, half, out_rows):
    up_ref, down_ref, out_ref = refs[-3:]
    ups, downs, outs = [], [], []
    for part in range(tail_ref.shape[0]):
        for row in (0, 2 * half):
            ups.append(tail_ref[part, row : row + half].astype(f32))
            downs.append(tail_ref[part, row + half : row + 2 * half].astype(f32))
        outs.append(tail_ref[part, 4 * half : 4 * half + out_rows].astype(f32))
    up_ref[...] = jnp.swapaxes(jnp.concatenate(ups, axis=0), 0, 1)
    down_ref[...] = jnp.concatenate(downs, axis=0)
    out_ref[...] = jnp.concatenate(outs, axis=0)


def unpack(tail, half, out_rows, waits):
    frame_parts, rows, width = tail.shape
    parts = max(1, 128 // (2 * half))
    return pl.pallas_call(
        partial(unpack_kernel, half=half, out_rows=out_rows),
        grid=(frame_parts // parts,),
        in_specs=[pl.BlockSpec((parts, rows, width), lambda n: (n, 0, 0))]
        + [pl.BlockSpec(memory_space=pl.ANY) for _ in waits],
        out_specs=[
            pl.BlockSpec((width, parts * 2 * half), lambda n: (0, n)),
            pl.BlockSpec((parts * 2 * half, width), lambda n: (n, 0)),
            pl.BlockSpec((parts * out_rows, width), lambda n: (n, 0)),
        ],
        out_shape=[
            jax.ShapeDtypeStruct((width, frame_parts * 2 * half), f32),
            jax.ShapeDtypeStruct((frame_parts * 2 * half, width), f32),
            jax.ShapeDtypeStruct((frame_parts * out_rows, width), f32),
        ],
        compiler_params=pltpu.CompilerParams(vmem_limit_bytes=32 << 20),
        cost_estimate=pl.CostEstimate(
            flops=0, bytes_accessed=frame_parts * rows * width * 6, transcendentals=0
        ),
        name="unpack",
    )(tail, *waits)


def unpack_heads_kernel(
    me_ref, left_ref, right_ref, *refs, left_order, right_order, slot_count, group_count
):
    out_ref, bias_ref = refs[-2:]
    pair = out_ref.shape[2] // HD

    def at(member, order):
        place = 0
        for stage, bit in enumerate(order):
            place = place + ((member // bit) % 2) * (1 << stage)
        return place

    def total(slot, rows):
        result = 0.0
        for group in range(group_count):
            member = (group * slot_count + slot) ^ me_ref[0]
            left = left_ref[at(member, left_order), rows]
            right = right_ref[at(member, right_order), rows]
            result = result + jnp.concatenate([left, right], axis=1).astype(f32)
        return result

    first = pl.program_id(0) * pair
    for kind in range(3):
        rows = slice(kind * HD, (kind + 1) * HD)
        pieces = [total(first + n, rows) for n in range(pair)]
        out_ref[kind] = jnp.swapaxes(jnp.concatenate(pieces, axis=0), 0, 1)
    for n in range(pair):
        bias_ref[n] = total(first + n, slice(3 * HD, 3 * HD + 16))[:8, :128]


def unpack_heads(me, left, right, left_order, right_order, slot_count, waits):
    frame_parts, rows, width = left.shape
    pair = 128 // HD
    whole = pl.BlockSpec((frame_parts, rows, width), lambda n, m: (0, 0, 0))
    return pl.pallas_call(
        partial(
            unpack_heads_kernel,
            left_order=left_order,
            right_order=right_order,
            slot_count=slot_count,
            group_count=frame_parts // slot_count,
        ),
        grid_spec=pltpu.PrefetchScalarGridSpec(
            num_scalar_prefetch=1,
            grid=(slot_count // pair,),
            in_specs=[whole, whole] + [pl.BlockSpec(memory_space=pl.ANY) for _ in waits],
            out_specs=[
                pl.BlockSpec((3, 2 * width, 128), lambda n, m: (0, 0, n)),
                pl.BlockSpec((pair, 8, 128), lambda n, m: (n, 0, 0)),
            ],
        ),
        out_shape=[
            jax.ShapeDtypeStruct((3, 2 * width, slot_count * HD), f32),
            jax.ShapeDtypeStruct((slot_count, 8, 128), f32),
        ],
        compiler_params=pltpu.CompilerParams(vmem_limit_bytes=40 << 20),
        cost_estimate=pl.CostEstimate(
            flops=0, bytes_accessed=frame_parts * rows * width * 8, transcendentals=0
        ),
        name="unpack_heads",
    )(me, left, right, *waits)


ROWS = 128


def project_kernel(
    heads_ref, weight_ref, bias_ref, tokens_ref, mod_ref, attended_ref, branch_ref, hidden_ref
):
    attended = jnp.concatenate([heads_ref[n] for n in range(heads_ref.shape[0])], axis=1)
    attended_ref[...] = attended
    branch = dot(attended, weight_ref[...]) + bias_ref[...]
    branch_ref[...] = branch
    gate_one, shift_two, scale_two = mod_ref[0, 2:3], mod_ref[0, 3:4], mod_ref[0, 4:5]
    normed = layer_norm(tokens_ref[...].astype(f32) + gate_one * branch)[0]
    hidden_ref[...] = (normed * (1.0 + scale_two) + shift_two).astype(bf16)


def project(heads, weight, bias, tokens, modulation):
    frame_parts, rows, lanes = heads.shape
    width = weight.shape[0]
    unit_steps = rows // modulation.shape[0] // ROWS
    block = pl.BlockSpec((ROWS, width), lambda n: (n, 0))
    return pl.pallas_call(
        project_kernel,
        grid=(rows // ROWS,),
        in_specs=[
            pl.BlockSpec((frame_parts, ROWS, lanes), lambda n: (0, n, 0)),
            pl.BlockSpec((width, width), lambda n: (0, 0)),
            pl.BlockSpec((1, width), lambda n: (0, 0)),
            block,
            pl.BlockSpec((1, 6, width), lambda n: (n // unit_steps, 0, 0)),
        ],
        out_specs=[block, block, block],
        out_shape=[
            jax.ShapeDtypeStruct((rows, width), bf16),
            jax.ShapeDtypeStruct((rows, width), f32),
            jax.ShapeDtypeStruct((rows, width), bf16),
        ],
        compiler_params=pltpu.CompilerParams(vmem_limit_bytes=32 << 20),
        cost_estimate=pl.CostEstimate(
            flops=2 * rows * width * width, bytes_accessed=12 * rows * width, transcendentals=0
        ),
        name="project",
    )(heads, weight, bias, tokens, modulation)


def middle_kernel(
    tokens_ref,
    branch_ref,
    two_a_ref,
    two_b_ref,
    back_a_ref,
    back_b_ref,
    grad_ref,
    mod_ref,
    bias_ref,
    weight_ref,
    result_ref,
    middle_grad_ref,
    one_ref,
    heads_ref,
    sums_ref,
    *,
    unit_steps,
):
    gate_one, scale_two, gate_two = mod_ref[0, 2:3], mod_ref[0, 4:5], mod_ref[0, 5:6]
    branch_one = branch_ref[...]
    middle = tokens_ref[...].astype(f32) + gate_one * branch_one
    normed, inverse = layer_norm(middle)
    branch_two = two_a_ref[...] + two_b_ref[...] + bias_ref[...]
    grad = grad_ref[...].astype(f32)
    result_ref[...] = (middle + gate_two * branch_two).astype(bf16)
    back = back_a_ref[...] + back_b_ref[...]
    grad_middle = grad + norm_back(back * (1.0 + scale_two), normed, inverse)
    middle_grad_ref[...] = grad_middle
    grad_one = (gate_one * grad_middle).astype(bf16)
    one_ref[...] = grad_one
    heads = dot_nt(grad_one, weight_ref[...]).astype(bf16)
    lanes = heads_ref.shape[2]
    for part in range(heads_ref.shape[0]):
        heads_ref[part] = heads[:, part * lanes : (part + 1) * lanes]

    @pl.when(pl.program_id(0) % unit_steps == 0)
    def _():
        sums_ref[...] = jnp.zeros_like(sums_ref)

    for row, values in enumerate(
        (grad_middle * branch_one, back, back * normed, grad * branch_two, grad_one.astype(f32))
    ):
        sums_ref[0, row : row + 1] += jnp.sum(values, axis=0, keepdims=True)


def middle_back(
    tokens, branch_one, two_a, two_b, back_a, back_b, grad, modulation, bias, weight, frame_parts
):
    rows, width = tokens.shape
    units = modulation.shape[0]
    unit_steps = rows // units // ROWS
    lanes = width // frame_parts
    block = pl.BlockSpec((ROWS, width), lambda n: (n, 0))
    return pl.pallas_call(
        partial(middle_kernel, unit_steps=unit_steps),
        grid=(rows // ROWS,),
        in_specs=[block] * 7
        + [
            pl.BlockSpec((1, 6, width), lambda n: (n // unit_steps, 0, 0)),
            pl.BlockSpec((1, width), lambda n: (0, 0)),
            pl.BlockSpec((width, width), lambda n: (0, 0)),
        ],
        out_specs=[
            block,
            block,
            block,
            pl.BlockSpec((frame_parts, ROWS, lanes), lambda n: (0, n, 0)),
            pl.BlockSpec((1, 8, width), lambda n: (n // unit_steps, 0, 0)),
        ],
        out_shape=[
            jax.ShapeDtypeStruct((rows, width), bf16),
            jax.ShapeDtypeStruct((rows, width), f32),
            jax.ShapeDtypeStruct((rows, width), bf16),
            jax.ShapeDtypeStruct((frame_parts, rows, lanes), bf16),
            jax.ShapeDtypeStruct((units, 8, width), f32),
        ],
        compiler_params=pltpu.CompilerParams(vmem_limit_bytes=40 << 20),
        cost_estimate=pl.CostEstimate(
            flops=2 * rows * width * width, bytes_accessed=40 * rows * width, transcendentals=0
        ),
        name="middle_back",
    )(tokens, branch_one, two_a, two_b, back_a, back_b, grad, modulation, bias, weight)


def add_pairs_kernel(*refs):
    out_ref = refs[-1]
    row = 0
    for pair in range(len(refs) // 2):
        left, right = refs[2 * pair], refs[2 * pair + 1]
        size = left.shape[2]
        out_ref[:, :, row : row + size, :] = left[...] + right[...]
        row += size


def add_pairs(*pairs):
    chips, shards, _, width = pairs[0].shape
    rows = sum(values.shape[2] for values in pairs[::2])

    def spec(size):
        return pl.BlockSpec((1, shards, size, width), lambda n: (n, 0, 0, 0))

    return pl.pallas_call(
        add_pairs_kernel,
        grid=(chips,),
        in_specs=[spec(values.shape[2]) for values in pairs],
        out_specs=spec(rows),
        out_shape=jax.ShapeDtypeStruct((chips, shards, rows, width), bf16),
        compiler_params=pltpu.CompilerParams(vmem_limit_bytes=32 << 20),
        cost_estimate=pl.CostEstimate(
            flops=0, bytes_accessed=6 * chips * shards * rows * width, transcendentals=0
        ),
        name="add_pairs",
    )(*pairs)


def mlp_kernel(
    core_ref,
    hidden_ref,
    grad_ref,
    bias_ref,
    bias_other_ref,
    up_ref,
    up_other_ref,
    down_ref,
    down_other_ref,
    branch_ref,
    back_ref,
    keep_ref,
    send_ref,
    keep_bias_ref,
    send_bias_ref,
    hidden_t,
    grad_t,
):
    step = pl.program_id(0)
    rows, width = hidden_ref.shape

    @pl.when(step == 0)
    def _():
        branch_ref[...] = jnp.zeros_like(branch_ref)
        back_ref[...] = jnp.zeros_like(back_ref)
        for start in range(0, width, 256):
            cols = slice(start, start + 256)
            hidden_t[cols, :] = jnp.swapaxes(hidden_ref[:, cols].astype(f32), 0, 1).astype(bf16)
            grad_t[cols, :] = jnp.swapaxes(grad_ref[:, cols].astype(f32), 0, 1).astype(bf16)

    slope = math.sqrt(2.0 / math.pi)
    for up, down, bias, out_ref, out_bias_ref in (
        (up_other_ref, down_other_ref, bias_other_ref, send_ref, send_bias_ref),
        (up_ref, down_ref, bias_ref, keep_ref, keep_bias_ref),
    ):
        shards, part = up.shape[1], up.shape[2]
        units = shards * part
        up_rows = up[0].reshape(units, width)
        down_rows = down[0].reshape(units, width)
        pre = dot(up_rows, hidden_t[...]) + bias[0]
        square = pre * pre
        bend = jnp.tanh(slope * pre * (1.0 + 0.044715 * square))
        activated = (0.5 * pre * (1.0 + bend)).astype(bf16)
        gain = 0.5 * (1.0 + bend) + (0.5 * slope) * pre * (1.0 - bend * bend) * (
            1.0 + (3 * 0.044715) * square
        )
        grad_pre = (dot(down_rows, grad_t[...]) * gain).astype(bf16)
        out_bias_ref[0] = jnp.sum(grad_pre.astype(f32), axis=1, keepdims=True)
        out_ref[0, :, :part, :] = (
            dot(grad_pre, hidden_ref[...]).astype(bf16).reshape(shards, part, width)
        )
        out_ref[0, :, part:, :] = (
            dot(activated, grad_ref[...]).astype(bf16).reshape(shards, part, width)
        )
        branch_ref[...] += dot_tn(activated, down_rows)
        back_ref[...] += dot_tn(grad_pre, up_rows)


def mlp(core, hidden, grad, bias, weights, part):
    frame_parts, shards, _, width = weights.shape
    rows = hidden.shape[0]
    steps = frame_parts // 2
    units = shards * part

    def own(m, c):
        return 2 * m + c[0]

    def other(m, c):
        return 2 * m + 1 - c[0]

    def weight_spec(which, row):
        return pl.BlockSpec((1, shards, part, width), lambda m, c: (which(m, c), 0, row, 0))

    whole = pl.BlockSpec((rows, width), lambda m, c: (0, 0), pipeline_mode=pl.Buffered(1))
    sums = pl.BlockSpec((rows, width), lambda m, c: (0, 0))
    out = pl.BlockSpec((1, shards, 2 * part, width), lambda m, c: (m, 0, 0, 0))
    column = pl.BlockSpec((1, units, 1), lambda m, c: (m, 0, 0))
    work = rows * width * units * frame_parts
    return pl.pallas_call(
        mlp_kernel,
        grid_spec=pltpu.PrefetchScalarGridSpec(
            num_scalar_prefetch=1,
            grid=(steps,),
            in_specs=[
                whole,
                whole,
                pl.BlockSpec((1, units, 1), lambda m, c: (own(m, c), 0, 0)),
                pl.BlockSpec((1, units, 1), lambda m, c: (other(m, c), 0, 0)),
                weight_spec(own, 0),
                weight_spec(other, 0),
                weight_spec(own, 1),
                weight_spec(other, 1),
            ],
            out_specs=[sums, sums, out, out, column, column],
            scratch_shapes=[pltpu.VMEM((width, rows), bf16), pltpu.VMEM((width, rows), bf16)],
        ),
        out_shape=[
            jax.ShapeDtypeStruct((rows, width), f32),
            jax.ShapeDtypeStruct((rows, width), f32),
            jax.ShapeDtypeStruct((steps, shards, 2 * part, width), bf16),
            jax.ShapeDtypeStruct((steps, shards, 2 * part, width), bf16),
            jax.ShapeDtypeStruct((steps, units, 1), f32),
            jax.ShapeDtypeStruct((steps, units, 1), f32),
        ],
        compiler_params=pltpu.CompilerParams(vmem_limit_bytes=48 << 20),
        cost_estimate=pl.CostEstimate(
            flops=12 * work,
            bytes_accessed=frame_parts * units * width * 8,
            transcendentals=rows * units * frame_parts,
        ),
        name="mlp",
    )(core, hidden, grad, bias, bias, weights, weights, weights, weights)


def on_device(
    tokens,
    noise_steps,
    ada_weight,
    ada_bias,
    qkv_weight,
    qv_bias,
    out_weight,
    out_bias,
    up_weight,
    up_bias,
    down_weight,
    down_bias,
    cotangent,
):
    clip_count, local_frames, local_patches, model_width = tokens.shape
    tensor_count = lax.axis_size("tensor")
    frame_devices = lax.axis_size("frame")
    frame_at = lax.axis_index("frame")
    tensor_at = lax.axis_index("tensor")
    patch_count = local_patches * tensor_count
    hidden_width = up_weight.shape[1] * tensor_count
    head_total = model_width // HD
    shard_heads = head_total // tensor_count
    head_count = head_total // frame_devices
    lanes = head_count * HD
    unit_total = clip_count * local_frames
    units = unit_total // tensor_count
    sharers = tensor_count // clip_count
    share_at = 0 if sharers == 1 else tensor_at % sharers
    own_rows = units * patch_count
    all_rows = frame_devices * own_rows
    slot = frame_at % shard_heads
    group_at = frame_at // shard_heads
    shard_groups = tensor_count // head_count
    core = frame_at % 2
    chips = frame_devices // 2
    unit_shape = (units, patch_count, model_width)
    column_part = model_width // tensor_count


    def swap_frame(values):
        return lax.all_to_all(values, "frame", split_axis=0, concat_axis=0, tiled=True)

    def shifted(values, shift):
        return lax.ppermute(
            values, "tensor", [(t, (t + shift) % tensor_count) for t in range(tensor_count)]
        )

    def tensor_parts(values):
        return [shifted(values, tensor_count - 1 - n) for n in range(tensor_count - 1)] + [values]

    def tensor_sum(parts):
        total = parts[-1].astype(f32)
        for n in range(tensor_count - 1):
            total = total + shifted(parts[n], n + 1).astype(f32)
        return total

    def exchange(parts):
        last = tensor_count - 1
        return [shifted(parts[last - 1 - n], last - n) for n in range(last)] + [parts[last]]

    def to_relative(values):
        return [
            lax.dynamic_index_in_dim(
                values, (tensor_at + 1 + n) % tensor_count, 0, keepdims=False
            )
            for n in range(tensor_count)
        ]

    def rolled(values, start):
        if isinstance(start, int):
            start = start % tensor_count
            return jnp.concatenate([values[start:], values[:start]])
        return lax.dynamic_slice_in_dim(
            jnp.concatenate([values, values]), start % tensor_count, tensor_count, axis=0
        )


    def head_pairs(head, member):
        pairs = []
        for i in range(frame_devices):
            for t in range(member, tensor_count, sharers):
                shard = (t - member + i // shard_heads + head * shard_groups) % tensor_count
                pairs.append((i * tensor_count + shard, i * tensor_count + t))
        return pairs

    def from_owners(values, head):
        total = None
        for member in range(sharers):
            got = lax.ppermute(values, ("frame", "tensor"), head_pairs(head, member))
            total = got if total is None else total + got
        return total

    def to_owners(pieces):
        total = 0.0
        for head, piece in enumerate(pieces):
            for member in range(sharers):
                pairs = [(user, owner) for owner, user in head_pairs(head, member)]
                total = total + lax.ppermute(piece, ("frame", "tensor"), pairs).astype(f32)
        return total.astype(bf16)

    def to_units(values):
        parts = to_relative(
            values.reshape(tensor_count, units, local_patches, model_width)
        )
        return jnp.stack(exchange(parts), axis=1).reshape(units, patch_count, model_width)

    def from_units(values):
        parts = values.reshape(units, tensor_count, local_patches, model_width)
        mine = jnp.stack(exchange([parts[:, n] for n in range(tensor_count)]))
        return rolled(mine, -1 - tensor_at).reshape(
            clip_count, local_frames, local_patches, model_width
        )

    def core_swap(values):
        return lax.ppermute(values, "frame", [(i, i ^ 1) for i in range(frame_devices)])

    def scatter(values):
        return lax.psum_scatter(
            values.reshape(-1, model_width),
            "frame",
            scatter_dimension=0,
            axis_index_groups=[list(range(c, frame_devices, 2)) for c in range(2)],
            tiled=True,
        ).reshape(values.shape[1:])

    bits = [1 << n for n in range(frame_devices.bit_length() - 1)]
    bit_orders = (tuple(bits[1:] + bits[:1]), tuple(bits[:0:-1] + bits[:1]))

    def doubled(values):
        outs = []
        width = values.shape[1] // 2
        for n, order in enumerate(bit_orders):
            part = values[:, n * width : (n + 1) * width]
            for bit in order:
                pairs = [(i, i ^ bit) for i in range(frame_devices)]
                part = jnp.concatenate([part, lax.ppermute(part, "frame", pairs)])
            outs.append(part.reshape(frame_devices, -1, width))
        return outs

    def frame_parts(values):
        return (
            lax.all_gather(values, "frame", axis=0, tiled=True)
            .reshape(frame_devices, -1, model_width)
        )

    unit_tokens = to_units(tokens)
    act_noise = noise_activation(noise_steps, model_width).reshape(unit_total, model_width)
    mod_local = jnp.einsum(
        "ud,dkj->ukj", act_noise, ada_weight, preferred_element_type=f32
    ) + ada_bias.astype(f32)
    modulation = (
        rolled(
            jnp.stack(
                exchange(to_relative(mod_local.reshape(tensor_count, units * 6, column_part)))
            ),
            -1 - tensor_at,
        )
        .reshape(tensor_count, units, 6, column_part)
        .transpose(1, 2, 0, 3)
        .reshape(units, 6, model_width)
    )
    shift_one = modulation[:, None, 0]
    scale_one = modulation[:, None, 1]
    gate_one = modulation[:, None, 2]
    shift_two = modulation[:, None, 3]
    scale_two = modulation[:, None, 4]
    gate_two = modulation[:, None, 5]

    slot_weight = lax.dynamic_slice_in_dim(qkv_weight, slot * HD, HD, axis=2)
    slot_weight = slot_weight.transpose(1, 2, 0).reshape(3 * HD, model_width)
    slot_bias = lax.dynamic_slice_in_dim(qv_bias, slot * HD, HD, axis=1).reshape(1, 2 * HD)
    slot_bias = jnp.pad(slot_bias, ((0, 15), (0, model_width - 2 * HD)))
    slot_pack = jnp.concatenate([slot_weight, slot_bias])

    def own_part(values):
        size = values.shape[0] // frame_devices
        return lax.dynamic_slice_in_dim(values, frame_at * size, size, axis=0)

    hidden_part = hidden_width // (tensor_count * frame_devices)
    half = hidden_part // 2
    out_rows = out_weight.shape[0] // frame_devices
    up_part = lax.dynamic_slice_in_dim(
        up_weight, frame_at * hidden_part, hidden_part, axis=1
    ).transpose(1, 0)
    down_part = own_part(down_weight)
    bias_part = lax.dynamic_slice_in_dim(up_bias, frame_at * hidden_part, hidden_part, axis=0)
    bias_part = jnp.pad(bias_part[None, :], ((0, 15), (0, model_width - hidden_part)))
    first_pack = jnp.concatenate([up_part[:half], down_part[:half], bias_part])
    second_pack = jnp.concatenate([up_part[half:], down_part[half:]])
    out_pack = own_part(out_weight)
    slot_pack, unit_tokens = lax.optimization_barrier((slot_pack, unit_tokens))
    head_pack = jnp.stack([from_owners(slot_pack, head) for head in range(head_count)])
    first_pack, head_pack = lax.optimization_barrier(
        (jnp.concatenate([first_pack, out_pack]), head_pack)
    )
    first_list = tensor_parts(first_pack)
    out_at = first_pack.shape[0] - out_rows
    first_parts = jnp.concatenate(
        [
            jnp.stack([part[:out_at] for part in first_list]),
            rolled(jnp.stack([part[out_at:] for part in first_list]), -1 - share_at),
        ],
        axis=1,
    ).reshape(-1, model_width)
    head_weight = (
        head_pack[:, : 3 * HD]
        .reshape(head_count, 3, HD, model_width)
        .transpose(1, 0, 2, 3)
        .reshape(3 * lanes, model_width)
    )
    head_bias = head_pack[:, 3 * HD, : 2 * HD]
    head_bias = head_bias.reshape(head_count, 2, HD).transpose(1, 0, 2).reshape(2, lanes)
    head_bias = head_bias.astype(f32)
    qkv_bias = jnp.concatenate([head_bias[0], jnp.zeros((lanes,), f32), head_bias[1]])

    token_values = unit_tokens.astype(f32)
    normed_one, inverse_one = layer_norm(token_values)
    hidden_one = (normed_one * (1.0 + scale_one) + shift_one).astype(bf16)
    hidden_all = lax.all_gather(
        hidden_one.reshape(own_rows, model_width), "frame", axis=0, tiled=True
    )

    first_all = lax.all_gather(first_parts, "frame", axis=0, tiled=True)
    first_all = first_all.reshape(frame_devices, tensor_count, -1, model_width)
    up_bias_all = first_all[:, :, 2 * half, :hidden_part].astype(f32)
    first_bias = up_bias_all[:, :, :half].reshape(frame_devices, tensor_count * half, 1)
    second_bias = up_bias_all[:, :, half:].reshape(frame_devices, tensor_count * half, 1)
    head_parts = HD // out_rows
    out_full = (
        first_all[:, :, 2 * half + 16 :]
        .reshape(shard_heads, head_parts, head_count, shard_groups, out_rows, model_width)
        .transpose(3, 0, 2, 1, 4, 5)
        .reshape(model_width, model_width)
    )

    projected = (dot_nt(hidden_all, head_weight) + qkv_bias).astype(bf16)
    queries = projected[:, :lanes]
    keys = projected[:, lanes : 2 * lanes]
    values = projected[:, 2 * lanes :]

    def share(mine):
        if sharers == 1:
            return mine
        pieces = [mine]
        for shift in range(1, sharers):
            perm = [
                (t, (t // sharers) * sharers + (t + shift) % sharers) for t in range(tensor_count)
            ]
            pieces.append(lax.ppermute(mine, "tensor", perm))
        stacked = jnp.stack(pieces)
        stacked = jnp.stack(
            [
                lax.dynamic_index_in_dim(
                    stacked, (share_at - member) % sharers, 0, keepdims=False
                )
                for member in range(sharers)
            ]
        )
        return (
            stacked.reshape(sharers, frame_devices, own_rows, lanes)
            .transpose(1, 0, 2, 3)
            .reshape(sharers * all_rows, lanes)
        )

    def unshare(partial_sums):
        if sharers == 1:
            return partial_sums
        pieces = (
            partial_sums.reshape(frame_devices, sharers, own_rows, lanes)
            .transpose(1, 0, 2, 3)
            .reshape(sharers, all_rows, lanes)
        )
        total = lax.dynamic_index_in_dim(pieces, share_at, 0, keepdims=False).astype(f32)
        for shift in range(1, sharers):
            perm = [
                (t, (t // sharers) * sharers + (t + shift) % sharers) for t in range(tensor_count)
            ]
            piece = lax.dynamic_index_in_dim(
                pieces, (share_at + shift) % sharers, 0, keepdims=False
            )
            total = total + lax.ppermute(piece, "tensor", perm).astype(f32)
        return total.astype(bf16)

    keys_all = share(keys)
    values_all = share(values)
    unit_ids = jnp.arange(frame_devices * units, dtype=jnp.int32)
    frame_ids = (
        (unit_ids // units) * local_frames + share_at * units + unit_ids % units
    )
    values_t = values_all.T
    steps = all_rows // patch_count
    second_pack, queries = lax.optimization_barrier((second_pack, queries))
    second_list = tensor_parts(second_pack)
    cut = steps * 11 // 16
    heads_a, lse_a = attend(
        queries, keys_all, values_t, frame_ids, head_count, patch_count, 0, cut, ()
    )
    heads_a, *second_list = lax.optimization_barrier((heads_a, *second_list))
    second_parts = jnp.concatenate(second_list)
    cotangent, second_parts = lax.optimization_barrier((cotangent, second_parts))
    upstream = to_units(cotangent)
    heads_b, lse_b = attend(
        queries, keys_all, values_t, frame_ids, head_count, patch_count, cut, steps,
        (second_parts,),
    )
    attended_heads = jnp.concatenate([heads_a, heads_b])
    row_lse = jnp.concatenate([lse_a, lse_b])
    second_all = lax.all_gather(
        second_parts, "frame", axis=0, tiled=True
    ).reshape(frame_devices, tensor_count, -1, model_width)
    heads_here = swap_frame(attended_heads.reshape(frame_devices, own_rows, lanes))

    grad_two = (gate_two * upstream.astype(f32)).astype(bf16).reshape(own_rows, model_width)
    grad_down_bias = jnp.sum(grad_two.astype(f32), axis=0)

    flat_tokens = unit_tokens.reshape(own_rows, model_width)
    attended, branch_one, hidden_two = project(
        heads_here, out_full, out_bias.astype(f32)[None, :], flat_tokens, modulation
    )

    core_id = core.astype(jnp.int32).reshape(1)
    branch_a, back_a, keep_a, send_a, keep_bias_a, send_bias_a = mlp(
        core_id, hidden_two, grad_two, first_bias, first_all, half
    )
    got_a = core_swap(send_a)
    branch_b, back_b, keep_b, send_b, keep_bias_b, send_bias_b = mlp(
        core_id, hidden_two, grad_two, second_bias, second_all, half
    )
    got_b = core_swap(send_b)
    got_a, branch_b = lax.optimization_barrier((got_a, branch_b))
    back_b, first_half = lax.optimization_barrier((back_b, add_pairs(keep_a, got_a)))
    first_sum = scatter(first_half)
    result, grad_middle, grad_one, head_grads, unit_sums = middle_back(
        flat_tokens, branch_one, branch_a, branch_b, back_a, back_b,
        upstream.reshape(own_rows, model_width), modulation, down_bias.astype(f32)[None, :],
        out_full, frame_devices,
    )
    grad_heads = swap_frame(head_grads).reshape(all_rows, lanes)
    result = from_units(result.reshape(unit_shape))
    grad_middle = grad_middle.reshape(unit_shape)
    grad_gate_one, grad_shift_two, grad_scale_two, grad_gate_two = (
        unit_sums[:, n] for n in range(4)
    )
    grad_out_bias = jnp.sum(unit_sums[:, 4], axis=0)

    grad_out = (
        dot_tn(attended, grad_one)
        .astype(bf16)
        .reshape(shard_groups, shard_heads, head_count, head_parts, out_rows, model_width)
        .transpose(2, 0, 1, 3, 4, 5)
        .reshape(tensor_count, frame_devices, out_rows, model_width)
    )
    grad_out = rolled(grad_out, share_at + 1).transpose(1, 0, 2, 3)
    width_part = model_width // frame_devices

    def by_core(keep_part, send_part):
        pair = jnp.stack([keep_part, send_part], axis=1)
        return jnp.where(core == 0, pair, pair[:, ::-1]).reshape(
            (frame_devices,) + keep_part.shape[1:]
        )

    grad_up_bias = jnp.concatenate(
        [
            by_core(keep_bias_a, send_bias_a).reshape(frame_devices, tensor_count, half),
            by_core(keep_bias_b, send_bias_b).reshape(frame_devices, tensor_count, half),
        ],
        axis=2,
    )
    once = jnp.concatenate(
        [
            grad_down_bias.reshape(frame_devices, 1, width_part),
            grad_out_bias.reshape(frame_devices, 1, width_part),
        ],
        axis=2,
    )
    bias_row = jnp.concatenate(
        [jnp.broadcast_to(once, (frame_devices, tensor_count, 2 * width_part)), grad_up_bias],
        axis=2,
    ).astype(bf16)
    bias_row = jnp.pad(
        bias_row[:, :, None, :], ((0, 0), (0, 0), (0, 15), (0, model_width - bias_row.shape[2]))
    )
    out_pairs = jnp.concatenate([grad_out, bias_row], axis=2).reshape(
        chips, 2, tensor_count, out_rows + 16, model_width
    )
    got_out = core_swap(lax.dynamic_index_in_dim(out_pairs, 1 - core, 1, keepdims=False))
    late_half = add_pairs(
        keep_b,
        got_b,
        lax.dynamic_index_in_dim(out_pairs, core, 1, keepdims=False),
        got_out,
    )
    late_sum = scatter(late_half)
    first_list = exchange([first_sum[n] for n in range(tensor_count)])

    keys_t = keys_all.T
    grad_q_a, *sums = attend_back(
        queries, keys_all, values_all, keys_t, attended_heads, row_lse, grad_heads,
        frame_ids, head_count, patch_count, 0, cut, (), f32, (late_half, result),
    )
    *sums, first_list = lax.optimization_barrier((*sums, first_list))
    first_total = sum(part.astype(f32) for part in first_list).astype(bf16)
    grad_q_b, grad_k_all, grad_v_all = attend_back(
        queries, keys_all, values_all, keys_t, attended_heads, row_lse, grad_heads,
        frame_ids, head_count, patch_count, cut, steps, tuple(sums), bf16, (first_total,),
    )
    grad_q = jnp.concatenate([grad_q_a, grad_q_b])
    grad_k = unshare(grad_k_all)
    grad_v = unshare(grad_v_all)
    grad_projected = jnp.concatenate([grad_q, grad_k, grad_v], axis=1)
    grad_hidden_part, grad_projected = lax.optimization_barrier(
        (dot(grad_projected, head_weight).astype(bf16), grad_projected)
    )
    grad_hidden_one = lax.psum_scatter(grad_hidden_part, "frame", scatter_dimension=0, tiled=True)
    grad_hidden_one = grad_hidden_one.astype(f32).reshape(unit_shape)

    late_total = tensor_sum([late_sum[n] for n in range(tensor_count)]).astype(bf16)
    grad_head_weight = dot_tn(grad_projected, hidden_all).astype(bf16)
    grad_slots = (
        grad_head_weight.reshape(3, head_count, HD, model_width)
        .transpose(1, 0, 2, 3)
        .reshape(head_count, 3 * HD, model_width)
    )
    grad_head_bias = jnp.stack(
        [jnp.sum(grad_q.astype(f32), axis=0), jnp.sum(grad_v.astype(f32), axis=0)]
    ).astype(bf16)
    grad_head_bias = grad_head_bias.reshape(2, head_count, HD).transpose(1, 0, 2)
    grad_head_bias = jnp.pad(
        grad_head_bias.reshape(head_count, 1, 2 * HD),
        ((0, 0), (0, 15), (0, model_width - 2 * HD)),
    )
    grad_slots = jnp.concatenate([grad_slots, grad_head_bias], axis=1)

    slots_total = to_owners([grad_slots[head] for head in range(head_count)])

    slots_left, slots_right = doubled(slots_total)
    grad_hidden_one, slots_left, slots_right = lax.optimization_barrier(
        (grad_hidden_one, slots_left, slots_right)
    )
    grad_scale_one = jnp.sum(grad_hidden_one * normed_one, axis=1)
    grad_shift_one = jnp.sum(grad_hidden_one, axis=1)
    grad_tokens = (
        grad_middle
        + norm_back(grad_hidden_one * (1.0 + scale_one), normed_one, inverse_one)
    ).astype(bf16)
    tail_all = frame_parts(jnp.concatenate([first_total, late_total]))
    grad_tokens = from_units(grad_tokens)
    grad_modulation = jnp.stack(
        [
            grad_shift_one,
            grad_scale_one,
            grad_gate_one,
            grad_shift_two,
            grad_scale_two,
            grad_gate_two,
        ],
        axis=1,
    )
    unit_steps = lax.dynamic_slice_in_dim(
        noise_steps.reshape(unit_total), tensor_at * units, units
    ).astype(f32)
    grad_mod_parts = exchange(
        to_relative(
            jnp.concatenate(
                [
                    grad_modulation.reshape(units, 6, tensor_count, column_part)
                    .transpose(2, 0, 1, 3)
                    .reshape(tensor_count, units, 6 * column_part),
                    jnp.broadcast_to(unit_steps[None, :, None], (tensor_count, units, 128)),
                ],
                axis=2,
            )
        )
    )
    grad_mod_all = lax.all_gather(
        jnp.stack(grad_mod_parts).reshape(unit_total, -1), "frame", axis=0, tiled=True
    )
    act_all = noise_activation(grad_mod_all[:, -1], model_width)
    grad_mod_all = grad_mod_all[:, :-128].reshape(-1, 6, column_part)
    grad_ada_weight = jnp.einsum(
        "ud,ukj->dkj", act_all.astype(f32), grad_mod_all, precision=lax.Precision.HIGH
    )
    grad_ada_bias = jnp.sum(grad_mod_all, axis=0)
    final_up, final_down, final_out = unpack(tail_all, half, out_rows, (grad_tokens,))
    tail_bias = tail_all[:, 4 * half + out_rows].astype(f32)
    final_down_bias = tail_bias[:, :width_part].reshape(model_width)
    final_out_bias = tail_bias[:, width_part : 2 * width_part].reshape(model_width)
    final_up_bias = tail_bias[:, 2 * width_part : 2 * width_part + hidden_part].reshape(
        up_bias.shape
    )
    final_qkv, bias_sums = unpack_heads(
        frame_at.astype(jnp.int32).reshape(1), slots_left, slots_right, *bit_orders, shard_heads, ()
    )
    final_qkv = final_qkv.transpose(1, 0, 2)
    final_qv_bias = (
        bias_sums[:, 0].reshape(shard_heads, 2, HD).transpose(1, 0, 2).reshape(qv_bias.shape)
    )
    return (
        result,
        grad_tokens.astype(f32),
        grad_ada_weight,
        grad_ada_bias,
        final_qkv,
        final_qv_bias,
        final_out,
        final_out_bias,
        final_up,
        final_up_bias,
        final_down,
        final_down_bias,
    )


def solution(mesh):
    in_specs = (
        P(None, "frame", "tensor", None),
        P(None, "frame"),
        P(None, None, "tensor"),
        P(None, "tensor"),
        P(None, None, "tensor"),
        P(None, "tensor"),
        P("tensor", None),
        P(),
        P(None, "tensor"),
        P("tensor"),
        P("tensor", None),
        P(),
        P(None, "frame", "tensor", None),
    )
    out_specs = (
        P(None, "frame", "tensor", None),
        P(None, "frame", "tensor", None),
        P(None, None, "tensor"),
        P(None, "tensor"),
        P(None, None, "tensor"),
        P(None, "tensor"),
        P("tensor", None),
        P(),
        P(None, "tensor"),
        P("tensor"),
        P("tensor", None),
        P(),
    )
    return jax.shard_map(
        on_device, mesh=mesh, in_specs=in_specs, out_specs=out_specs, check_vma=False
    )
```

```python
from functools import partial
import math

import jax
import jax.numpy as jnp
from jax import lax
from jax.experimental import pallas as pl
from jax.experimental.pallas import tpu as pltpu
from jax.sharding import PartitionSpec as P

HD = 64
f32 = jnp.float32
bf16 = jnp.bfloat16
score_scale = HD ** (-0.5)


def noise_embedding(noise_steps, model_width):
    half_width = model_width // 2
    frequency = jnp.exp(-math.log(10000.0) * jnp.arange(half_width, dtype=f32) / half_width)
    angles = noise_steps.astype(f32)[..., None] * frequency
    return jnp.concatenate([jnp.cos(angles), jnp.sin(angles)], axis=-1)


def noise_activation(noise_steps, model_width):
    return jax.nn.silu(noise_embedding(noise_steps, model_width)).astype(bf16)


def layer_norm(values):
    centred = values - jnp.mean(values, axis=-1, keepdims=True)
    inverse = lax.rsqrt(jnp.mean(centred * centred, axis=-1, keepdims=True) + 1e-06)
    return (centred * inverse, inverse)


def norm_back(grad_normed, normed, inverse):
    return inverse * (
        grad_normed
        - jnp.mean(grad_normed, axis=-1, keepdims=True)
        - normed * jnp.mean(grad_normed * normed, axis=-1, keepdims=True)
    )


def dot(left, right):
    return lax.dot_general(left, right, (((1,), (0,)), ((), ())), preferred_element_type=f32)


def dot_nt(left, right):
    return lax.dot_general(left, right, (((1,), (1,)), ((), ())), preferred_element_type=f32)


def dot_tn(left, right):
    return lax.dot_general(left, right, (((0,), (0,)), ((), ())), preferred_element_type=f32)


GROUP = 8


def head_blocks(transposed, head_count):
    rows = lax.broadcasted_iota(jnp.int32, transposed.shape, 0) // HD
    return jnp.concatenate(
        [jnp.where(rows == head, transposed, 0.0) for head in range(head_count)], axis=1
    ).astype(bf16)


def head_rows(natural, head_count):
    lanes = lax.broadcasted_iota(jnp.int32, natural.shape, 1) // HD
    return jnp.concatenate(
        [jnp.where(lanes == head, natural, 0.0) for head in range(head_count)], axis=0
    ).astype(bf16)


def over_key_frames(key_stop, step, carry):
    done = 0
    size = 1
    while size < GROUP:
        once = (key_stop // size) % 2
        carry = lax.fori_loop(
            0, once, lambda _, c, first=done, size=size: step(first, size, c), carry
        )
        done = done + once * size
        size *= 2
    return lax.fori_loop(
        0, key_stop // GROUP, lambda n, c: step(done + GROUP * n, GROUP, c), carry
    )


def attend_kernel(frame_ids, q_ref, k_ref, vt_ref, *refs, head_count, patch_count, first):
    out_ref, lse_ref = refs[-2:]
    key_stop = frame_ids[pl.program_id(0) + first] + 1
    q_cols = head_blocks(jnp.swapaxes(q_ref[...].astype(f32), 0, 1) * score_scale, head_count)
    width = head_count * patch_count

    def step(first, frames, carry):
        row_max, row_total, sums = carry
        start = pl.multiple_of(first * patch_count, patch_count)
        scores = dot(k_ref[pl.ds(start, frames * patch_count), :], q_cols)
        new_max = jnp.maximum(row_max, jnp.max(scores, axis=0, keepdims=True))
        rescale = jnp.exp(row_max - new_max)
        weights = jnp.exp(scores - new_max)
        row_total = row_total * rescale + jnp.sum(weights, axis=0, keepdims=True)
        weights = weights.astype(bf16)
        values_t = vt_ref[:, pl.ds(start, frames * patch_count)]
        parts = []
        for head in range(head_count):
            cols = slice(head * patch_count, (head + 1) * patch_count)
            rows = slice(head * HD, (head + 1) * HD)
            parts.append(sums[head] * rescale[:, cols] + dot(values_t[rows], weights[:, cols]))
        return (new_max, row_total, tuple(parts))

    row_max, row_total, sums = over_key_frames(
        key_stop,
        step,
        (
            jnp.full((1, width), -1e30, f32),
            jnp.zeros((1, width), f32),
            tuple(jnp.zeros((HD, patch_count), f32) for _ in range(head_count)),
        ),
    )
    inverse = 1.0 / row_total
    out_t = jnp.concatenate(
        [
            sums[head] * inverse[:, head * patch_count : (head + 1) * patch_count]
            for head in range(head_count)
        ],
        axis=0,
    )
    out_ref[...] = jnp.swapaxes(out_t, 0, 1).astype(bf16)
    lse_ref[0] = row_max + jnp.log(row_total)


def pair_count(frame_total, first, steps):
    return steps * (frame_total * (2 * first + steps) // (2 * (first + steps)) + 1) // 2


def attend(queries, keys, values_t, frame_ids, head_count, patch_count, first, last, waits):
    lanes = queries.shape[1]
    key_rows = keys.shape[0]
    steps = last - first
    row_count = steps * patch_count
    width = head_count * patch_count
    work = pair_count(key_rows // patch_count, first, steps) * patch_count * width
    return pl.pallas_call(
        partial(
            attend_kernel, head_count=head_count, patch_count=patch_count, first=first
        ),
        grid_spec=pltpu.PrefetchScalarGridSpec(
            num_scalar_prefetch=1,
            grid=(steps,),
            in_specs=[
                pl.BlockSpec((patch_count, lanes), lambda j, ids: (j + first, 0)),
                pl.BlockSpec((key_rows, lanes), lambda j, ids: (0, 0)),
                pl.BlockSpec((lanes, key_rows), lambda j, ids: (0, 0)),
            ]
            + [pl.BlockSpec(memory_space=pl.ANY) for _ in waits],
            out_specs=[
                pl.BlockSpec((patch_count, lanes), lambda j, ids: (j, 0)),
                pl.BlockSpec((1, 1, width), lambda j, ids: (j, 0, 0)),
            ],
        ),
        out_shape=[
            jax.ShapeDtypeStruct((row_count, lanes), bf16),
            jax.ShapeDtypeStruct((steps, 1, width), f32),
        ],
        compiler_params=pltpu.CompilerParams(vmem_limit_bytes=40 << 20),
        cost_estimate=pl.CostEstimate(
            flops=work * 1024, bytes_accessed=8 * row_count * lanes, transcendentals=work
        ),
        name="attend",
    )(frame_ids, queries, keys, values_t, *waits)


def attend_back_kernel(
    frame_ids,
    q_ref,
    grad_ref,
    out_ref,
    lse_ref,
    k_ref,
    v_ref,
    kt_ref,
    *refs,
    head_count,
    patch_count,
    first,
    has_start,
):
    dq_ref, dk_ref, dv_ref, dk_sum, dv_sum = refs[-5:]
    position = pl.program_id(0)
    key_stop = frame_ids[position + first] + 1

    @pl.when(position == 0)
    def _():
        dk_sum[...] = refs[0][...] if has_start else jnp.zeros_like(dk_sum)
        dv_sum[...] = refs[1][...] if has_start else jnp.zeros_like(dv_sum)

    q_rows = q_ref[...].astype(f32) * score_scale
    grad_rows = grad_ref[...].astype(f32)
    grad_t = jnp.swapaxes(grad_rows, 0, 1)
    grad_out_t = grad_t * jnp.swapaxes(out_ref[...].astype(f32), 0, 1)
    delta = jnp.concatenate(
        [
            jnp.sum(grad_out_t[head * HD : (head + 1) * HD], axis=0, keepdims=True)
            for head in range(head_count)
        ],
        axis=1,
    )
    q_cols = head_blocks(jnp.swapaxes(q_rows, 0, 1), head_count)
    grad_cols = head_blocks(grad_t, head_count)
    q_stack = head_rows(q_rows, head_count)
    grad_stack = head_rows(grad_rows, head_count)
    lse = lse_ref[0]

    def step(first, frames, sums):
        start = pl.multiple_of(first * patch_count, patch_count)
        here = pl.ds(start, frames * patch_count)
        scores = dot(k_ref[here, :], q_cols)
        grad_probs = dot(v_ref[here, :], grad_cols)
        probs = jnp.exp(scores - lse)
        grad_scores = (probs * (grad_probs - delta)).astype(bf16)
        dv_sum[here, :] += dot(probs.astype(bf16), grad_stack)
        dk_sum[here, :] += dot(grad_scores, q_stack)
        keys_t = kt_ref[:, here]
        return tuple(
            sums[head]
            + dot(
                keys_t[head * HD : (head + 1) * HD],
                grad_scores[:, head * patch_count : (head + 1) * patch_count],
            )
            for head in range(head_count)
        )

    sums = over_key_frames(
        key_stop, step, tuple(jnp.zeros((HD, patch_count), f32) for _ in range(head_count))
    )
    dq_t = jnp.concatenate(sums, axis=0) * score_scale
    dq_ref[...] = jnp.swapaxes(dq_t, 0, 1).astype(bf16)

    @pl.when(position == pl.num_programs(0) - 1)
    def _():
        dk_ref[...] = dk_sum[...].astype(dk_ref.dtype)
        dv_ref[...] = dv_sum[...].astype(dv_ref.dtype)


def attend_back(
    queries, keys, values, keys_t, out, lse, grad, frame_ids, head_count, patch_count, first, last, start, sum_type, waits
):
    lanes = queries.shape[1]
    key_rows = keys.shape[0]
    steps = last - first
    row_count = steps * patch_count
    width = head_count * patch_count
    work = pair_count(key_rows // patch_count, first, steps) * patch_count * width
    block = pl.BlockSpec((patch_count, lanes), lambda j, ids: (j + first, 0))
    whole = pl.BlockSpec((key_rows, lanes), lambda j, ids: (0, 0))
    return pl.pallas_call(
        partial(
            attend_back_kernel,
            head_count=head_count,
            patch_count=patch_count,
            first=first,
            has_start=len(start) > 0,
        ),
        grid_spec=pltpu.PrefetchScalarGridSpec(
            num_scalar_prefetch=1,
            grid=(steps,),
            in_specs=[
                block,
                block,
                block,
                pl.BlockSpec((1, 1, width), lambda j, ids: (j + first, 0, 0)),
                whole,
                whole,
                pl.BlockSpec((lanes, key_rows), lambda j, ids: (0, 0)),
            ]
            + [whole for _ in start]
            + [pl.BlockSpec(memory_space=pl.ANY) for _ in waits],
            out_specs=[
                pl.BlockSpec((patch_count, lanes), lambda j, ids: (j, 0)),
                whole,
                whole,
            ],
            scratch_shapes=[
                pltpu.VMEM((key_rows, lanes), f32),
                pltpu.VMEM((key_rows, lanes), f32),
            ],
        ),
        out_shape=[
            jax.ShapeDtypeStruct((row_count, lanes), bf16),
            jax.ShapeDtypeStruct((key_rows, lanes), sum_type),
            jax.ShapeDtypeStruct((key_rows, lanes), sum_type),
        ],
        compiler_params=pltpu.CompilerParams(vmem_limit_bytes=48 << 20),
        cost_estimate=pl.CostEstimate(
            flops=work * 2560, bytes_accessed=16 * row_count * lanes, transcendentals=work
        ),
        name="attend_back",
    )(frame_ids, queries, grad, out, lse, keys, values, keys_t, *start, *waits)


def unpack_kernel(tail_ref, *refs, half, out_rows):
    up_ref, down_ref, out_ref = refs[-3:]
    ups, downs, outs = [], [], []
    for part in range(tail_ref.shape[0]):
        for row in (0, 2 * half):
            ups.append(tail_ref[part, row : row + half].astype(f32))
            downs.append(tail_ref[part, row + half : row + 2 * half].astype(f32))
        outs.append(tail_ref[part, 4 * half : 4 * half + out_rows].astype(f32))
    up_ref[...] = jnp.swapaxes(jnp.concatenate(ups, axis=0), 0, 1)
    down_ref[...] = jnp.concatenate(downs, axis=0)
    out_ref[...] = jnp.concatenate(outs, axis=0)


def unpack(tail, half, out_rows, waits):
    frame_parts, rows, width = tail.shape
    parts = max(1, 128 // (2 * half))
    return pl.pallas_call(
        partial(unpack_kernel, half=half, out_rows=out_rows),
        grid=(frame_parts // parts,),
        in_specs=[pl.BlockSpec((parts, rows, width), lambda n: (n, 0, 0))]
        + [pl.BlockSpec(memory_space=pl.ANY) for _ in waits],
        out_specs=[
            pl.BlockSpec((width, parts * 2 * half), lambda n: (0, n)),
            pl.BlockSpec((parts * 2 * half, width), lambda n: (n, 0)),
            pl.BlockSpec((parts * out_rows, width), lambda n: (n, 0)),
        ],
        out_shape=[
            jax.ShapeDtypeStruct((width, frame_parts * 2 * half), f32),
            jax.ShapeDtypeStruct((frame_parts * 2 * half, width), f32),
            jax.ShapeDtypeStruct((frame_parts * out_rows, width), f32),
        ],
        compiler_params=pltpu.CompilerParams(vmem_limit_bytes=32 << 20),
        cost_estimate=pl.CostEstimate(
            flops=0, bytes_accessed=frame_parts * rows * width * 6, transcendentals=0
        ),
        name="unpack",
    )(tail, *waits)


def unpack_heads_kernel(
    me_ref, left_ref, right_ref, *refs, left_order, right_order, slot_count, group_count
):
    out_ref, bias_ref = refs[-2:]
    pair = out_ref.shape[2] // HD

    def at(member, order):
        place = 0
        for stage, bit in enumerate(order):
            place = place + ((member // bit) % 2) * (1 << stage)
        return place

    def total(slot, rows):
        result = 0.0
        for group in range(group_count):
            member = (group * slot_count + slot) ^ me_ref[0]
            left = left_ref[at(member, left_order), rows]
            right = right_ref[at(member, right_order), rows]
            result = result + jnp.concatenate([left, right], axis=1).astype(f32)
        return result

    first = pl.program_id(0) * pair
    for kind in range(3):
        rows = slice(kind * HD, (kind + 1) * HD)
        pieces = [total(first + n, rows) for n in range(pair)]
        out_ref[kind] = jnp.swapaxes(jnp.concatenate(pieces, axis=0), 0, 1)
    for n in range(pair):
        bias_ref[n] = total(first + n, slice(3 * HD, 3 * HD + 16))[:8, :128]


def unpack_heads(me, left, right, left_order, right_order, slot_count, waits):
    frame_parts, rows, width = left.shape
    pair = 128 // HD
    whole = pl.BlockSpec((frame_parts, rows, width), lambda n, m: (0, 0, 0))
    return pl.pallas_call(
        partial(
            unpack_heads_kernel,
            left_order=left_order,
            right_order=right_order,
            slot_count=slot_count,
            group_count=frame_parts // slot_count,
        ),
        grid_spec=pltpu.PrefetchScalarGridSpec(
            num_scalar_prefetch=1,
            grid=(slot_count // pair,),
            in_specs=[whole, whole] + [pl.BlockSpec(memory_space=pl.ANY) for _ in waits],
            out_specs=[
                pl.BlockSpec((3, 2 * width, 128), lambda n, m: (0, 0, n)),
                pl.BlockSpec((pair, 8, 128), lambda n, m: (n, 0, 0)),
            ],
        ),
        out_shape=[
            jax.ShapeDtypeStruct((3, 2 * width, slot_count * HD), f32),
            jax.ShapeDtypeStruct((slot_count, 8, 128), f32),
        ],
        compiler_params=pltpu.CompilerParams(vmem_limit_bytes=40 << 20),
        cost_estimate=pl.CostEstimate(
            flops=0, bytes_accessed=frame_parts * rows * width * 8, transcendentals=0
        ),
        name="unpack_heads",
    )(me, left, right, *waits)


ROWS = 128


def project_kernel(
    heads_ref, weight_ref, bias_ref, tokens_ref, mod_ref, attended_ref, branch_ref, hidden_ref
):
    attended = jnp.concatenate([heads_ref[n] for n in range(heads_ref.shape[0])], axis=1)
    attended_ref[...] = attended
    branch = dot(attended, weight_ref[...]) + bias_ref[...]
    branch_ref[...] = branch
    gate_one, shift_two, scale_two = mod_ref[0, 2:3], mod_ref[0, 3:4], mod_ref[0, 4:5]
    normed = layer_norm(tokens_ref[...].astype(f32) + gate_one * branch)[0]
    hidden_ref[...] = (normed * (1.0 + scale_two) + shift_two).astype(bf16)


def project(heads, weight, bias, tokens, modulation):
    frame_parts, rows, lanes = heads.shape
    width = weight.shape[0]
    unit_steps = rows // modulation.shape[0] // ROWS
    block = pl.BlockSpec((ROWS, width), lambda n: (n, 0))
    return pl.pallas_call(
        project_kernel,
        grid=(rows // ROWS,),
        in_specs=[
            pl.BlockSpec((frame_parts, ROWS, lanes), lambda n: (0, n, 0)),
            pl.BlockSpec((width, width), lambda n: (0, 0)),
            pl.BlockSpec((1, width), lambda n: (0, 0)),
            block,
            pl.BlockSpec((1, 6, width), lambda n: (n // unit_steps, 0, 0)),
        ],
        out_specs=[block, block, block],
        out_shape=[
            jax.ShapeDtypeStruct((rows, width), bf16),
            jax.ShapeDtypeStruct((rows, width), f32),
            jax.ShapeDtypeStruct((rows, width), bf16),
        ],
        compiler_params=pltpu.CompilerParams(vmem_limit_bytes=32 << 20),
        cost_estimate=pl.CostEstimate(
            flops=2 * rows * width * width, bytes_accessed=12 * rows * width, transcendentals=0
        ),
        name="project",
    )(heads, weight, bias, tokens, modulation)


def middle_kernel(
    tokens_ref,
    branch_ref,
    two_a_ref,
    two_b_ref,
    back_a_ref,
    back_b_ref,
    grad_ref,
    mod_ref,
    bias_ref,
    weight_ref,
    result_ref,
    middle_grad_ref,
    one_ref,
    heads_ref,
    sums_ref,
    *,
    unit_steps,
):
    gate_one, scale_two, gate_two = mod_ref[0, 2:3], mod_ref[0, 4:5], mod_ref[0, 5:6]
    branch_one = branch_ref[...]
    middle = tokens_ref[...].astype(f32) + gate_one * branch_one
    normed, inverse = layer_norm(middle)
    branch_two = two_a_ref[...] + two_b_ref[...] + bias_ref[...]
    grad = grad_ref[...].astype(f32)
    result_ref[...] = (middle + gate_two * branch_two).astype(bf16)
    back = back_a_ref[...] + back_b_ref[...]
    grad_middle = grad + norm_back(back * (1.0 + scale_two), normed, inverse)
    middle_grad_ref[...] = grad_middle
    grad_one = (gate_one * grad_middle).astype(bf16)
    one_ref[...] = grad_one
    heads = dot_nt(grad_one, weight_ref[...]).astype(bf16)
    lanes = heads_ref.shape[2]
    for part in range(heads_ref.shape[0]):
        heads_ref[part] = heads[:, part * lanes : (part + 1) * lanes]

    @pl.when(pl.program_id(0) % unit_steps == 0)
    def _():
        sums_ref[...] = jnp.zeros_like(sums_ref)

    for row, values in enumerate(
        (grad_middle * branch_one, back, back * normed, grad * branch_two, grad_one.astype(f32))
    ):
        sums_ref[0, row : row + 1] += jnp.sum(values, axis=0, keepdims=True)


def middle_back(
    tokens, branch_one, two_a, two_b, back_a, back_b, grad, modulation, bias, weight, frame_parts
):
    rows, width = tokens.shape
    units = modulation.shape[0]
    unit_steps = rows // units // ROWS
    lanes = width // frame_parts
    block = pl.BlockSpec((ROWS, width), lambda n: (n, 0))
    return pl.pallas_call(
        partial(middle_kernel, unit_steps=unit_steps),
        grid=(rows // ROWS,),
        in_specs=[block] * 7
        + [
            pl.BlockSpec((1, 6, width), lambda n: (n // unit_steps, 0, 0)),
            pl.BlockSpec((1, width), lambda n: (0, 0)),
            pl.BlockSpec((width, width), lambda n: (0, 0)),
        ],
        out_specs=[
            block,
            block,
            block,
            pl.BlockSpec((frame_parts, ROWS, lanes), lambda n: (0, n, 0)),
            pl.BlockSpec((1, 8, width), lambda n: (n // unit_steps, 0, 0)),
        ],
        out_shape=[
            jax.ShapeDtypeStruct((rows, width), bf16),
            jax.ShapeDtypeStruct((rows, width), f32),
            jax.ShapeDtypeStruct((rows, width), bf16),
            jax.ShapeDtypeStruct((frame_parts, rows, lanes), bf16),
            jax.ShapeDtypeStruct((units, 8, width), f32),
        ],
        compiler_params=pltpu.CompilerParams(vmem_limit_bytes=40 << 20),
        cost_estimate=pl.CostEstimate(
            flops=2 * rows * width * width, bytes_accessed=40 * rows * width, transcendentals=0
        ),
        name="middle_back",
    )(tokens, branch_one, two_a, two_b, back_a, back_b, grad, modulation, bias, weight)


def add_pairs_kernel(*refs):
    out_ref = refs[-1]
    row = 0
    for pair in range(len(refs) // 2):
        left, right = refs[2 * pair], refs[2 * pair + 1]
        size = left.shape[2]
        out_ref[:, :, row : row + size, :] = left[...] + right[...]
        row += size


def add_pairs(*pairs):
    chips, shards, _, width = pairs[0].shape
    rows = sum(values.shape[2] for values in pairs[::2])

    def spec(size):
        return pl.BlockSpec((1, shards, size, width), lambda n: (n, 0, 0, 0))

    return pl.pallas_call(
        add_pairs_kernel,
        grid=(chips,),
        in_specs=[spec(values.shape[2]) for values in pairs],
        out_specs=spec(rows),
        out_shape=jax.ShapeDtypeStruct((chips, shards, rows, width), bf16),
        compiler_params=pltpu.CompilerParams(vmem_limit_bytes=32 << 20),
        cost_estimate=pl.CostEstimate(
            flops=0, bytes_accessed=6 * chips * shards * rows * width, transcendentals=0
        ),
        name="add_pairs",
    )(*pairs)


def mlp_kernel(
    core_ref,
    hidden_ref,
    grad_ref,
    bias_ref,
    bias_other_ref,
    up_ref,
    up_other_ref,
    down_ref,
    down_other_ref,
    branch_ref,
    back_ref,
    keep_ref,
    send_ref,
    keep_bias_ref,
    send_bias_ref,
    hidden_t,
    grad_t,
):
    step = pl.program_id(0)
    rows, width = hidden_ref.shape

    @pl.when(step == 0)
    def _():
        branch_ref[...] = jnp.zeros_like(branch_ref)
        back_ref[...] = jnp.zeros_like(back_ref)
        for start in range(0, width, 256):
            cols = slice(start, start + 256)
            hidden_t[cols, :] = jnp.swapaxes(hidden_ref[:, cols].astype(f32), 0, 1).astype(bf16)
            grad_t[cols, :] = jnp.swapaxes(grad_ref[:, cols].astype(f32), 0, 1).astype(bf16)

    slope = math.sqrt(2.0 / math.pi)
    for up, down, bias, out_ref, out_bias_ref in (
        (up_other_ref, down_other_ref, bias_other_ref, send_ref, send_bias_ref),
        (up_ref, down_ref, bias_ref, keep_ref, keep_bias_ref),
    ):
        shards, part = up.shape[1], up.shape[2]
        units = shards * part
        up_rows = up[0].reshape(units, width)
        down_rows = down[0].reshape(units, width)
        pre = dot(up_rows, hidden_t[...]) + bias[0]
        square = pre * pre
        bend = jnp.tanh(slope * pre * (1.0 + 0.044715 * square))
        activated = (0.5 * pre * (1.0 + bend)).astype(bf16)
        gain = 0.5 * (1.0 + bend) + (0.5 * slope) * pre * (1.0 - bend * bend) * (
            1.0 + (3 * 0.044715) * square
        )
        grad_pre = (dot(down_rows, grad_t[...]) * gain).astype(bf16)
        out_bias_ref[0] = jnp.sum(grad_pre.astype(f32), axis=1, keepdims=True)
        out_ref[0, :, :part, :] = (
            dot(grad_pre, hidden_ref[...]).astype(bf16).reshape(shards, part, width)
        )
        out_ref[0, :, part:, :] = (
            dot(activated, grad_ref[...]).astype(bf16).reshape(shards, part, width)
        )
        branch_ref[...] += dot_tn(activated, down_rows)
        back_ref[...] += dot_tn(grad_pre, up_rows)


def mlp(core, hidden, grad, bias, weights, part):
    frame_parts, shards, _, width = weights.shape
    rows = hidden.shape[0]
    steps = frame_parts // 2
    units = shards * part

    def own(m, c):
        return 2 * m + c[0]

    def other(m, c):
        return 2 * m + 1 - c[0]

    def weight_spec(which, row):
        return pl.BlockSpec((1, shards, part, width), lambda m, c: (which(m, c), 0, row, 0))

    whole = pl.BlockSpec((rows, width), lambda m, c: (0, 0), pipeline_mode=pl.Buffered(1))
    sums = pl.BlockSpec((rows, width), lambda m, c: (0, 0))
    out = pl.BlockSpec((1, shards, 2 * part, width), lambda m, c: (m, 0, 0, 0))
    column = pl.BlockSpec((1, units, 1), lambda m, c: (m, 0, 0))
    work = rows * width * units * frame_parts
    return pl.pallas_call(
        mlp_kernel,
        grid_spec=pltpu.PrefetchScalarGridSpec(
            num_scalar_prefetch=1,
            grid=(steps,),
            in_specs=[
                whole,
                whole,
                pl.BlockSpec((1, units, 1), lambda m, c: (own(m, c), 0, 0)),
                pl.BlockSpec((1, units, 1), lambda m, c: (other(m, c), 0, 0)),
                weight_spec(own, 0),
                weight_spec(other, 0),
                weight_spec(own, 1),
                weight_spec(other, 1),
            ],
            out_specs=[sums, sums, out, out, column, column],
            scratch_shapes=[pltpu.VMEM((width, rows), bf16), pltpu.VMEM((width, rows), bf16)],
        ),
        out_shape=[
            jax.ShapeDtypeStruct((rows, width), f32),
            jax.ShapeDtypeStruct((rows, width), f32),
            jax.ShapeDtypeStruct((steps, shards, 2 * part, width), bf16),
            jax.ShapeDtypeStruct((steps, shards, 2 * part, width), bf16),
            jax.ShapeDtypeStruct((steps, units, 1), f32),
            jax.ShapeDtypeStruct((steps, units, 1), f32),
        ],
        compiler_params=pltpu.CompilerParams(vmem_limit_bytes=48 << 20),
        cost_estimate=pl.CostEstimate(
            flops=12 * work,
            bytes_accessed=frame_parts * units * width * 8,
            transcendentals=rows * units * frame_parts,
        ),
        name="mlp",
    )(core, hidden, grad, bias, bias, weights, weights, weights, weights)


def on_device(
    tokens,
    noise_steps,
    ada_weight,
    ada_bias,
    qkv_weight,
    qv_bias,
    out_weight,
    out_bias,
    up_weight,
    up_bias,
    down_weight,
    down_bias,
    cotangent,
):
    clip_count, local_frames, local_patches, model_width = tokens.shape
    tensor_count = lax.axis_size("tensor")
    frame_devices = lax.axis_size("frame")
    frame_at = lax.axis_index("frame")
    tensor_at = lax.axis_index("tensor")
    patch_count = local_patches * tensor_count
    hidden_width = up_weight.shape[1] * tensor_count
    head_total = model_width // HD
    shard_heads = head_total // tensor_count
    head_count = head_total // frame_devices
    lanes = head_count * HD
    unit_total = clip_count * local_frames
    units = unit_total // tensor_count
    sharers = tensor_count // clip_count
    share_at = 0 if sharers == 1 else tensor_at % sharers
    own_rows = units * patch_count
    all_rows = frame_devices * own_rows
    slot = frame_at % shard_heads
    group_at = frame_at // shard_heads
    shard_groups = tensor_count // head_count
    core = frame_at % 2
    chips = frame_devices // 2
    unit_shape = (units, patch_count, model_width)
    column_part = model_width // tensor_count


    def swap_frame(values):
        return lax.all_to_all(values, "frame", split_axis=0, concat_axis=0, tiled=True)

    def shifted(values, shift):
        return lax.ppermute(
            values, "tensor", [(t, (t + shift) % tensor_count) for t in range(tensor_count)]
        )

    def tensor_parts(values):
        return [shifted(values, tensor_count - 1 - n) for n in range(tensor_count - 1)] + [values]

    def tensor_sum(parts):
        total = parts[-1].astype(f32)
        for n in range(tensor_count - 1):
            total = total + shifted(parts[n], n + 1).astype(f32)
        return total

    def exchange(parts):
        last = tensor_count - 1
        return [shifted(parts[last - 1 - n], last - n) for n in range(last)] + [parts[last]]

    def to_relative(values):
        return [
            lax.dynamic_index_in_dim(
                values, (tensor_at + 1 + n) % tensor_count, 0, keepdims=False
            )
            for n in range(tensor_count)
        ]

    def rolled(values, start):
        if isinstance(start, int):
            start = start % tensor_count
            return jnp.concatenate([values[start:], values[:start]])
        return lax.dynamic_slice_in_dim(
            jnp.concatenate([values, values]), start % tensor_count, tensor_count, axis=0
        )


    def head_pairs(head, member):
        pairs = []
        for i in range(frame_devices):
            for t in range(member, tensor_count, sharers):
                shard = (t - member + i // shard_heads + head * shard_groups) % tensor_count
                pairs.append((i * tensor_count + shard, i * tensor_count + t))
        return pairs

    def from_owners(values, head):
        total = None
        for member in range(sharers):
            got = lax.ppermute(values, ("frame", "tensor"), head_pairs(head, member))
            total = got if total is None else total + got
        return total

    def to_owners(pieces):
        total = 0.0
        for head, piece in enumerate(pieces):
            for member in range(sharers):
                pairs = [(user, owner) for owner, user in head_pairs(head, member)]
                total = total + lax.ppermute(piece, ("frame", "tensor"), pairs).astype(f32)
        return total.astype(bf16)

    def to_units(values):
        parts = to_relative(
            values.reshape(tensor_count, units, local_patches, model_width)
        )
        return jnp.stack(exchange(parts), axis=1).reshape(units, patch_count, model_width)

    def from_units(values):
        parts = values.reshape(units, tensor_count, local_patches, model_width)
        mine = jnp.stack(exchange([parts[:, n] for n in range(tensor_count)]))
        return rolled(mine, -1 - tensor_at).reshape(
            clip_count, local_frames, local_patches, model_width
        )

    def core_swap(values):
        return lax.ppermute(values, "frame", [(i, i ^ 1) for i in range(frame_devices)])

    def scatter(values):
        return lax.psum_scatter(
            values.reshape(-1, model_width),
            "frame",
            scatter_dimension=0,
            axis_index_groups=[list(range(c, frame_devices, 2)) for c in range(2)],
            tiled=True,
        ).reshape(values.shape[1:])

    bits = [1 << n for n in range(frame_devices.bit_length() - 1)]
    bit_orders = (tuple(bits[1:] + bits[:1]), tuple(bits[:0:-1] + bits[:1]))

    def doubled(values):
        outs = []
        width = values.shape[1] // 2
        for n, order in enumerate(bit_orders):
            part = values[:, n * width : (n + 1) * width]
            for bit in order:
                pairs = [(i, i ^ bit) for i in range(frame_devices)]
                part = jnp.concatenate([part, lax.ppermute(part, "frame", pairs)])
            outs.append(part.reshape(frame_devices, -1, width))
        return outs

    def frame_parts(values):
        return (
            lax.all_gather(values, "frame", axis=0, tiled=True)
            .reshape(frame_devices, -1, model_width)
        )

    unit_tokens = to_units(tokens)
    act_noise = noise_activation(noise_steps, model_width).reshape(unit_total, model_width)
    mod_local = jnp.einsum(
        "ud,dkj->ukj", act_noise, ada_weight, preferred_element_type=f32
    ) + ada_bias.astype(f32)
    modulation = (
        rolled(
            jnp.stack(
                exchange(to_relative(mod_local.reshape(tensor_count, units * 6, column_part)))
            ),
            -1 - tensor_at,
        )
        .reshape(tensor_count, units, 6, column_part)
        .transpose(1, 2, 0, 3)
        .reshape(units, 6, model_width)
    )
    shift_one = modulation[:, None, 0]
    scale_one = modulation[:, None, 1]
    gate_one = modulation[:, None, 2]
    shift_two = modulation[:, None, 3]
    scale_two = modulation[:, None, 4]
    gate_two = modulation[:, None, 5]

    slot_weight = lax.dynamic_slice_in_dim(qkv_weight, slot * HD, HD, axis=2)
    slot_weight = slot_weight.transpose(1, 2, 0).reshape(3 * HD, model_width)
    slot_bias = lax.dynamic_slice_in_dim(qv_bias, slot * HD, HD, axis=1).reshape(1, 2 * HD)
    slot_bias = jnp.pad(slot_bias, ((0, 15), (0, model_width - 2 * HD)))
    slot_pack = jnp.concatenate([slot_weight, slot_bias])

    def own_part(values):
        size = values.shape[0] // frame_devices
        return lax.dynamic_slice_in_dim(values, frame_at * size, size, axis=0)

    hidden_part = hidden_width // (tensor_count * frame_devices)
    half = hidden_part // 2
    out_rows = out_weight.shape[0] // frame_devices
    up_part = lax.dynamic_slice_in_dim(
        up_weight, frame_at * hidden_part, hidden_part, axis=1
    ).transpose(1, 0)
    down_part = own_part(down_weight)
    bias_part = lax.dynamic_slice_in_dim(up_bias, frame_at * hidden_part, hidden_part, axis=0)
    bias_part = jnp.pad(bias_part[None, :], ((0, 15), (0, model_width - hidden_part)))
    first_pack = jnp.concatenate([up_part[:half], down_part[:half], bias_part])
    second_pack = jnp.concatenate([up_part[half:], down_part[half:]])
    out_pack = own_part(out_weight)
    slot_pack, unit_tokens = lax.optimization_barrier((slot_pack, unit_tokens))
    head_pack = jnp.stack([from_owners(slot_pack, head) for head in range(head_count)])
    first_pack, head_pack = lax.optimization_barrier(
        (jnp.concatenate([first_pack, out_pack]), head_pack)
    )
    first_list = tensor_parts(first_pack)
    out_at = first_pack.shape[0] - out_rows
    first_parts = jnp.concatenate(
        [
            jnp.stack([part[:out_at] for part in first_list]),
            rolled(jnp.stack([part[out_at:] for part in first_list]), -1 - share_at),
        ],
        axis=1,
    ).reshape(-1, model_width)
    head_weight = (
        head_pack[:, : 3 * HD]
        .reshape(head_count, 3, HD, model_width)
        .transpose(1, 0, 2, 3)
        .reshape(3 * lanes, model_width)
    )
    head_bias = head_pack[:, 3 * HD, : 2 * HD]
    head_bias = head_bias.reshape(head_count, 2, HD).transpose(1, 0, 2).reshape(2, lanes)
    head_bias = head_bias.astype(f32)
    qkv_bias = jnp.concatenate([head_bias[0], jnp.zeros((lanes,), f32), head_bias[1]])

    token_values = unit_tokens.astype(f32)
    normed_one, inverse_one = layer_norm(token_values)
    hidden_one = (normed_one * (1.0 + scale_one) + shift_one).astype(bf16)
    hidden_all = lax.all_gather(
        hidden_one.reshape(own_rows, model_width), "frame", axis=0, tiled=True
    )

    first_all = lax.all_gather(first_parts, "frame", axis=0, tiled=True)
    first_all = first_all.reshape(frame_devices, tensor_count, -1, model_width)
    up_bias_all = first_all[:, :, 2 * half, :hidden_part].astype(f32)
    first_bias = up_bias_all[:, :, :half].reshape(frame_devices, tensor_count * half, 1)
    second_bias = up_bias_all[:, :, half:].reshape(frame_devices, tensor_count * half, 1)
    head_parts = HD // out_rows
    out_full = (
        first_all[:, :, 2 * half + 16 :]
        .reshape(shard_heads, head_parts, head_count, shard_groups, out_rows, model_width)
        .transpose(3, 0, 2, 1, 4, 5)
        .reshape(model_width, model_width)
    )

    projected = (dot_nt(hidden_all, head_weight) + qkv_bias).astype(bf16)
    queries = projected[:, :lanes]
    keys = projected[:, lanes : 2 * lanes]
    values = projected[:, 2 * lanes :]

    def share(mine):
        if sharers == 1:
            return mine
        pieces = [mine]
        for shift in range(1, sharers):
            perm = [
                (t, (t // sharers) * sharers + (t + shift) % sharers) for t in range(tensor_count)
            ]
            pieces.append(lax.ppermute(mine, "tensor", perm))
        stacked = jnp.stack(pieces)
        stacked = jnp.stack(
            [
                lax.dynamic_index_in_dim(
                    stacked, (share_at - member) % sharers, 0, keepdims=False
                )
                for member in range(sharers)
            ]
        )
        return (
            stacked.reshape(sharers, frame_devices, own_rows, lanes)
            .transpose(1, 0, 2, 3)
            .reshape(sharers * all_rows, lanes)
        )

    def unshare(partial_sums):
        if sharers == 1:
            return partial_sums
        pieces = (
            partial_sums.reshape(frame_devices, sharers, own_rows, lanes)
            .transpose(1, 0, 2, 3)
            .reshape(sharers, all_rows, lanes)
        )
        total = lax.dynamic_index_in_dim(pieces, share_at, 0, keepdims=False).astype(f32)
        for shift in range(1, sharers):
            perm = [
                (t, (t // sharers) * sharers + (t + shift) % sharers) for t in range(tensor_count)
            ]
            piece = lax.dynamic_index_in_dim(
                pieces, (share_at + shift) % sharers, 0, keepdims=False
            )
            total = total + lax.ppermute(piece, "tensor", perm).astype(f32)
        return total.astype(bf16)

    keys_all = share(keys)
    values_all = share(values)
    unit_ids = jnp.arange(frame_devices * units, dtype=jnp.int32)
    frame_ids = (
        (unit_ids // units) * local_frames + share_at * units + unit_ids % units
    )
    values_t = values_all.T
    steps = all_rows // patch_count
    second_pack, queries = lax.optimization_barrier((second_pack, queries))
    second_list = tensor_parts(second_pack)
    cut = steps * 11 // 16
    heads_a, lse_a = attend(
        queries, keys_all, values_t, frame_ids, head_count, patch_count, 0, cut, ()
    )
    heads_a, *second_list = lax.optimization_barrier((heads_a, *second_list))
    second_parts = jnp.concatenate(second_list)
    cotangent, second_parts = lax.optimization_barrier((cotangent, second_parts))
    upstream = to_units(cotangent)
    heads_b, lse_b = attend(
        queries, keys_all, values_t, frame_ids, head_count, patch_count, cut, steps,
        (second_parts,),
    )
    attended_heads = jnp.concatenate([heads_a, heads_b])
    row_lse = jnp.concatenate([lse_a, lse_b])
    second_all = lax.all_gather(
        second_parts, "frame", axis=0, tiled=True
    ).reshape(frame_devices, tensor_count, -1, model_width)
    heads_here = swap_frame(attended_heads.reshape(frame_devices, own_rows, lanes))

    grad_two = (gate_two * upstream.astype(f32)).astype(bf16).reshape(own_rows, model_width)
    grad_down_bias = jnp.sum(grad_two.astype(f32), axis=0)

    flat_tokens = unit_tokens.reshape(own_rows, model_width)
    attended, branch_one, hidden_two = project(
        heads_here, out_full, out_bias.astype(f32)[None, :], flat_tokens, modulation
    )

    core_id = core.astype(jnp.int32).reshape(1)
    branch_a, back_a, keep_a, send_a, keep_bias_a, send_bias_a = mlp(
        core_id, hidden_two, grad_two, first_bias, first_all, half
    )
    got_a = core_swap(send_a)
    branch_b, back_b, keep_b, send_b, keep_bias_b, send_bias_b = mlp(
        core_id, hidden_two, grad_two, second_bias, second_all, half
    )
    got_b = core_swap(send_b)
    got_a, branch_b = lax.optimization_barrier((got_a, branch_b))
    back_b, first_half = lax.optimization_barrier((back_b, add_pairs(keep_a, got_a)))
    first_sum = scatter(first_half)
    result, grad_middle, grad_one, head_grads, unit_sums = middle_back(
        flat_tokens, branch_one, branch_a, branch_b, back_a, back_b,
        upstream.reshape(own_rows, model_width), modulation, down_bias.astype(f32)[None, :],
        out_full, frame_devices,
    )
    grad_heads = swap_frame(head_grads).reshape(all_rows, lanes)
    result = from_units(result.reshape(unit_shape))
    grad_middle = grad_middle.reshape(unit_shape)
    grad_gate_one, grad_shift_two, grad_scale_two, grad_gate_two = (
        unit_sums[:, n] for n in range(4)
    )
    grad_out_bias = jnp.sum(unit_sums[:, 4], axis=0)

    grad_out = (
        dot_tn(attended, grad_one)
        .astype(bf16)
        .reshape(shard_groups, shard_heads, head_count, head_parts, out_rows, model_width)
        .transpose(2, 0, 1, 3, 4, 5)
        .reshape(tensor_count, frame_devices, out_rows, model_width)
    )
    grad_out = rolled(grad_out, share_at + 1).transpose(1, 0, 2, 3)
    width_part = model_width // frame_devices

    def by_core(keep_part, send_part):
        pair = jnp.stack([keep_part, send_part], axis=1)
        return jnp.where(core == 0, pair, pair[:, ::-1]).reshape(
            (frame_devices,) + keep_part.shape[1:]
        )

    grad_up_bias = jnp.concatenate(
        [
            by_core(keep_bias_a, send_bias_a).reshape(frame_devices, tensor_count, half),
            by_core(keep_bias_b, send_bias_b).reshape(frame_devices, tensor_count, half),
        ],
        axis=2,
    )
    once = jnp.concatenate(
        [
            grad_down_bias.reshape(frame_devices, 1, width_part),
            grad_out_bias.reshape(frame_devices, 1, width_part),
        ],
        axis=2,
    )
    bias_row = jnp.concatenate(
        [jnp.broadcast_to(once, (frame_devices, tensor_count, 2 * width_part)), grad_up_bias],
        axis=2,
    ).astype(bf16)
    bias_row = jnp.pad(
        bias_row[:, :, None, :], ((0, 0), (0, 0), (0, 15), (0, model_width - bias_row.shape[2]))
    )
    out_pairs = jnp.concatenate([grad_out, bias_row], axis=2).reshape(
        chips, 2, tensor_count, out_rows + 16, model_width
    )
    got_out = core_swap(lax.dynamic_index_in_dim(out_pairs, 1 - core, 1, keepdims=False))
    late_half = add_pairs(
        keep_b,
        got_b,
        lax.dynamic_index_in_dim(out_pairs, core, 1, keepdims=False),
        got_out,
    )
    late_sum = scatter(late_half)
    first_list = exchange([first_sum[n] for n in range(tensor_count)])

    keys_t = keys_all.T
    grad_q_a, *sums = attend_back(
        queries, keys_all, values_all, keys_t, attended_heads, row_lse, grad_heads,
        frame_ids, head_count, patch_count, 0, cut, (), f32, (late_half, result),
    )
    *sums, first_list = lax.optimization_barrier((*sums, first_list))
    first_total = sum(part.astype(f32) for part in first_list).astype(bf16)
    grad_q_b, grad_k_all, grad_v_all = attend_back(
        queries, keys_all, values_all, keys_t, attended_heads, row_lse, grad_heads,
        frame_ids, head_count, patch_count, cut, steps, tuple(sums), bf16, (first_total,),
    )
    grad_q = jnp.concatenate([grad_q_a, grad_q_b])
    grad_k = unshare(grad_k_all)
    grad_v = unshare(grad_v_all)
    grad_projected = jnp.concatenate([grad_q, grad_k, grad_v], axis=1)
    grad_hidden_part, grad_projected = lax.optimization_barrier(
        (dot(grad_projected, head_weight).astype(bf16), grad_projected)
    )
    grad_hidden_one = lax.psum_scatter(grad_hidden_part, "frame", scatter_dimension=0, tiled=True)
    grad_hidden_one = grad_hidden_one.astype(f32).reshape(unit_shape)

    late_total = tensor_sum([late_sum[n] for n in range(tensor_count)]).astype(bf16)
    grad_head_weight = dot_tn(grad_projected, hidden_all).astype(bf16)
    grad_slots = (
        grad_head_weight.reshape(3, head_count, HD, model_width)
        .transpose(1, 0, 2, 3)
        .reshape(head_count, 3 * HD, model_width)
    )
    grad_head_bias = jnp.stack(
        [jnp.sum(grad_q.astype(f32), axis=0), jnp.sum(grad_v.astype(f32), axis=0)]
    ).astype(bf16)
    grad_head_bias = grad_head_bias.reshape(2, head_count, HD).transpose(1, 0, 2)
    grad_head_bias = jnp.pad(
        grad_head_bias.reshape(head_count, 1, 2 * HD),
        ((0, 0), (0, 15), (0, model_width - 2 * HD)),
    )
    grad_slots = jnp.concatenate([grad_slots, grad_head_bias], axis=1)

    slots_total = to_owners([grad_slots[head] for head in range(head_count)])

    slots_left, slots_right = doubled(slots_total)
    grad_hidden_one, slots_left, slots_right = lax.optimization_barrier(
        (grad_hidden_one, slots_left, slots_right)
    )
    grad_scale_one = jnp.sum(grad_hidden_one * normed_one, axis=1)
    grad_shift_one = jnp.sum(grad_hidden_one, axis=1)
    grad_tokens = (
        grad_middle
        + norm_back(grad_hidden_one * (1.0 + scale_one), normed_one, inverse_one)
    ).astype(bf16)
    tail_all = frame_parts(jnp.concatenate([first_total, late_total]))
    grad_tokens = from_units(grad_tokens)
    grad_modulation = jnp.stack(
        [
            grad_shift_one,
            grad_scale_one,
            grad_gate_one,
            grad_shift_two,
            grad_scale_two,
            grad_gate_two,
        ],
        axis=1,
    )
    unit_steps = lax.dynamic_slice_in_dim(
        noise_steps.reshape(unit_total), tensor_at * units, units
    ).astype(f32)
    grad_mod_parts = exchange(
        to_relative(
            jnp.concatenate(
                [
                    grad_modulation.reshape(units, 6, tensor_count, column_part)
                    .transpose(2, 0, 1, 3)
                    .reshape(tensor_count, units, 6 * column_part),
                    jnp.broadcast_to(unit_steps[None, :, None], (tensor_count, units, 128)),
                ],
                axis=2,
            )
        )
    )
    grad_mod_all = lax.all_gather(
        jnp.stack(grad_mod_parts).reshape(unit_total, -1), "frame", axis=0, tiled=True
    )
    act_all = noise_activation(grad_mod_all[:, -1], model_width)
    grad_mod_all = grad_mod_all[:, :-128].reshape(-1, 6, column_part)
    grad_ada_weight = jnp.einsum(
        "ud,ukj->dkj", act_all.astype(f32), grad_mod_all, precision=lax.Precision.HIGH
    )
    grad_ada_bias = jnp.sum(grad_mod_all, axis=0)
    final_up, final_down, final_out = unpack(tail_all, half, out_rows, (grad_tokens,))
    tail_bias = tail_all[:, 4 * half + out_rows].astype(f32)
    final_down_bias = tail_bias[:, :width_part].reshape(model_width)
    final_out_bias = tail_bias[:, width_part : 2 * width_part].reshape(model_width)
    final_up_bias = tail_bias[:, 2 * width_part : 2 * width_part + hidden_part].reshape(
        up_bias.shape
    )
    final_qkv, bias_sums = unpack_heads(
        frame_at.astype(jnp.int32).reshape(1), slots_left, slots_right, *bit_orders, shard_heads, ()
    )
    final_qkv = final_qkv.transpose(1, 0, 2)
    final_qv_bias = (
        bias_sums[:, 0].reshape(shard_heads, 2, HD).transpose(1, 0, 2).reshape(qv_bias.shape)
    )
    return (
        result,
        grad_tokens.astype(f32),
        grad_ada_weight,
        grad_ada_bias,
        final_qkv,
        final_qv_bias,
        final_out,
        final_out_bias,
        final_up,
        final_up_bias,
        final_down,
        final_down_bias,
    )


def solution(mesh):
    in_specs = (
        P(None, "frame", "tensor", None),
        P(None, "frame"),
        P(None, None, "tensor"),
        P(None, "tensor"),
        P(None, None, "tensor"),
        P(None, "tensor"),
        P("tensor", None),
        P(),
        P(None, "tensor"),
        P("tensor"),
        P("tensor", None),
        P(),
        P(None, "frame", "tensor", None),
    )
    out_specs = (
        P(None, "frame", "tensor", None),
        P(None, "frame", "tensor", None),
        P(None, None, "tensor"),
        P(None, "tensor"),
        P(None, None, "tensor"),
        P(None, "tensor"),
        P("tensor", None),
        P(),
        P(None, "tensor"),
        P("tensor"),
        P("tensor", None),
        P(),
    )
    return jax.shard_map(
        on_device, mesh=mesh, in_specs=in_specs, out_specs=out_specs, check_vma=False
    )
```
